256 devices in a mesh: section: 2 (over x_hi), fsdp: 64 (over y, z, x_lo), dp: 2 (over core).
Axes of the slice: x: 4 (x_hi: 2, x_lo: 2; x = x_hi * 2 + x_lo), y: 4, z: 8, core: 2. Of those that a mesh axis runs over, the one named last changes fastest.
Arguments:
- hidden: bfloat16 [4, 512, 8192], P(('section', 'dp'), 'fsdp'), may hold values from -7 to 7
- cotangent: bfloat16 [4, 512, 8192], P(('section', 'dp'), None, 'fsdp'), may hold values from -6 to 6
- seg_ids: int32 [4, 512], P(('section', 'dp')), may hold values from 0 to 8, as said below
- advantage: float32 [4, 8], P(('section', 'dp')), may hold values from -4 to 4
- w_query: bfloat16 [8192, 8192], P('fsdp'), may hold values from -6 to 6
- w_key: bfloat16 [8192, 1024], P('fsdp'), may hold values from -6 to 6
- w_value: bfloat16 [8192, 1024], P('fsdp'), may hold values from -6 to 6
Outputs:
- rollout_query: bfloat16 [8192, 8192], P(None, 'fsdp')
- rollout_key: bfloat16 [8192, 8192], P(None, 'fsdp')
- rollout_value: bfloat16 [8192, 8192], P(None, 'fsdp')
The draws below stay inside these ranges and needn't reach their ends.
Inputs may be any that keep to these rules, and one draw needn't show every extreme that they name: `seg_ids`: in each block ids never fall; each id below 8 covers 1 to 64 positions, one of them exactly 64, and every id below 8 appears; id 8 marks padding at the block's end.
All inputs are finite; a program needn't handle non-finite values.
Results may differ from the reference program's by a relative error of at most 0.015.
The reference program's roundings to bfloat16 on the way (of `normed`, `attention_bf`, `grad_context` and `dscore`) count: a program that leaves them out, or rounds other values in their place, can miss the bound.
Values may be sent and summed in bfloat16 or wider, within the bound.
No kernel may reach another device: no remote copies, remote signals or barrier semaphores. Data moves between devices by JAX's collectives and lax.ppermute only.
A program may use at most 64 MiB of HBM per device.

```python
import jax
import jax.numpy as jnp
from jax import lax

D = 8192
H = 64
KVH = 8
HD = 128
BLOCK = 512
RESP = 8
SHARE = 8
QPK = 1
COPIES = 64
MOST = 64
GROUPS = 4


def draw_seg_ids(key, part):
    divisors = jax.random.randint(jax.random.fold_in(key, 11), (GROUPS, RESP), 1, 9)
    lengths = MOST // divisors
    chosen = jax.random.randint(jax.random.fold_in(key, 12), (GROUPS, 1), 0, RESP)
    lengths = jnp.where(jnp.arange(RESP)[None, :] == chosen, MOST, lengths)
    ends = jnp.cumsum(lengths, axis=1)
    places = jnp.arange(BLOCK)
    return jnp.sum((places[None, :, None] >= ends[:, None, :]).astype(jnp.int32), axis=2).astype(jnp.int32)


def draw_hidden(key, part):
    field = jax.random.truncated_normal(jax.random.fold_in(key, 21), -6.0, 6.0, (GROUPS, BLOCK, D), jnp.float32)
    return field.astype(jnp.bfloat16)


def draw_w_query(key, part):
    field = jax.random.truncated_normal(jax.random.fold_in(key, 31), -6.0, 6.0, (D, H * HD), jnp.float32)
    return field.astype(jnp.bfloat16)


def draw_w_key(key, part):
    field = jax.random.truncated_normal(jax.random.fold_in(key, 41), -6.0, 6.0, (D, KVH * HD), jnp.float32)
    return field.astype(jnp.bfloat16)


def block_levels(stream_key, shape, cuts, low, high):
    factor_of = 1.0
    for axis_at, shards_of in cuts:
        steps = jax.random.uniform(jax.random.fold_in(jax.random.fold_in(stream_key, 6), axis_at), (shards_of,), jnp.float32, low / len(cuts), high / len(cuts))
        factor_of = factor_of * jnp.repeat(jnp.exp(steps), shape[axis_at] // shards_of).reshape((-1,) + (1,) * (len(shape) - 1 - axis_at))
    return factor_of


def normal_values(key, extent, width, most, shards=(), kind=jnp.bfloat16):
    entries = width * jax.random.normal(key, extent, jnp.float32)
    if shards:
        entries = entries * block_levels(key, extent, shards, -0.22, 0.18)
    return jnp.clip(entries, -most, most).astype(kind)


def setup_inputs(seed: int = 0) -> dict:
    keys = jax.random.split(jax.random.key(seed), 8)
    return {
        "hidden": draw_hidden(jax.random.fold_in(keys[7], 71), 0),
        "cotangent": normal_values(keys[1], (GROUPS, BLOCK, H * HD), 1.0, 6.0, ((0, 4), (2, 64))),
        "seg_ids": draw_seg_ids(jax.random.fold_in(keys[7], 71), 0),
        "advantage": normal_values(keys[3], (GROUPS, RESP), 1.0, 4.0, ((0, 4),), jnp.float32),
        "w_query": draw_w_query(jax.random.fold_in(keys[7], 71), 0),
        "w_key": draw_w_key(jax.random.fold_in(keys[7], 71), 0),
        "w_value": normal_values(keys[6], (D, KVH * HD), 1.0, 6.0, ((0, 64),)),
    }


step_rate = 200.0
rope_base = 1000000.0
norm_eps = 1e-06
masked_score = -1e+30

def rotate(field, cosine_table, sine_table):
    half_width = field.shape[-1] // 2
    lead_half = field[..., :half_width]
    tail_half = field[..., half_width:]
    return jnp.concatenate([lead_half * cosine_table - tail_half * sine_table, tail_half * cosine_table + lead_half * sine_table], -1)

def unrotate(field, cosine_table, sine_table):
    half_width = field.shape[-1] // 2
    lead_half = field[..., :half_width]
    tail_half = field[..., half_width:]
    return jnp.concatenate([lead_half * cosine_table + tail_half * sine_table, tail_half * cosine_table - lead_half * sine_table], -1)

def angles(seg_row):
    span_count = seg_row.shape[0]
    earlier = lax.optimization_barrier(jnp.sum((seg_row[None, :] < seg_row[:, None]).astype(jnp.int32), axis=1))
    positions = jnp.arange(span_count, dtype=jnp.int32) - earlier
    frequency = rope_base ** (-jnp.arange(HD // 2, dtype=jnp.float32) * 2.0 / HD)
    phase_grid = positions.astype(jnp.float32)[:, None] * frequency[None, :]
    return (jnp.cos(phase_grid)[:, None, :], jnp.sin(phase_grid)[:, None, :])

def token_weights(seg_row, advantage_row):
    id_range = jnp.arange(RESP + 1, dtype=jnp.int32)
    onehot = (seg_row[:, None] == id_range[None, :]).astype(jnp.float32)
    counts = lax.optimization_barrier(jnp.sum(onehot, axis=0))[:RESP]
    per_token = -advantage_row.astype(jnp.float32) / counts
    return lax.optimization_barrier(jnp.sum(onehot[:, :RESP] * per_token[None, :], axis=1))

def attend_back(q_rot, k_rot, v_bf, grad_context, allowed):
    highest = lax.Precision.HIGHEST
    score_scale = HD ** (-0.5)
    query_f = q_rot.astype(jnp.float32)
    key_f = k_rot.astype(jnp.float32)
    value_f = v_bf.astype(jnp.float32)
    context_f = grad_context.astype(jnp.float32)
    scores = jnp.einsum('tkjqd,ukd->kjqtu', query_f, key_f, precision=highest) * score_scale
    scores = jnp.where(allowed, scores, masked_score)
    row_top = lax.optimization_barrier(jnp.max(scores, axis=-1, keepdims=True))
    exponent = jnp.exp(scores - row_top)
    attention = exponent / lax.optimization_barrier(jnp.sum(exponent, axis=-1, keepdims=True))
    attention_bf = attention.astype(jnp.bfloat16)
    grad_prob = jnp.einsum('tkjqd,ukd->kjqtu', context_f, value_f, precision=highest)
    inner_sum = lax.optimization_barrier(jnp.sum(attention * grad_prob, axis=-1, keepdims=True))
    dscore = (attention * (grad_prob - inner_sum)).astype(jnp.bfloat16).astype(jnp.float32)
    grad_query = jnp.einsum('kjqtu,ukd->tkjqd', dscore, key_f, precision=highest) * score_scale
    grad_key = jnp.einsum('kjqtu,tkjqd->ukjd', dscore, query_f, precision=highest) * score_scale
    grad_value = jnp.einsum('kjqtu,tkjqd->ukjd', attention_bf.astype(jnp.float32), context_f, precision=highest)
    return (grad_query, grad_key, grad_value)

def rounded(field):
    return lax.optimization_barrier(field.astype(jnp.bfloat16)).astype(jnp.float32)

def reference(hidden, cotangent, seg_ids, advantage, w_query, w_key, w_value):
    inv_width = D ** (-0.5)
    block_len = BLOCK
    total_q = jnp.zeros((D, H * HD), jnp.float32)
    total_k = jnp.zeros((D, KVH * HD), jnp.float32)
    total_v = jnp.zeros((D, KVH * HD), jnp.float32)
    for group_index in range(GROUPS):
        token_rows = hidden[group_index].astype(jnp.float32)
        normed = (token_rows * lax.rsqrt(lax.optimization_barrier(jnp.mean(token_rows * token_rows, axis=-1, keepdims=True)) + norm_eps)).astype(jnp.bfloat16)
        queries = jnp.dot(normed, w_query, preferred_element_type=jnp.float32) * inv_width
        key_proj = jnp.dot(normed, w_key, preferred_element_type=jnp.float32) * inv_width
        value_proj = jnp.dot(normed, w_value, preferred_element_type=jnp.float32) * inv_width
        seg_row = seg_ids[group_index]
        cosine_table, sine_table = angles(seg_row)
        q_rot = rotate(queries.reshape(block_len, H, HD), cosine_table, sine_table).astype(jnp.bfloat16)
        k_rot = rotate(key_proj.reshape(block_len, KVH, HD), cosine_table, sine_table).astype(jnp.bfloat16)
        v_bf = value_proj.astype(jnp.bfloat16).reshape(block_len, KVH, HD)
        weight_row = token_weights(seg_row, advantage[group_index])
        grad_context = (cotangent[group_index].astype(jnp.float32) * weight_row[:, None]).astype(jnp.bfloat16)
        place = jnp.arange(block_len, dtype=jnp.int32)
        allowed = (seg_row[:, None] == seg_row[None, :]) & (place[None, :] <= place[:, None])
        grad_query, grad_key, grad_value = attend_back(q_rot.reshape(block_len, KVH, SHARE, QPK, HD), k_rot, v_bf, grad_context.reshape(block_len, KVH, SHARE, QPK, HD), allowed)
        grad_query = unrotate(grad_query.reshape(block_len, H, HD), cosine_table, sine_table)
        grad_key = unrotate(grad_key.reshape(block_len, COPIES, HD), cosine_table, sine_table)
        scaled_q = (grad_query.reshape(block_len, H * HD) * inv_width).astype(jnp.bfloat16)
        scaled_k = (grad_key.reshape(block_len, COPIES * HD) * inv_width).astype(jnp.bfloat16)
        scaled_v = (grad_value.reshape(block_len, COPIES * HD) * inv_width).astype(jnp.bfloat16)
        part_q = rounded(jnp.dot(normed.T, scaled_q, preferred_element_type=jnp.float32))
        part_k = rounded(jnp.dot(normed.T, scaled_k, preferred_element_type=jnp.float32))
        part_v = rounded(jnp.dot(normed.T, scaled_v, preferred_element_type=jnp.float32))
        total_q = total_q + part_q
        total_k = total_k + lax.optimization_barrier(jnp.sum(part_k.reshape(D, KVH, SHARE, HD), axis=2)).reshape(D, KVH * HD)
        total_v = total_v + lax.optimization_barrier(jnp.sum(part_v.reshape(D, KVH, SHARE, HD), axis=2)).reshape(D, KVH * HD)
    new_q = (w_query.astype(jnp.float32) - step_rate * total_q).astype(jnp.bfloat16)
    new_k = (w_key.astype(jnp.float32) - step_rate * total_k).astype(jnp.bfloat16)
    new_v = (w_value.astype(jnp.float32) - step_rate * total_v).astype(jnp.bfloat16)
    rollout_key = jnp.repeat(new_k.reshape(D, KVH, HD), SHARE, axis=1).reshape(D, COPIES * HD)
    rollout_value = jnp.repeat(new_v.reshape(D, KVH, HD), SHARE, axis=1).reshape(D, COPIES * HD)
    return (new_q, rollout_key, rollout_value)
```

```python
import jax
import jax.numpy as jnp
from jax import lax
from jax.sharding import Mesh, PartitionSpec as P

D = 8192
HD = 128
RESP = 8

step_rate = 200.0
rope_base = 1000000.0
norm_eps = 1e-06
masked_score = -1e30

YZ = ("y", "zh", "zl")
KH = ("y", "zh")
MEM = ("zl", "core")
X = ("xh", "xl")
FS = ("y", "zh", "zl", "xl")


def rotate(field, cosine_table, sine_table):
    half_width = field.shape[-1] // 2
    lead_half = field[..., :half_width]
    tail_half = field[..., half_width:]
    return jnp.concatenate(
        [
            lead_half * cosine_table - tail_half * sine_table,
            tail_half * cosine_table + lead_half * sine_table,
        ],
        -1,
    )


def angles(seg_row):
    span_count = seg_row.shape[0]
    earlier = jnp.sum((seg_row[None, :] < seg_row[:, None]).astype(jnp.int32), axis=1)
    positions = jnp.arange(span_count, dtype=jnp.int32) - earlier
    frequency = rope_base ** (-jnp.arange(HD // 2, dtype=jnp.float32) * 2.0 / HD)
    phase_grid = positions.astype(jnp.float32)[:, None] * frequency[None, :]
    return jnp.cos(phase_grid), jnp.sin(phase_grid)


def token_weights(seg_row, advantage_row):
    id_range = jnp.arange(RESP + 1, dtype=jnp.int32)
    onehot = (seg_row[:, None] == id_range[None, :]).astype(jnp.float32)
    counts = jnp.sum(onehot, axis=0)[:RESP]
    per_token = -advantage_row / counts
    return jnp.sum(onehot[:, :RESP] * per_token[None, :], axis=1)


def attend_back(q_rot, k_rot, v_bf, grad_context, allowed):
    score_scale = HD ** (-0.5)
    f32 = jnp.float32
    scores = jnp.einsum("td,ud->tu", q_rot, k_rot, preferred_element_type=f32) * score_scale
    scores = jnp.where(allowed, scores, masked_score)
    row_top = jnp.max(scores, axis=-1, keepdims=True)
    exponent = jnp.exp(scores - row_top)
    attention = exponent / jnp.sum(exponent, axis=-1, keepdims=True)
    attention_bf = attention.astype(jnp.bfloat16)
    grad_prob = jnp.einsum("td,ud->tu", grad_context, v_bf, preferred_element_type=f32)
    inner_sum = jnp.sum(attention * grad_prob, axis=-1, keepdims=True)
    dscore = (attention * (grad_prob - inner_sum)).astype(jnp.bfloat16)
    grad_query = jnp.einsum("tu,ud->td", dscore, k_rot, preferred_element_type=f32) * score_scale
    grad_key = jnp.einsum("tu,td->ud", dscore, q_rot, preferred_element_type=f32) * score_scale
    grad_value = jnp.einsum("tu,td->ud", attention_bf, grad_context, preferred_element_type=f32)
    return grad_query, grad_key, grad_value


def swap(x):
    return lax.ppermute(x, ("xl", "core"), [(0, 0), (1, 2), (2, 1), (3, 3)])


def flip(x, axes):
    n = 2 ** len(axes)
    return lax.ppermute(x, axes, [(i, n - 1 - i) for i in range(n)])


def exchange(x, axes):
    return lax.all_to_all(x, axes, split_axis=0, concat_axis=0, tiled=True)


def spread(x, axes):
    n = lax.axis_size(axes)
    return exchange(jnp.broadcast_to(x[None], (n,) + x.shape), axes)


def ordered(mine, other, bit):
    first = jnp.where(bit == 0, mine, other)
    second = jnp.where(bit == 0, other, mine)
    return first, second


def local(hidden, cotangent, seg_ids, advantage, w_query, w_key, w_value):
    f32 = jnp.float32
    bf16 = jnp.bfloat16
    inv_width = D ** (-0.5)
    xh = lax.axis_index("xh")
    xl = lax.axis_index("xl")
    core = lax.axis_index("core")
    zl = lax.axis_index("zl")
    member = zl * 2 + core
    ring = xh * 2 + xl

    token_rows = hidden[0].astype(f32)
    normed_own = (
        token_rows * lax.rsqrt(jnp.mean(token_rows * token_rows, axis=-1, keepdims=True) + norm_eps)
    ).astype(bf16)
    normed_own = swap(normed_own)
    cot = swap(cotangent[0])
    seg_row = swap(seg_ids[0])
    adv_row = swap(advantage[0])
    normed = lax.all_gather(normed_own, YZ + ("core",), axis=0, tiled=True)
    block_len = normed.shape[0]

    wq = w_query.reshape(2, 64, 32, 2, HD)
    wq = lax.dynamic_index_in_dim(wq, xh, 0, keepdims=False)
    wq = lax.dynamic_index_in_dim(wq, core, 2, keepdims=False)
    wq = exchange(wq.transpose(1, 0, 2), YZ)
    wq_l = flip(wq, ("xl",))
    wq_h = flip(wq, ("xh",))
    wq_b = flip(wq, X)
    mine = ordered(wq, wq_l, xl)
    theirs = ordered(wq_h, wq_b, xl)
    row0 = ordered(mine[0], theirs[0], xh)
    row1 = ordered(mine[1], theirs[1], xh)
    q_cols = jnp.stack([row0[0], row0[1], row1[0], row1[1]], axis=1).reshape(D, HD)

    wkv = jnp.concatenate([w_key.reshape(128, 8, HD), w_value.reshape(128, 8, HD)], axis=-1)
    wkv = swap(exchange(wkv.transpose(1, 0, 2), KH))

    cosine_table, sine_table = angles(seg_row)
    weight_row = token_weights(seg_row, adv_row)
    grad_context = (cot.astype(f32) * weight_row[:, None]).astype(bf16)
    place = jnp.arange(block_len, dtype=jnp.int32)
    allowed = (seg_row[:, None] == seg_row[None, :]) & (place[None, :] <= place[:, None])

    normed_m = lax.dynamic_index_in_dim(
        normed.reshape(block_len, 8, 8, HD), member, 2, keepdims=False
    ).reshape(block_len, 1024)
    kv_part = jnp.dot(normed_m, wkv.reshape(1024, 2 * HD), preferred_element_type=f32)
    kv_own = jnp.sum(exchange(kv_part.reshape(8, 64, 2 * HD), MEM), axis=0) * inv_width
    cos_own = lax.dynamic_slice_in_dim(cosine_table, member * 64, 64)
    sin_own = lax.dynamic_slice_in_dim(sine_table, member * 64, 64)
    kv_own = jnp.concatenate(
        [rotate(kv_own[:, :HD], cos_own, sin_own), kv_own[:, HD:]], -1
    ).astype(bf16)
    kv = spread(kv_own, MEM).reshape(block_len, 2 * HD)

    queries = jnp.dot(normed, q_cols, preferred_element_type=f32) * inv_width
    q_rot = rotate(queries, cosine_table, sine_table).astype(bf16)

    grad_query, grad_key, grad_value = attend_back(
        q_rot, kv[:, :HD], kv[:, HD:], grad_context, allowed
    )
    scaled_q = (rotate(grad_query, cosine_table, -sine_table) * inv_width).astype(bf16)
    scaled_kv = (
        jnp.concatenate([rotate(grad_key, cosine_table, -sine_table), grad_value], -1) * inv_width
    ).astype(bf16)
    kv_sum = exchange(scaled_kv.reshape(8, 64, 2 * HD), MEM).astype(f32)
    kv_sum = jnp.sum(kv_sum, axis=0).astype(bf16)
    kv_sum = spread(kv_sum, MEM).reshape(block_len, 2 * HD)

    contract = (((0,), (0,)), ((), ()))
    part_q = lax.dot_general(normed, scaled_q, contract, preferred_element_type=f32).astype(bf16)
    part_q = exchange(part_q.reshape(4, 2048, HD), X).astype(f32)
    old_q = lax.dynamic_slice_in_dim(q_cols, ring * 2048, 2048)
    new_q = (old_q.astype(f32) - step_rate * jnp.sum(part_q, axis=0)).astype(bf16)
    near = swap(new_q)
    far = lax.ppermute(
        new_q,
        ("xh", "xl", "core"),
        [(h * 4 + l * 2 + c, (1 - h) * 4 + c * 2 + l) for h in (0, 1) for l in (0, 1) for c in (0, 1)],
    )
    near_c = flip(near, ("core",))
    far_c = flip(far, ("core",))
    near = ordered(near, near_c, core)
    far = ordered(far, far_c, core)
    low = ordered(near[0], far[0], xh)
    high = ordered(near[1], far[1], xh)
    roll_q = jnp.stack([low[0], high[0], low[1], high[1]], axis=0).reshape(D, HD)

    part_kv = lax.dot_general(normed_m, kv_sum, contract, preferred_element_type=f32).astype(bf16)
    part_kv = exchange(part_kv.reshape(4, 256, 2 * HD), X).astype(f32)
    old_kv = lax.dynamic_slice_in_dim(wkv, ring * 2, 2).reshape(256, 2 * HD)
    new_kv = (old_kv.astype(f32) - step_rate * jnp.sum(part_kv, axis=0)).astype(bf16)
    new_kv = spread(new_kv, ("zl",))
    new_kv = spread(new_kv, X)
    other = flip(new_kv, ("core",))
    new_kv = jnp.stack(ordered(new_kv, other, core), axis=0)
    new_kv = new_kv.reshape(2, 4, 4, 2, 128, 2 * HD).transpose(1, 3, 2, 0, 4, 5).reshape(D, 2 * HD)
    return roll_q, new_kv[:, :HD], new_kv[:, HD:]


def solution(mesh):
    grid = Mesh(
        mesh.devices.reshape(2, 4, 2, 4, 2, 2), ("xh", "y", "zh", "zl", "xl", "core")
    )
    groups = ("xh", "core")
    in_specs = (
        P(groups, FS, None),
        P(groups, None, FS),
        P(groups, None),
        P(groups, None),
        P(FS, None),
        P(FS, None),
        P(FS, None),
    )
    out_specs = (P(None, FS), P(None, FS), P(None, FS))
    return jax.shard_map(local, mesh=grid, in_specs=in_specs, out_specs=out_specs, check_vma=False)
```

```python
import jax
import jax.numpy as jnp
from jax import lax
from jax.sharding import Mesh, PartitionSpec as P

D = 8192
HD = 128
RESP = 8

step_rate = 200.0
rope_base = 1000000.0
norm_eps = 1e-06
masked_score = -1e30

YZ = ("y", "zh", "zl")
KH = ("y", "zh")
MEM = ("zl", "core")
X = ("xh", "xl")
FS = ("y", "zh", "zl", "xl")
Z = ("zh", "zl")


def rotate(field, cosine_table, sine_table):
    half_width = field.shape[-1] // 2
    lead_half = field[..., :half_width]
    tail_half = field[..., half_width:]
    return jnp.concatenate(
        [
            lead_half * cosine_table - tail_half * sine_table,
            tail_half * cosine_table + lead_half * sine_table,
        ],
        -1,
    )


def angles(seg_row):
    span_count = seg_row.shape[0]
    earlier = jnp.sum((seg_row[None, :] < seg_row[:, None]).astype(jnp.int32), axis=1)
    positions = jnp.arange(span_count, dtype=jnp.int32) - earlier
    frequency = rope_base ** (-jnp.arange(HD // 2, dtype=jnp.float32) * 2.0 / HD)
    phase_grid = positions.astype(jnp.float32)[:, None] * frequency[None, :]
    return jnp.cos(phase_grid), jnp.sin(phase_grid)


def token_weights(seg_row, advantage_row):
    id_range = jnp.arange(RESP + 1, dtype=jnp.int32)
    onehot = (seg_row[:, None] == id_range[None, :]).astype(jnp.float32)
    counts = jnp.sum(onehot, axis=0)[:RESP]
    per_token = -advantage_row / counts
    return jnp.sum(onehot[:, :RESP] * per_token[None, :], axis=1)


def attend_back(q_rot, k_rot, v_bf, grad_context, allowed):
    score_scale = HD ** (-0.5)
    f32 = jnp.float32
    scores = jnp.einsum("td,ud->tu", q_rot, k_rot, preferred_element_type=f32) * score_scale
    scores = jnp.where(allowed, scores, masked_score)
    row_top = jnp.max(scores, axis=-1, keepdims=True)
    exponent = jnp.exp(scores - row_top)
    attention = exponent / jnp.sum(exponent, axis=-1, keepdims=True)
    attention_bf = attention.astype(jnp.bfloat16)
    grad_prob = jnp.einsum("td,ud->tu", grad_context, v_bf, preferred_element_type=f32)
    inner_sum = jnp.sum(attention * grad_prob, axis=-1, keepdims=True)
    dscore = (attention * (grad_prob - inner_sum)).astype(jnp.bfloat16)
    grad_query = jnp.einsum("tu,ud->td", dscore, k_rot, preferred_element_type=f32) * score_scale
    grad_key = jnp.einsum("tu,td->ud", dscore, q_rot, preferred_element_type=f32) * score_scale
    grad_value = jnp.einsum("tu,td->ud", attention_bf, grad_context, preferred_element_type=f32)
    return grad_query, grad_key, grad_value


def swap(x):
    return lax.ppermute(x, ("xl", "core"), [(0, 0), (1, 2), (2, 1), (3, 3)])


def flip(x, axes):
    n = 2 ** len(axes)
    return lax.ppermute(x, axes, [(i, n - 1 - i) for i in range(n)])


def shift(x, axes, step):
    n = lax.axis_size(axes)
    return lax.ppermute(x, axes, [((i + step) % n, i) for i in range(n)])


def exchange(x, axes):
    return lax.all_to_all(x, axes, split_axis=0, concat_axis=0, tiled=True)


def spread(x, axes):
    n = lax.axis_size(axes)
    return exchange(jnp.broadcast_to(x[None], (n,) + x.shape), axes)


def ordered(mine, other, bit):
    first = jnp.where(bit == 0, mine, other)
    second = jnp.where(bit == 0, other, mine)
    return first, second


def x_ring(x, xh, xl):
    low = ordered(x, flip(x, ("xl",)), xl)
    high = ordered(flip(x, ("xh",)), flip(x, X), xl)
    col0 = ordered(low[0], high[0], xh)
    col1 = ordered(low[1], high[1], xh)
    return (col0[0], col1[0]), (col0[1], col1[1])


def ring_pieces(x, axes):
    n = lax.axis_size(axes)
    up = [x]
    down = [x]
    for _ in range(n // 2 - 1):
        up.append(shift(up[-1], axes, 1))
        down.append(shift(down[-1], axes, -1))
    half = x.shape[0] // 2
    if x.ndim == 2:
        width = x.shape[1] // 2
        far = jnp.concatenate(
            [shift(up[-1][:, :width], axes, 1), shift(down[-1][:, width:], axes, -1)], axis=1
        )
    else:
        far = jnp.concatenate(
            [shift(up[-1][:half], axes, 1), shift(down[-1][half:], axes, -1)], axis=0
        )
    return up + [far] + down[:0:-1]


def gather_rows(own):
    width = own.shape[1] // 2
    first, second = own[:, :width], own[:, width:]
    ys = jnp.stack([first] + [shift(first, ("y",), s) for s in (1, 2, 3)], axis=0)
    zs = jnp.stack(ring_pieces(second, Z), axis=0)
    firsts = [p.reshape(32, width) for p in ring_pieces(ys, Z)]
    seconds = [p.reshape(64, width) for p in ring_pieces(zs, ("y",))]
    firsts = firsts + [flip(p, ("core",)) for p in firsts]
    seconds = seconds + [flip(p, ("core",)) for p in seconds]
    return jnp.concatenate(firsts, axis=0), jnp.concatenate(seconds, axis=0)


def row_maps(core, y, z):
    f = jnp.arange(512, dtype=jnp.int32)
    c = core ^ (f // 256)
    first = ((((y + f // 8 % 4) % 4) * 8 + (z + f // 32 % 8) % 8) * 2 + c) * 8 + f % 8
    second = ((((y + f // 64 % 4) % 4) * 8 + (z + f // 8 % 8) % 8) * 2 + c) * 8 + f % 8
    at = jnp.concatenate([first, second])
    return at[None, :] == f[:, None]


def local(hidden, cotangent, seg_ids, advantage, w_query, w_key, w_value):
    f32 = jnp.float32
    bf16 = jnp.bfloat16
    inv_width = D ** (-0.5)
    xh = lax.axis_index("xh")
    xl = lax.axis_index("xl")
    core = lax.axis_index("core")
    zl = lax.axis_index("zl")
    member = zl * 2 + core
    ring = xh * 2 + xl

    token_rows = hidden[0].astype(f32)
    normed_own = (
        token_rows * lax.rsqrt(jnp.mean(token_rows * token_rows, axis=-1, keepdims=True) + norm_eps)
    ).astype(bf16)
    first, second = gather_rows(swap(normed_own))
    cot = swap(cotangent[0])
    seg_row = swap(seg_ids[0])
    adv_row = swap(advantage[0])
    block_len = first.shape[0]

    wq = w_query.reshape(2, 64, 32, 2, HD)
    wq = lax.dynamic_index_in_dim(wq, xh, 0, keepdims=False)
    wq = lax.dynamic_index_in_dim(wq, core, 2, keepdims=False)
    wq = exchange(wq.transpose(1, 0, 2), YZ)
    wkv = jnp.concatenate([w_key.reshape(4, 32, 8, HD), w_value.reshape(4, 32, 8, HD)], axis=-1)
    wkv = lax.dynamic_index_in_dim(wkv, xh * 2 + core, 0, keepdims=False)
    wkv = exchange(wkv.transpose(1, 0, 2), KH)
    wkv = spread(wkv, ("zl",))

    wq = x_ring(wq, xh, xl)
    q_cols = jnp.stack([wq[h][l] for l in (0, 1) for h in (0, 1)], axis=1).reshape(D, HD)
    wkv = x_ring(wkv, xh, xl)
    wkv = jnp.stack([wkv[h][l] for l in (0, 1) for h in (0, 1)], axis=0)
    wkv = jnp.stack(ordered(wkv, flip(wkv, ("core",)), core), axis=0)
    wkv = wkv.reshape(2, 2, 2, 4, 8, 32, 2 * HD).transpose(4, 3, 1, 2, 0, 5, 6).reshape(D, 2 * HD)
    cols = jnp.concatenate([q_cols, wkv], axis=1)

    cosine_table, sine_table = angles(seg_row)
    weight_row = token_weights(seg_row, adv_row)
    grad_context = (cot.astype(f32) * weight_row[:, None]).astype(bf16)
    place = jnp.arange(block_len, dtype=jnp.int32)
    allowed = (seg_row[:, None] == seg_row[None, :]) & (place[None, :] <= place[:, None])
    maps = row_maps(core, lax.axis_index("y"), lax.axis_index(Z))

    half = D // 2
    projected = jnp.concatenate(
        [
            jnp.dot(first, cols[:half], preferred_element_type=f32),
            jnp.dot(second, cols[half:], preferred_element_type=f32),
        ],
        axis=0,
    )
    projected = (
        jnp.dot(maps.astype(f32), projected, precision=lax.Precision.HIGHEST) * inv_width
    )
    q_rot = rotate(projected[:, :HD], cosine_table, sine_table).astype(bf16)
    k_rot = rotate(projected[:, HD : 2 * HD], cosine_table, sine_table).astype(bf16)
    v_bf = projected[:, 2 * HD :].astype(bf16)

    grad_query, grad_key, grad_value = attend_back(q_rot, k_rot, v_bf, grad_context, allowed)
    scaled_q = (rotate(grad_query, cosine_table, -sine_table) * inv_width).astype(bf16)
    scaled_kv = (
        jnp.concatenate([rotate(grad_key, cosine_table, -sine_table), grad_value], -1) * inv_width
    ).astype(bf16)

    contract = (((0,), (0,)), ((), ()))
    maps_bf = maps.astype(bf16)

    def to_rows(x):
        rows = lax.dot_general(maps_bf, x, contract, preferred_element_type=f32).astype(bf16)
        return rows[:block_len], rows[block_len:]

    q_first, q_second = to_rows(scaled_q)
    part_q = jnp.concatenate(
        [
            lax.dot_general(first, q_first, contract, preferred_element_type=f32).astype(bf16),
            lax.dot_general(second, q_second, contract, preferred_element_type=f32).astype(bf16),
        ],
        axis=0,
    )
    part_q, scaled_kv = lax.optimization_barrier((part_q, scaled_kv))
    part_q = exchange(part_q.reshape(4, 2048, HD), X).astype(f32)
    old_q = lax.dynamic_slice_in_dim(q_cols, ring * 2048, 2048)
    new_q = (old_q.astype(f32) - step_rate * jnp.sum(part_q, axis=0)).astype(bf16)
    near = swap(new_q)
    far = lax.ppermute(
        new_q,
        ("xh", "xl", "core"),
        [(h * 4 + l * 2 + c, (1 - h) * 4 + c * 2 + l) for h in (0, 1) for l in (0, 1) for c in (0, 1)],
    )
    near = ordered(near, flip(near, ("core",)), core)
    far = ordered(far, flip(far, ("core",)), core)
    low = ordered(near[0], far[0], xh)
    high = ordered(near[1], far[1], xh)
    roll_q = jnp.stack([low[0], high[0], low[1], high[1]], axis=0).reshape(D, HD)

    kv_sum = exchange(scaled_kv.reshape(8, 64, 2 * HD), MEM).astype(f32)
    kv_sum = jnp.sum(kv_sum, axis=0).astype(bf16)
    kv_sum = spread(kv_sum, MEM).reshape(block_len, 2 * HD)
    kv_first, kv_second = to_rows(kv_sum)

    def member_cols(x):
        return lax.dynamic_index_in_dim(
            x.reshape(block_len, 4, 8, HD), member, 2, keepdims=False
        ).reshape(block_len, 512)

    part_kv = jnp.concatenate(
        [
            lax.dot_general(
                member_cols(first), kv_first, contract, preferred_element_type=f32
            ).astype(bf16),
            lax.dot_general(
                member_cols(second), kv_second, contract, preferred_element_type=f32
            ).astype(bf16),
        ],
        axis=0,
    )
    part_kv = exchange(part_kv.reshape(4, 256, 2 * HD), X).astype(f32)
    old_kv = wkv.reshape(4, 2, 8, 128, 2 * HD)
    old_kv = lax.dynamic_index_in_dim(old_kv, ring, 0, keepdims=False)
    old_kv = lax.dynamic_index_in_dim(old_kv, member, 1, keepdims=False).reshape(256, 2 * HD)
    new_kv = (old_kv.astype(f32) - step_rate * jnp.sum(part_kv, axis=0)).astype(bf16)
    new_kv = spread(new_kv, ("zl",))
    new_kv = x_ring(new_kv, xh, xl)
    new_kv = jnp.stack([new_kv[h][l] for h in (0, 1) for l in (0, 1)], axis=0)
    other = flip(new_kv, ("core",))
    new_kv = jnp.stack(ordered(new_kv, other, core), axis=0)
    new_kv = new_kv.reshape(2, 4, 4, 2, 128, 2 * HD).transpose(1, 3, 2, 0, 4, 5).reshape(D, 2 * HD)
    return roll_q, new_kv[:, :HD], new_kv[:, HD:]


def solution(mesh):
    grid = Mesh(
        mesh.devices.reshape(2, 4, 2, 4, 2, 2), ("xh", "y", "zh", "zl", "xl", "core")
    )
    groups = ("xh", "core")
    in_specs = (
        P(groups, FS, None),
        P(groups, None, FS),
        P(groups, None),
        P(groups, None),
        P(FS, None),
        P(FS, None),
        P(FS, None),
    )
    out_specs = (P(None, FS), P(None, FS), P(None, FS))
    return jax.shard_map(local, mesh=grid, in_specs=in_specs, out_specs=out_specs, check_vma=False)
```

```python
import jax
import jax.numpy as jnp
from jax import lax
from jax.experimental import pallas as pl
from jax.experimental.pallas import tpu as pltpu
from jax.sharding import Mesh, PartitionSpec as P

D = 8192
HD = 128
RESP = 8

step_rate = 200.0
rope_base = 1000000.0
norm_eps = 1e-06
masked_score = -1e30

YZ = ("y", "zh", "zl")
KH = ("y", "zh")
MEM = ("zl", "core")
X = ("xh", "xl")
FS = ("y", "zh", "zl", "xl")
Z = ("zh", "zl")


def rotate(field, cosine_table, sine_table):
    half_width = field.shape[-1] // 2
    lead_half = field[..., :half_width]
    tail_half = field[..., half_width:]
    return jnp.concatenate(
        [
            lead_half * cosine_table - tail_half * sine_table,
            tail_half * cosine_table + lead_half * sine_table,
        ],
        -1,
    )


def angles(seg_row):
    span_count = seg_row.shape[0]
    earlier = jnp.sum((seg_row[None, :] < seg_row[:, None]).astype(jnp.int32), axis=1)
    positions = jnp.arange(span_count, dtype=jnp.int32) - earlier
    frequency = rope_base ** (-jnp.arange(HD // 2, dtype=jnp.float32) * 2.0 / HD)
    phase_grid = positions.astype(jnp.float32)[:, None] * frequency[None, :]
    return jnp.cos(phase_grid), jnp.sin(phase_grid)


def token_weights(seg_row, advantage_row):
    id_range = jnp.arange(RESP + 1, dtype=jnp.int32)
    onehot = (seg_row[:, None] == id_range[None, :]).astype(jnp.float32)
    counts = jnp.sum(onehot, axis=0)[:RESP]
    per_token = -advantage_row / counts
    return jnp.sum(onehot[:, :RESP] * per_token[None, :], axis=1)


def attend_back(q_rot, k_rot, v_bf, grad_context, allowed):
    score_scale = HD ** (-0.5)
    f32 = jnp.float32
    scores = jnp.einsum("td,ud->tu", q_rot, k_rot, preferred_element_type=f32) * score_scale
    scores = jnp.where(allowed, scores, masked_score)
    row_top = jnp.max(scores, axis=-1, keepdims=True)
    exponent = jnp.exp(scores - row_top)
    attention = exponent / jnp.sum(exponent, axis=-1, keepdims=True)
    attention_bf = attention.astype(jnp.bfloat16)
    grad_prob = jnp.einsum("td,ud->tu", grad_context, v_bf, preferred_element_type=f32)
    inner_sum = jnp.sum(attention * grad_prob, axis=-1, keepdims=True)
    dscore = (attention * (grad_prob - inner_sum)).astype(jnp.bfloat16)
    grad_query = jnp.einsum("tu,ud->td", dscore, k_rot, preferred_element_type=f32) * score_scale
    grad_key = jnp.einsum("tu,td->ud", dscore, q_rot, preferred_element_type=f32) * score_scale
    grad_value = jnp.einsum("tu,td->ud", attention_bf, grad_context, preferred_element_type=f32)
    return grad_query, grad_key, grad_value


def swap(x):
    return lax.ppermute(x, ("xl", "core"), [(0, 0), (1, 2), (2, 1), (3, 3)])


def flip(x, axes):
    n = 2 ** len(axes)
    return lax.ppermute(x, axes, [(i, n - 1 - i) for i in range(n)])


def shift(x, axes, step):
    n = lax.axis_size(axes)
    return lax.ppermute(x, axes, [((i + step) % n, i) for i in range(n)])


def exchange(x, axes):
    return lax.all_to_all(x, axes, split_axis=0, concat_axis=0, tiled=True)


def spread(x, axes):
    n = lax.axis_size(axes)
    return exchange(jnp.broadcast_to(x[None], (n,) + x.shape), axes)


def ordered(mine, other, bit):
    first = jnp.where(bit == 0, mine, other)
    second = jnp.where(bit == 0, other, mine)
    return first, second


def x_ring(x, xh, xl):
    low = ordered(x, flip(x, ("xl",)), xl)
    high = ordered(flip(x, ("xh",)), flip(x, X), xl)
    col0 = ordered(low[0], high[0], xh)
    col1 = ordered(low[1], high[1], xh)
    return (col0[0], col1[0]), (col0[1], col1[1])


def place(pieces, shape, at):
    arrays = [p for p, _ in pieces]

    def body(at_ref, *refs):
        sources, out, sems = refs[:-2], refs[-2], refs[-1]
        copies = [
            pltpu.make_async_copy(source, where(out, at_ref), sems.at[n])
            for n, (source, (_, where)) in enumerate(zip(sources, pieces))
        ]
        for copy in copies:
            copy.start()
        for copy in copies:
            copy.wait()

    return pl.pallas_call(
        body,
        out_shape=jax.ShapeDtypeStruct(shape, arrays[0].dtype),
        in_specs=[pl.BlockSpec(memory_space=pltpu.SMEM)]
        + [pl.BlockSpec(memory_space=pl.ANY)] * len(arrays),
        out_specs=pl.BlockSpec(memory_space=pl.ANY),
        scratch_shapes=[pltpu.SemaphoreType.DMA((len(arrays),))],
        name="place",
    )(at, *arrays)


def gather_rows(own, y, z):
    at = jnp.stack([y, z]).astype(jnp.int32)
    half = D // 2
    first, second = own[:, :half], own[:, half:]

    ys = [(first, lambda o, at: o.at[at[0]])]
    for step in (1, 2, 3):
        ys.append(
            (shift(first, ("y",), step), lambda o, at, s=step: o.at[lax.rem(at[0] + s, 4)])
        )

    zs = [(second, lambda o, at: o.at[at[1]])]
    up = down = second
    for step in (1, 2, 3):
        up, down = shift(up, Z, 1), shift(down, Z, -1)
        zs.append((up, lambda o, at, s=step: o.at[lax.rem(at[1] + s, 8)]))
        zs.append((down, lambda o, at, s=step: o.at[lax.rem(at[1] + 8 - s, 8)]))
    quarter = half // 2
    up, down = shift(up[:, :quarter], Z, 1), shift(down[:, quarter:], Z, -1)
    zs.append((up, lambda o, at: o.at[lax.rem(at[1] + 4, 8), :, pl.ds(0, quarter)]))
    zs.append((down, lambda o, at: o.at[lax.rem(at[1] + 4, 8), :, pl.ds(quarter, quarter)]))

    first = place(ys, (4, 8, half), at)
    low = pl.ds(0, half)
    out = [(first, lambda o, at: o.at[:, at[1], :, low])]
    up = down = first
    for step in (1, 2, 3):
        up, down = shift(up, Z, 1), shift(down, Z, -1)
        out.append((up, lambda o, at, s=step: o.at[:, lax.rem(at[1] + s, 8), :, low]))
        out.append((down, lambda o, at, s=step: o.at[:, lax.rem(at[1] + 8 - s, 8), :, low]))
    up, down = shift(up[:2], Z, 1), shift(down[2:], Z, -1)
    out.append((up, lambda o, at: o.at[pl.ds(0, 2), lax.rem(at[1] + 4, 8), :, low]))
    out.append((down, lambda o, at: o.at[pl.ds(2, 2), lax.rem(at[1] + 4, 8), :, low]))

    second = place(zs, (8, 8, half), at)
    high = pl.ds(half, half)
    up, down = shift(second, ("y",), 1), shift(second, ("y",), -1)
    out.append((second, lambda o, at: o.at[at[0], :, :, high]))
    out.append((up, lambda o, at: o.at[lax.rem(at[0] + 1, 4), :, :, high]))
    out.append((down, lambda o, at: o.at[lax.rem(at[0] + 3, 4), :, :, high]))
    up, down = shift(up[:4], ("y",), 1), shift(down[4:], ("y",), -1)
    out.append((up, lambda o, at: o.at[lax.rem(at[0] + 2, 4), pl.ds(0, 4), :, high]))
    out.append((down, lambda o, at: o.at[lax.rem(at[0] + 2, 4), pl.ds(4, 4), :, high]))
    return place(out, (4, 8, 8, D), at).reshape(256, D)


def member_parts(own, other, kv_own, kv_other, member):
    def body(at_ref, own_ref, other_ref, a_ref, b_ref, out_ref):
        contract = (((0,), (0,)), ((), ()))
        out_ref[...] = (
            lax.dot_general(own_ref[...], a_ref[...], contract, preferred_element_type=jnp.float32)
            + lax.dot_general(
                other_ref[...], b_ref[...], contract, preferred_element_type=jnp.float32
            )
        ).astype(jnp.bfloat16)

    rows = pl.BlockSpec((256, HD), lambda b, at: (0, b * 8 + at[0]))
    whole = pl.BlockSpec((256, 2 * HD), lambda b, at: (0, 0))
    return pl.pallas_call(
        body,
        out_shape=jax.ShapeDtypeStruct((1024, 2 * HD), jnp.bfloat16),
        grid_spec=pltpu.PrefetchScalarGridSpec(
            num_scalar_prefetch=1,
            grid=(8,),
            in_specs=[rows, rows, whole, whole],
            out_specs=pl.BlockSpec((HD, 2 * HD), lambda b, at: (b, 0)),
        ),
        name="member_parts",
    )(member.reshape(1).astype(jnp.int32), own, other, kv_own, kv_other)


def local(hidden, cotangent, seg_ids, advantage, w_query, w_key, w_value):
    f32 = jnp.float32
    bf16 = jnp.bfloat16
    inv_width = D ** (-0.5)
    xh = lax.axis_index("xh")
    xl = lax.axis_index("xl")
    core = lax.axis_index("core")
    zl = lax.axis_index("zl")
    member = zl * 2 + core
    ring = xh * 2 + xl

    token_rows = hidden[0].astype(f32)
    normed_own = (
        token_rows * lax.rsqrt(jnp.mean(token_rows * token_rows, axis=-1, keepdims=True) + norm_eps)
    ).astype(bf16)
    own = gather_rows(swap(normed_own), lax.axis_index("y"), lax.axis_index(Z))
    other = flip(own, ("core",))
    cot = swap(cotangent[0])
    seg_row = swap(seg_ids[0])
    adv_row = swap(advantage[0])
    block_len = 512

    def by_core(x):
        x = x.reshape(32, 2, 8, x.shape[-1])
        mine = lax.dynamic_index_in_dim(x, core, 1, keepdims=False)
        theirs = lax.dynamic_index_in_dim(x, 1 - core, 1, keepdims=False)
        return mine.reshape(256, x.shape[-1]), theirs.reshape(256, x.shape[-1])

    def in_place(mine, theirs):
        n = mine.shape[-1]
        both = ordered(mine.reshape(32, 8, n), theirs.reshape(32, 8, n), core)
        return jnp.stack(both, axis=1).reshape(block_len, n)

    wq = w_query.reshape(2, 64, 32, 2, HD)
    wq = lax.dynamic_index_in_dim(wq, xh, 0, keepdims=False)
    wq = lax.dynamic_index_in_dim(wq, core, 2, keepdims=False).transpose(1, 0, 2)
    wkv = jnp.stack([w_key.reshape(4, 4, 8, 8, HD), w_value.reshape(4, 4, 8, 8, HD)], axis=2)
    wkv = lax.dynamic_index_in_dim(wkv, xh * 2 + core, 0, keepdims=False)
    wkv = wkv.transpose(3, 0, 1, 2, 4).reshape(32, 16, HD)
    cut = exchange(jnp.concatenate([wq, wkv], axis=1), YZ)
    wq = cut[:, :64]
    wkv = spread(cut[:, 64:], ("zl",))

    wq = x_ring(wq, xh, xl)
    q_cols = jnp.stack([wq[h][l] for l in (0, 1) for h in (0, 1)], axis=1).reshape(D, HD)
    wkv = x_ring(wkv, xh, xl)
    wkv = jnp.stack([wkv[h][l] for l in (0, 1) for h in (0, 1)], axis=0)
    wkv = jnp.stack(ordered(wkv, flip(wkv, ("core",)), core), axis=0)
    wkv = wkv.reshape(2, 2, 2, 4, 32, 2, 8, HD).transpose(4, 1, 2, 0, 3, 6, 5, 7)
    wkv = wkv.reshape(D, 2 * HD)

    cosine_table, sine_table = angles(seg_row)
    weight_row = token_weights(seg_row, adv_row)
    grad_context = (cot.astype(f32) * weight_row[:, None]).astype(bf16)
    position = jnp.arange(block_len, dtype=jnp.int32)
    allowed = (seg_row[:, None] == seg_row[None, :]) & (position[None, :] <= position[:, None])

    def project(cols):
        return in_place(
            jnp.dot(own, cols, preferred_element_type=f32),
            jnp.dot(other, cols, preferred_element_type=f32),
        ) * inv_width

    queries = project(q_cols)
    keys_values = project(wkv)
    q_rot = rotate(queries, cosine_table, sine_table).astype(bf16)
    k_rot = rotate(keys_values[:, :HD], cosine_table, sine_table).astype(bf16)
    v_bf = keys_values[:, HD:].astype(bf16)

    grad_query, grad_key, grad_value = attend_back(q_rot, k_rot, v_bf, grad_context, allowed)
    scaled_q = (rotate(grad_query, cosine_table, -sine_table) * inv_width).astype(bf16)
    scaled_kv = (
        jnp.concatenate([rotate(grad_key, cosine_table, -sine_table), grad_value], -1) * inv_width
    ).astype(bf16)

    contract = (((0,), (0,)), ((), ()))
    q_own, q_other = by_core(scaled_q)
    part_q = (
        lax.dot_general(own, q_own, contract, preferred_element_type=f32)
        + lax.dot_general(other, q_other, contract, preferred_element_type=f32)
    ).astype(bf16).reshape(4, 2048, HD)
    part_q, scaled_kv = lax.optimization_barrier((part_q, scaled_kv))

    def to_ring(mask, axes):
        return flip(lax.dynamic_index_in_dim(part_q, ring ^ mask, 0, keepdims=False), axes)

    sum_q = (
        lax.dynamic_index_in_dim(part_q, ring, 0, keepdims=False).astype(f32)
        + to_ring(1, ("xl",)).astype(f32)
        + to_ring(3, X).astype(f32)
        + to_ring(2, ("xh",)).astype(f32)
    )
    old_q = lax.dynamic_slice_in_dim(q_cols, ring * 2048, 2048)
    new_q = (old_q.astype(f32) - step_rate * sum_q).astype(bf16)
    near = swap(new_q)
    far = lax.ppermute(
        new_q,
        ("xh", "xl", "core"),
        [(h * 4 + l * 2 + c, (1 - h) * 4 + c * 2 + l) for h in (0, 1) for l in (0, 1) for c in (0, 1)],
    )
    near = ordered(near, flip(near, ("core",)), core)
    far = ordered(far, flip(far, ("core",)), core)
    low = ordered(near[0], far[0], xh)
    high = ordered(near[1], far[1], xh)
    roll_q = jnp.stack([low[0], high[0], low[1], high[1]], axis=0).reshape(D, HD)

    kv_sum = exchange(scaled_kv.reshape(8, 64, 2 * HD), MEM).astype(f32)
    kv_sum = jnp.sum(kv_sum, axis=0).astype(bf16)
    kv_sum = spread(kv_sum, MEM).reshape(block_len, 2 * HD)
    kv_own, kv_other = by_core(kv_sum)
    part_kv = member_parts(own, other, kv_own, kv_other, member)
    part_kv = exchange(part_kv.reshape(4, 256, 2 * HD), X).astype(f32)
    old_kv = wkv.reshape(4, 2, 8, 128, 2 * HD)
    old_kv = lax.dynamic_index_in_dim(old_kv, ring, 0, keepdims=False)
    old_kv = lax.dynamic_index_in_dim(old_kv, member, 1, keepdims=False).reshape(256, 2 * HD)
    new_kv = (old_kv.astype(f32) - step_rate * jnp.sum(part_kv, axis=0)).astype(bf16)
    new_kv = spread(new_kv, ("zl",))
    new_kv = x_ring(new_kv, xh, xl)
    new_kv = jnp.stack([new_kv[h][l] for h in (0, 1) for l in (0, 1)], axis=0)
    new_kv = jnp.stack(ordered(new_kv, flip(new_kv, ("core",)), core), axis=0)
    new_kv = new_kv.reshape(2, 4, 4, 2, 128, 2 * HD).transpose(1, 3, 2, 0, 4, 5).reshape(D, 2 * HD)
    return roll_q, new_kv[:, :HD], new_kv[:, HD:]


def solution(mesh):
    grid = Mesh(
        mesh.devices.reshape(2, 4, 2, 4, 2, 2), ("xh", "y", "zh", "zl", "xl", "core")
    )
    groups = ("xh", "core")
    in_specs = (
        P(groups, FS, None),
        P(groups, None, FS),
        P(groups, None),
        P(groups, None),
        P(FS, None),
        P(FS, None),
        P(FS, None),
    )
    out_specs = (P(None, FS), P(None, FS), P(None, FS))
    return jax.shard_map(local, mesh=grid, in_specs=in_specs, out_specs=out_specs, check_vma=False)
```

```python
import jax
import jax.numpy as jnp
from jax import lax
from jax.experimental import pallas as pl
from jax.experimental.pallas import tpu as pltpu
from jax.sharding import Mesh, PartitionSpec as P

D = 8192
HD = 128
RESP = 8

step_rate = 200.0
rope_base = 1000000.0
norm_eps = 1e-06
masked_score = -1e30

YZ = ("y", "zh", "zl")
MEM = ("zl", "core")
X = ("xh", "xl")
FS = ("y", "zh", "zl", "xl")


def rotate(field, cosine_table, sine_table):
    half_width = field.shape[-1] // 2
    lead_half = field[..., :half_width]
    tail_half = field[..., half_width:]
    return jnp.concatenate(
        [
            lead_half * cosine_table - tail_half * sine_table,
            tail_half * cosine_table + lead_half * sine_table,
        ],
        -1,
    )


def angles(seg_row):
    span_count = seg_row.shape[0]
    earlier = jnp.sum((seg_row[None, :] < seg_row[:, None]).astype(jnp.int32), axis=1)
    positions = jnp.arange(span_count, dtype=jnp.int32) - earlier
    frequency = rope_base ** (-jnp.arange(HD // 2, dtype=jnp.float32) * 2.0 / HD)
    phase_grid = positions.astype(jnp.float32)[:, None] * frequency[None, :]
    return jnp.cos(phase_grid), jnp.sin(phase_grid)


def token_weights(seg_row, advantage_row):
    id_range = jnp.arange(RESP + 1, dtype=jnp.int32)
    onehot = (seg_row[:, None] == id_range[None, :]).astype(jnp.float32)
    counts = jnp.sum(onehot, axis=0)[:RESP]
    per_token = -advantage_row / counts
    return jnp.sum(onehot[:, :RESP] * per_token[None, :], axis=1)


def attend_back(q_rot, k_rot, v_bf, grad_context, allowed):
    score_scale = HD ** (-0.5)
    f32 = jnp.float32
    scores = jnp.einsum("td,ud->tu", q_rot, k_rot, preferred_element_type=f32) * score_scale
    scores = jnp.where(allowed, scores, masked_score)
    row_top = jnp.max(scores, axis=-1, keepdims=True)
    exponent = jnp.exp(scores - row_top)
    attention = exponent / jnp.sum(exponent, axis=-1, keepdims=True)
    attention_bf = attention.astype(jnp.bfloat16)
    grad_prob = jnp.einsum("td,ud->tu", grad_context, v_bf, preferred_element_type=f32)
    inner_sum = jnp.sum(attention * grad_prob, axis=-1, keepdims=True)
    dscore = (attention * (grad_prob - inner_sum)).astype(jnp.bfloat16)
    grad_query = jnp.einsum("tu,ud->td", dscore, k_rot, preferred_element_type=f32) * score_scale
    grad_key = jnp.einsum("tu,td->ud", dscore, q_rot, preferred_element_type=f32) * score_scale
    grad_value = jnp.einsum("tu,td->ud", attention_bf, grad_context, preferred_element_type=f32)
    return grad_query, grad_key, grad_value


def swap(x):
    return lax.ppermute(x, ("xl", "core"), [(0, 0), (1, 2), (2, 1), (3, 3)])


def flip(x, axes):
    n = 2 ** len(axes)
    return lax.ppermute(x, axes, [(i, n - 1 - i) for i in range(n)])


def exchange(x, axes):
    return lax.all_to_all(x, axes, split_axis=0, concat_axis=0, tiled=True)


def spread(x, axes):
    n = lax.axis_size(axes)
    return exchange(jnp.broadcast_to(x[None], (n,) + x.shape), axes)


def ordered(mine, other, bit):
    first = jnp.where(bit == 0, mine, other)
    second = jnp.where(bit == 0, other, mine)
    return first, second


def x_ring(x, xh, xl):
    low = ordered(x, flip(x, ("xl",)), xl)
    high = ordered(flip(x, ("xh",)), flip(x, X), xl)
    col0 = ordered(low[0], high[0], xh)
    col1 = ordered(low[1], high[1], xh)
    return (col0[0], col1[0]), (col0[1], col1[1])


def member_parts(normed, kv, member):
    def body(at_ref, rows_ref, kv_ref, out_ref):
        out_ref[...] = lax.dot_general(
            rows_ref[...],
            kv_ref[...],
            (((0,), (0,)), ((), ())),
            preferred_element_type=jnp.float32,
        ).astype(jnp.bfloat16)

    return pl.pallas_call(
        body,
        out_shape=jax.ShapeDtypeStruct((1024, 2 * HD), jnp.bfloat16),
        grid_spec=pltpu.PrefetchScalarGridSpec(
            num_scalar_prefetch=1,
            grid=(8,),
            in_specs=[
                pl.BlockSpec((512, HD), lambda b, at: (0, b * 8 + at[0])),
                pl.BlockSpec((512, 2 * HD), lambda b, at: (0, 0)),
            ],
            out_specs=pl.BlockSpec((HD, 2 * HD), lambda b, at: (b, 0)),
        ),
        name="member_parts",
    )(member.reshape(1).astype(jnp.int32), normed, kv)


def local(hidden, cotangent, seg_ids, advantage, w_query, w_key, w_value):
    f32 = jnp.float32
    bf16 = jnp.bfloat16
    inv_width = D ** (-0.5)
    xh = lax.axis_index("xh")
    xl = lax.axis_index("xl")
    core = lax.axis_index("core")
    zl = lax.axis_index("zl")
    member = zl * 2 + core
    ring = xh * 2 + xl

    token_rows = hidden[0].astype(f32)
    normed_own = (
        token_rows * lax.rsqrt(jnp.mean(token_rows * token_rows, axis=-1, keepdims=True) + norm_eps)
    ).astype(bf16)
    normed = lax.all_gather(swap(normed_own), YZ + ("core",), axis=0, tiled=True)
    cot = swap(cotangent[0])
    seg_row = swap(seg_ids[0])
    adv_row = swap(advantage[0])
    block_len = 512

    wq = w_query.reshape(2, 64, 32, 2, HD)
    wq = lax.dynamic_index_in_dim(wq, xh, 0, keepdims=False)
    wq = lax.dynamic_index_in_dim(wq, core, 2, keepdims=False).transpose(1, 0, 2)
    wkv = jnp.stack([w_key.reshape(4, 4, 8, 8, HD), w_value.reshape(4, 4, 8, 8, HD)], axis=2)
    wkv = lax.dynamic_index_in_dim(wkv, xh * 2 + core, 0, keepdims=False)
    wkv = wkv.transpose(3, 0, 1, 2, 4).reshape(32, 16, HD)
    cut = exchange(jnp.concatenate([wq, wkv], axis=1), YZ)
    wq = cut[:, :64]
    wkv = spread(cut[:, 64:], ("zl",))

    wq = x_ring(wq, xh, xl)
    q_cols = jnp.stack([wq[h][l] for l in (0, 1) for h in (0, 1)], axis=1).reshape(D, HD)
    wkv = x_ring(wkv, xh, xl)
    wkv = jnp.stack([wkv[h][l] for l in (0, 1) for h in (0, 1)], axis=0)
    wkv = jnp.stack(ordered(wkv, flip(wkv, ("core",)), core), axis=0)
    wkv = wkv.reshape(2, 2, 2, 4, 32, 2, 8, HD).transpose(4, 1, 2, 0, 3, 6, 5, 7)
    wkv = wkv.reshape(D, 2 * HD)

    cosine_table, sine_table = angles(seg_row)
    weight_row = token_weights(seg_row, adv_row)
    grad_context = (cot.astype(f32) * weight_row[:, None]).astype(bf16)
    position = jnp.arange(block_len, dtype=jnp.int32)
    allowed = (seg_row[:, None] == seg_row[None, :]) & (position[None, :] <= position[:, None])

    def project(cols):
        return jnp.dot(normed, cols, preferred_element_type=f32) * inv_width

    queries = project(q_cols)
    keys_values = project(wkv)
    q_rot = rotate(queries, cosine_table, sine_table).astype(bf16)
    k_rot = rotate(keys_values[:, :HD], cosine_table, sine_table).astype(bf16)
    v_bf = keys_values[:, HD:].astype(bf16)

    grad_query, grad_key, grad_value = attend_back(q_rot, k_rot, v_bf, grad_context, allowed)
    scaled_q = (rotate(grad_query, cosine_table, -sine_table) * inv_width).astype(bf16)
    scaled_kv = (
        jnp.concatenate([rotate(grad_key, cosine_table, -sine_table), grad_value], -1) * inv_width
    ).astype(bf16)

    contract = (((0,), (0,)), ((), ()))
    part_q = lax.dot_general(normed, scaled_q, contract, preferred_element_type=f32)
    part_q = part_q.astype(bf16).reshape(4, 2048, HD)
    part_q, scaled_kv = lax.optimization_barrier((part_q, scaled_kv))

    def to_ring(mask, axes):
        piece = lax.dynamic_index_in_dim(part_q, ring ^ mask, 0, keepdims=False)
        return flip(piece, axes)

    sum_q = (
        lax.dynamic_index_in_dim(part_q, ring, 0, keepdims=False).astype(f32)
        + to_ring(1, ("xl",)).astype(f32)
        + to_ring(3, X).astype(f32)
        + to_ring(2, ("xh",)).astype(f32)
    )
    old_q = lax.dynamic_slice_in_dim(q_cols, ring * 2048, 2048)
    new_q = (old_q.astype(f32) - step_rate * sum_q).astype(bf16)
    near = swap(new_q)
    far = lax.ppermute(
        new_q,
        ("xh", "xl", "core"),
        [
            (h * 4 + l * 2 + c, (1 - h) * 4 + c * 2 + l)
            for h in (0, 1)
            for l in (0, 1)
            for c in (0, 1)
        ],
    )
    near_other = flip(near, ("core",))
    far_other = flip(far, ("core",))
    near = ordered(near, near_other, core)
    far = ordered(far, far_other, core)
    low = ordered(near[0], far[0], xh)
    high = ordered(near[1], far[1], xh)
    roll_q = jnp.stack([low[0], high[0], low[1], high[1]], axis=0).reshape(D, HD)

    kv_sum = exchange(scaled_kv.reshape(8, 64, 2 * HD), MEM)
    kv_sum = kv_sum.astype(f32)
    kv_sum = jnp.sum(kv_sum, axis=0).astype(bf16)
    kv_sum = spread(kv_sum, MEM).reshape(block_len, 2 * HD)
    part_kv = member_parts(normed, kv_sum, member)
    part_kv = exchange(part_kv.reshape(4, 256, 2 * HD), X).astype(f32)
    old_kv = wkv.reshape(4, 2, 8, 128, 2 * HD)
    old_kv = lax.dynamic_index_in_dim(old_kv, ring, 0, keepdims=False)
    old_kv = lax.dynamic_index_in_dim(old_kv, member, 1, keepdims=False).reshape(256, 2 * HD)
    new_kv = (old_kv.astype(f32) - step_rate * jnp.sum(part_kv, axis=0)).astype(bf16)
    new_kv = spread(new_kv, ("zl",))
    new_kv = x_ring(new_kv, xh, xl)
    new_kv = jnp.stack([new_kv[h][l] for h in (0, 1) for l in (0, 1)], axis=0)
    new_kv = jnp.stack(ordered(new_kv, flip(new_kv, ("core",)), core), axis=0)
    new_kv = new_kv.reshape(2, 4, 4, 2, 128, 2 * HD).transpose(1, 3, 2, 0, 4, 5).reshape(D, 2 * HD)
    return roll_q, new_kv[:, :HD], new_kv[:, HD:]


def solution(mesh):
    grid = Mesh(
        mesh.devices.reshape(2, 4, 2, 4, 2, 2), ("xh", "y", "zh", "zl", "xl", "core")
    )
    groups = ("xh", "core")
    in_specs = (
        P(groups, FS, None),
        P(groups, None, FS),
        P(groups, None),
        P(groups, None),
        P(FS, None),
        P(FS, None),
        P(FS, None),
    )
    out_specs = (P(None, FS), P(None, FS), P(None, FS))

    return jax.shard_map(local, mesh=grid, in_specs=in_specs, out_specs=out_specs, check_vma=False)
```

```python
import jax
import jax.numpy as jnp
from jax import lax
from jax.experimental import pallas as pl
from jax.experimental.pallas import tpu as pltpu
from jax.sharding import Mesh, PartitionSpec as P

D = 8192
HD = 128
RESP = 8

step_rate = 200.0
rope_base = 1000000.0
norm_eps = 1e-06
masked_score = -1e30

YZ = ("y", "zh", "zl")
MEM = ("zl", "core")
X = ("xh", "xl")
FS = ("y", "zh", "zl", "xl")


def rotate(field, cosine_table, sine_table):
    half_width = field.shape[-1] // 2
    lead_half = field[..., :half_width]
    tail_half = field[..., half_width:]
    return jnp.concatenate(
        [
            lead_half * cosine_table - tail_half * sine_table,
            tail_half * cosine_table + lead_half * sine_table,
        ],
        -1,
    )


def angles(seg_row):
    span_count = seg_row.shape[0]
    earlier = jnp.sum((seg_row[None, :] < seg_row[:, None]).astype(jnp.int32), axis=1)
    positions = jnp.arange(span_count, dtype=jnp.int32) - earlier
    frequency = rope_base ** (-jnp.arange(HD // 2, dtype=jnp.float32) * 2.0 / HD)
    phase_grid = positions.astype(jnp.float32)[:, None] * frequency[None, :]
    return jnp.cos(phase_grid), jnp.sin(phase_grid)


def token_weights(seg_row, advantage_row):
    id_range = jnp.arange(RESP + 1, dtype=jnp.int32)
    onehot = (seg_row[:, None] == id_range[None, :]).astype(jnp.float32)
    counts = jnp.sum(onehot, axis=0)[:RESP]
    per_token = -advantage_row / counts
    return jnp.sum(onehot[:, :RESP] * per_token[None, :], axis=1)


def attend_back(q_rot, k_rot, v_bf, grad_context, allowed):
    score_scale = HD ** (-0.5)
    f32 = jnp.float32
    scores = jnp.einsum("td,ud->tu", q_rot, k_rot, preferred_element_type=f32) * score_scale
    scores = jnp.where(allowed, scores, masked_score)
    row_top = jnp.max(scores, axis=-1, keepdims=True)
    exponent = jnp.exp(scores - row_top)
    attention = exponent / jnp.sum(exponent, axis=-1, keepdims=True)
    attention_bf = attention.astype(jnp.bfloat16)
    grad_prob = jnp.einsum("td,ud->tu", grad_context, v_bf, preferred_element_type=f32)
    inner_sum = jnp.sum(attention * grad_prob, axis=-1, keepdims=True)
    dscore = (attention * (grad_prob - inner_sum)).astype(jnp.bfloat16)
    grad_query = jnp.einsum("tu,ud->td", dscore, k_rot, preferred_element_type=f32) * score_scale
    grad_key = jnp.einsum("tu,td->ud", dscore, q_rot, preferred_element_type=f32) * score_scale
    grad_value = jnp.einsum("tu,td->ud", attention_bf, grad_context, preferred_element_type=f32)
    return grad_query, grad_key, grad_value


def swap(x):
    return lax.ppermute(x, ("xl", "core"), [(0, 0), (1, 2), (2, 1), (3, 3)])


def flip(x, axes):
    n = 2 ** len(axes)
    return lax.ppermute(x, axes, [(i, n - 1 - i) for i in range(n)])


def exchange(x, axes):
    return lax.all_to_all(x, axes, split_axis=0, concat_axis=0, tiled=True)


def spread(x, axes):
    n = lax.axis_size(axes)
    return exchange(jnp.broadcast_to(x[None], (n,) + x.shape), axes)


def ordered(mine, other, bit):
    first = jnp.where(bit == 0, mine, other)
    second = jnp.where(bit == 0, other, mine)
    return first, second


def x_ring(x, xh, xl):
    near, wrap = flip(x, ("xl",)), flip(x, X)
    half = x.shape[0] // 2
    far = jnp.concatenate([flip(wrap[:half], ("xl",)), flip(near[half:], X)], axis=0)
    low = ordered(x, near, xl)
    high = ordered(far, wrap, xl)
    col0 = ordered(low[0], high[0], xh)
    col1 = ordered(low[1], high[1], xh)
    return (col0[0], col1[0]), (col0[1], col1[1])


def member_columns(normed, member):
    def body(at_ref, rows_ref, out_ref):
        out_ref[...] = rows_ref[...]

    return pl.pallas_call(
        body,
        out_shape=jax.ShapeDtypeStruct((512, 1024), jnp.bfloat16),
        grid_spec=pltpu.PrefetchScalarGridSpec(
            num_scalar_prefetch=1,
            grid=(8,),
            in_specs=[pl.BlockSpec((512, HD), lambda b, at: (0, b * 8 + at[0]))],
            out_specs=pl.BlockSpec((512, HD), lambda b, at: (0, b)),
        ),
        name="member_columns",
    )(member.reshape(1).astype(jnp.int32), normed)


def local(hidden, cotangent, seg_ids, advantage, w_query, w_key, w_value):
    f32 = jnp.float32
    bf16 = jnp.bfloat16
    inv_width = D ** (-0.5)
    xh = lax.axis_index("xh")
    xl = lax.axis_index("xl")
    core = lax.axis_index("core")
    zl = lax.axis_index("zl")
    member = zl * 2 + core
    ring = xh * 2 + xl

    token_rows = hidden[0].astype(f32)
    normed_own = (
        token_rows * lax.rsqrt(jnp.mean(token_rows * token_rows, axis=-1, keepdims=True) + norm_eps)
    ).astype(bf16)
    normed = lax.all_gather(swap(normed_own), YZ + ("core",), axis=0, tiled=True)
    cot = swap(cotangent[0])
    seg_row = swap(seg_ids[0])
    adv_row = swap(advantage[0])
    block_len = 512

    wq = w_query.reshape(2, 64, 32, 2, HD)
    wq = lax.dynamic_index_in_dim(wq, xh, 0, keepdims=False)
    wq = lax.dynamic_index_in_dim(wq, core, 2, keepdims=False).transpose(1, 0, 2)
    wkv = jnp.stack([w_key.reshape(4, 32, 8, HD), w_value.reshape(4, 32, 8, HD)], axis=1)
    wkv = lax.dynamic_index_in_dim(wkv, xh * 2 + core, 0, keepdims=False)
    wkv = wkv.transpose(2, 0, 1, 3).reshape(8, 1, 64, HD)
    wkv = jnp.broadcast_to(wkv, (8, 4, 64, HD)).reshape(32, 64, HD)
    cut = exchange(jnp.concatenate([wq, wkv], axis=1), YZ)
    cut = x_ring(cut, xh, xl)
    order = [(h, l) for l in (0, 1) for h in (0, 1)]
    q_cols = jnp.stack([cut[h][l][:, :64] for h, l in order], axis=1).reshape(D, HD)
    wkv = jnp.stack([cut[h][l][:, 64:] for h, l in order], axis=1)
    wkv = jnp.stack(ordered(wkv, flip(wkv, ("core",)), core), axis=2)
    wkv = wkv.reshape(128, 2, 2, 32, HD).transpose(0, 1, 3, 2, 4).reshape(D, 2 * HD)

    cosine_table, sine_table = angles(seg_row)
    weight_row = token_weights(seg_row, adv_row)
    grad_context = (cot.astype(f32) * weight_row[:, None]).astype(bf16)
    position = jnp.arange(block_len, dtype=jnp.int32)
    allowed = (seg_row[:, None] == seg_row[None, :]) & (position[None, :] <= position[:, None])

    def project(cols):
        return jnp.dot(normed, cols, preferred_element_type=f32) * inv_width

    queries = project(q_cols)
    keys_values = project(wkv)
    q_rot = rotate(queries, cosine_table, sine_table).astype(bf16)
    k_rot = rotate(keys_values[:, :HD], cosine_table, sine_table).astype(bf16)
    v_bf = keys_values[:, HD:].astype(bf16)

    grad_query, grad_key, grad_value = attend_back(q_rot, k_rot, v_bf, grad_context, allowed)
    scaled_q = (rotate(grad_query, cosine_table, -sine_table) * inv_width).astype(bf16)
    scaled_kv = (
        jnp.concatenate([rotate(grad_key, cosine_table, -sine_table), grad_value], -1) * inv_width
    ).astype(bf16)

    contract = (((0,), (0,)), ((), ()))
    part_q = lax.dot_general(normed, scaled_q, contract, preferred_element_type=f32)
    part_q = part_q.astype(bf16).reshape(4, 2048, HD)
    part_q, scaled_kv = lax.optimization_barrier((part_q, scaled_kv))

    def part_for(mask):
        return lax.dynamic_index_in_dim(part_q, ring ^ mask, 0, keepdims=False)

    def add(a, b):
        return (a.astype(f32) + b.astype(f32)).astype(bf16)

    far = part_for(2)
    first = flip(far[:1024], X)
    second = flip(far[1024:], ("xl",))
    near, wrap = part_for(1), part_for(3)
    near = jnp.concatenate([add(near[:1024], first), near[1024:]], axis=0)
    wrap = jnp.concatenate([wrap[:1024], add(wrap[1024:], second)], axis=0)
    near = flip(near, ("xl",))
    wrap = flip(wrap, X)
    sum_q = part_for(0).astype(f32) + near.astype(f32) + wrap.astype(f32)
    old_q = lax.dynamic_slice_in_dim(q_cols, ring * 2048, 2048)
    new_q = (old_q.astype(f32) - step_rate * sum_q).astype(bf16)
    near = swap(new_q)
    far = lax.ppermute(
        new_q,
        ("xh", "xl", "core"),
        [
            (h * 4 + l * 2 + c, (1 - h) * 4 + c * 2 + l)
            for h in (0, 1)
            for l in (0, 1)
            for c in (0, 1)
        ],
    )
    near_other = flip(near, ("core",))
    far_other = flip(far, ("core",))
    near = ordered(near, near_other, core)
    far = ordered(far, far_other, core)
    low = ordered(near[0], far[0], xh)
    high = ordered(near[1], far[1], xh)
    roll_q = jnp.stack([low[0], high[0], low[1], high[1]], axis=0).reshape(D, HD)

    kv_sum = exchange(scaled_kv.reshape(8, 64, 2 * HD), MEM)
    kv_sum = kv_sum.astype(f32)
    kv_sum = jnp.sum(kv_sum, axis=0).astype(bf16)
    kv_sum = spread(kv_sum, MEM).reshape(block_len, 2 * HD)
    part_kv = lax.dot_general(
        member_columns(normed, member), kv_sum, contract, preferred_element_type=f32
    ).astype(bf16)
    part_kv = exchange(part_kv.reshape(4, 256, 2 * HD), X).astype(f32)
    old_kv = wkv.reshape(4, 2, 8, 128, 2 * HD)
    old_kv = lax.dynamic_index_in_dim(old_kv, ring, 0, keepdims=False)
    old_kv = lax.dynamic_index_in_dim(old_kv, member, 1, keepdims=False).reshape(256, 2 * HD)
    new_kv = (old_kv.astype(f32) - step_rate * jnp.sum(part_kv, axis=0)).astype(bf16)
    new_kv = spread(new_kv, ("zl",))
    new_kv = x_ring(new_kv, xh, xl)
    new_kv = jnp.stack([new_kv[h][l] for h in (0, 1) for l in (0, 1)], axis=0)
    new_kv = jnp.stack(ordered(new_kv, flip(new_kv, ("core",)), core), axis=0)
    new_kv = new_kv.reshape(2, 4, 4, 2, 128, 2 * HD).transpose(1, 3, 2, 0, 4, 5).reshape(D, 2 * HD)
    return roll_q, new_kv[:, :HD], new_kv[:, HD:]


def solution(mesh):
    grid = Mesh(
        mesh.devices.reshape(2, 4, 2, 4, 2, 2), ("xh", "y", "zh", "zl", "xl", "core")
    )
    groups = ("xh", "core")
    in_specs = (
        P(groups, FS, None),
        P(groups, None, FS),
        P(groups, None),
        P(groups, None),
        P(FS, None),
        P(FS, None),
        P(FS, None),
    )
    out_specs = (P(None, FS), P(None, FS), P(None, FS))

    return jax.shard_map(local, mesh=grid, in_specs=in_specs, out_specs=out_specs, check_vma=False)
```

```python
import jax
import jax.numpy as jnp
from jax import lax
from jax.experimental import pallas as pl
from jax.experimental.pallas import tpu as pltpu
from jax.sharding import Mesh, PartitionSpec as P

D = 8192
HD = 128
RESP = 8

step_rate = 200.0
rope_base = 1000000.0
norm_eps = 1e-06
masked_score = -1e30

YZ = ("y", "zh", "zl")
MEM = ("zl", "core")
X = ("xh", "xl")
FS = ("y", "zh", "zl", "xl")


def rotate(field, cosine_table, sine_table):
    half_width = field.shape[-1] // 2
    lead_half = field[..., :half_width]
    tail_half = field[..., half_width:]
    return jnp.concatenate(
        [
            lead_half * cosine_table - tail_half * sine_table,
            tail_half * cosine_table + lead_half * sine_table,
        ],
        -1,
    )


def angles(seg_row):
    span_count = seg_row.shape[0]
    earlier = jnp.sum((seg_row[None, :] < seg_row[:, None]).astype(jnp.int32), axis=1)
    positions = jnp.arange(span_count, dtype=jnp.int32) - earlier
    frequency = rope_base ** (-jnp.arange(HD // 2, dtype=jnp.float32) * 2.0 / HD)
    phase_grid = positions.astype(jnp.float32)[:, None] * frequency[None, :]
    return jnp.cos(phase_grid), jnp.sin(phase_grid)


def token_weights(seg_row, advantage_row):
    id_range = jnp.arange(RESP + 1, dtype=jnp.int32)
    onehot = (seg_row[:, None] == id_range[None, :]).astype(jnp.float32)
    counts = jnp.sum(onehot, axis=0)[:RESP]
    per_token = -advantage_row / counts
    return jnp.sum(onehot[:, :RESP] * per_token[None, :], axis=1)


def attend_back(q_rot, k_rot, v_bf, grad_context, allowed):
    score_scale = HD ** (-0.5)
    f32 = jnp.float32
    scores = jnp.einsum("td,ud->tu", q_rot, k_rot, preferred_element_type=f32) * score_scale
    scores = jnp.where(allowed, scores, masked_score)
    row_top = jnp.max(scores, axis=-1, keepdims=True)
    exponent = jnp.exp(scores - row_top)
    attention = exponent / jnp.sum(exponent, axis=-1, keepdims=True)
    attention_bf = attention.astype(jnp.bfloat16)
    grad_prob = jnp.einsum("td,ud->tu", grad_context, v_bf, preferred_element_type=f32)
    inner_sum = jnp.sum(attention * grad_prob, axis=-1, keepdims=True)
    dscore = (attention * (grad_prob - inner_sum)).astype(jnp.bfloat16)
    grad_query = jnp.einsum("tu,ud->td", dscore, k_rot, preferred_element_type=f32) * score_scale
    grad_key = jnp.einsum("tu,td->ud", dscore, q_rot, preferred_element_type=f32) * score_scale
    grad_value = jnp.einsum("tu,td->ud", attention_bf, grad_context, preferred_element_type=f32)
    return grad_query, grad_key, grad_value


def swap(x):
    return lax.ppermute(x, ("xl", "core"), [(0, 0), (1, 2), (2, 1), (3, 3)])


def flip(x, axes):
    n = 2 ** len(axes)
    return lax.ppermute(x, axes, [(i, n - 1 - i) for i in range(n)])


def exchange(x, axes):
    return lax.all_to_all(x, axes, split_axis=0, concat_axis=0, tiled=True)


def spread(x, axes):
    n = lax.axis_size(axes)
    return exchange(jnp.broadcast_to(x[None], (n,) + x.shape), axes)


def ordered(mine, other, bit):
    first = jnp.where(bit == 0, mine, other)
    second = jnp.where(bit == 0, other, mine)
    return first, second


def ring_pieces(x):
    near, wrap = flip(x, ("xl",)), flip(x, X)
    half = x.shape[0] // 2
    return near, wrap, flip(wrap[:half], ("xl",)), flip(near[half:], X)


def x_ring(x, xh, xl):
    near, wrap, far_low, far_high = ring_pieces(x)
    far = jnp.concatenate([far_low, far_high], axis=0)
    low = ordered(x, near, xl)
    high = ordered(far, wrap, xl)
    col0 = ordered(low[0], high[0], xh)
    col1 = ordered(low[1], high[1], xh)
    return (col0[0], col1[0]), (col0[1], col1[1])


def pack_columns(w_query, w_key, w_value, at):
    def body(at_ref, q_ref, k_ref, v_ref, out_ref):
        for j in range(32):
            head = pl.multiple_of((2 * j + at_ref[2]) * HD, HD)
            out_ref[j, 0:64, :] = q_ref[:, pl.ds(head, HD)]
            key = slice(j // 4 * HD, (j // 4 + 1) * HD)
            out_ref[j, 64:96, :] = k_ref[:, key]
            out_ref[j, 96:128, :] = v_ref[:, key]

    quarter = pl.BlockSpec((32, 8 * HD), lambda i, at: (2 * at[1] + at[2], 0))
    return pl.pallas_call(
        body,
        out_shape=jax.ShapeDtypeStruct((32, 128, HD), jnp.bfloat16),
        grid_spec=pltpu.PrefetchScalarGridSpec(
            num_scalar_prefetch=1,
            grid=(1,),
            in_specs=[pl.BlockSpec((64, D), lambda i, at: (at[1], 0)), quarter, quarter],
            out_specs=pl.BlockSpec((32, 128, HD), lambda i, at: (0, 0, 0)),
        ),
        name="pack_columns",
    )(at, w_query, w_key, w_value)


def project(normed, pieces, others, at):
    def body(at_ref, rows_ref, *refs):
        mine, theirs = refs[:5], refs[5:10]
        out_ref, wq_ref, wkv_ref, member_ref = refs[10:]
        b = pl.program_id(0)
        xl, xh, core = at_ref[0], at_ref[1], at_ref[2]
        spots = ((xl, xh), (1 - xl, xh), (1 - xl, 1 - xh), (xl, 1 - xh))

        def block(group, n):
            if n < 3:
                return group[n][...]
            return jnp.where(b < 4, group[3][...], group[4][...])

        for n, (l, h) in enumerate(spots):
            own = block(mine, n)
            other = block(theirs, n)
            wq_ref[:, l, h] = own[:, :64]
            wkv_ref[:, l, h, core, :, 0:HD] = own[:, 64:96]
            wkv_ref[:, l, h, core, :, HD : 2 * HD] = own[:, 96:128]
            wkv_ref[:, l, h, 1 - core, :, 0:HD] = other[:, 64:96]
            wkv_ref[:, l, h, 1 - core, :, HD : 2 * HD] = other[:, 96:128]

        rows = rows_ref[...]
        member_ref[...] = rows_ref[:, pl.ds(pl.multiple_of(at_ref[3] * HD, HD), HD)]

        @pl.when(b == 0)
        def _():
            out_ref[...] = jnp.zeros_like(out_ref)

        out_ref[:, 0:HD] += jnp.dot(
            rows, wq_ref[...].reshape(1024, HD), preferred_element_type=jnp.float32
        )
        out_ref[:, HD : 3 * HD] += jnp.dot(
            rows, wkv_ref[...].reshape(1024, 2 * HD), preferred_element_type=jnp.float32
        )

    whole = pl.BlockSpec((4, 128, HD), lambda b, at: (b, 0, 0))
    first = pl.BlockSpec((4, 128, HD), lambda b, at: (jnp.minimum(b, 3), 0, 0))
    last = pl.BlockSpec((4, 128, HD), lambda b, at: (jnp.maximum(b, 4) - 4, 0, 0))
    group = [whole, whole, whole, first, last]
    bf16 = jnp.bfloat16
    return pl.pallas_call(
        body,
        out_shape=(
            jax.ShapeDtypeStruct((512, 3 * HD), jnp.float32),
            jax.ShapeDtypeStruct((32, 2, 2, 64, HD), bf16),
            jax.ShapeDtypeStruct((32, 2, 2, 2, 32, 2 * HD), bf16),
            jax.ShapeDtypeStruct((512, 1024), bf16),
        ),
        grid_spec=pltpu.PrefetchScalarGridSpec(
            num_scalar_prefetch=1,
            grid=(8,),
            in_specs=[pl.BlockSpec((512, 1024), lambda b, at: (0, b))] + group + group,
            out_specs=(
                pl.BlockSpec((512, 3 * HD), lambda b, at: (0, 0)),
                pl.BlockSpec((4, 2, 2, 64, HD), lambda b, at: (b, 0, 0, 0, 0)),
                pl.BlockSpec((4, 2, 2, 2, 32, 2 * HD), lambda b, at: (b, 0, 0, 0, 0, 0)),
                pl.BlockSpec((512, HD), lambda b, at: (0, b)),
            ),
        ),
        name="project",
    )(at, normed, *pieces, *others)


def local(hidden, cotangent, seg_ids, advantage, w_query, w_key, w_value):
    f32 = jnp.float32
    bf16 = jnp.bfloat16
    inv_width = D ** (-0.5)
    xh = lax.axis_index("xh")
    xl = lax.axis_index("xl")
    core = lax.axis_index("core")
    zl = lax.axis_index("zl")
    member = zl * 2 + core
    ring = xh * 2 + xl

    token_rows = hidden[0].astype(f32)
    normed_own = (
        token_rows * lax.rsqrt(jnp.mean(token_rows * token_rows, axis=-1, keepdims=True) + norm_eps)
    ).astype(bf16)
    normed = lax.all_gather(swap(normed_own), YZ + ("core",), axis=0, tiled=True)
    cot = swap(cotangent[0])
    seg_row = swap(seg_ids[0])
    adv_row = swap(advantage[0])
    block_len = 512

    at = jnp.stack([xl, xh, core, member]).astype(jnp.int32)
    cut = exchange(pack_columns(w_query, w_key, w_value, at), YZ)
    pieces = (cut,) + ring_pieces(cut)
    others = tuple(flip(p, ("core",)) for p in pieces)
    projected, q_cols, wkv, normed_m = project(normed, pieces, others, at)
    projected = projected * inv_width
    q_cols = q_cols.reshape(D, HD)

    cosine_table, sine_table = angles(seg_row)
    weight_row = token_weights(seg_row, adv_row)
    grad_context = (cot.astype(f32) * weight_row[:, None]).astype(bf16)
    position = jnp.arange(block_len, dtype=jnp.int32)
    allowed = (seg_row[:, None] == seg_row[None, :]) & (position[None, :] <= position[:, None])

    q_rot = rotate(projected[:, :HD], cosine_table, sine_table).astype(bf16)
    k_rot = rotate(projected[:, HD : 2 * HD], cosine_table, sine_table).astype(bf16)
    v_bf = projected[:, 2 * HD :].astype(bf16)

    grad_query, grad_key, grad_value = attend_back(q_rot, k_rot, v_bf, grad_context, allowed)
    scaled_q = (rotate(grad_query, cosine_table, -sine_table) * inv_width).astype(bf16)
    scaled_kv = (
        jnp.concatenate([rotate(grad_key, cosine_table, -sine_table), grad_value], -1) * inv_width
    ).astype(bf16)

    contract = (((0,), (0,)), ((), ()))
    part_q = lax.dot_general(normed, scaled_q, contract, preferred_element_type=f32)
    part_q = part_q.astype(bf16).reshape(4, 2048, HD)
    part_q, scaled_kv = lax.optimization_barrier((part_q, scaled_kv))

    def part_for(mask):
        return lax.dynamic_index_in_dim(part_q, ring ^ mask, 0, keepdims=False)

    def add(a, b):
        return (a.astype(f32) + b.astype(f32)).astype(bf16)

    far = part_for(2)
    first = flip(far[:1024], X)
    second = flip(far[1024:], ("xl",))
    near, wrap = part_for(1), part_for(3)
    near = jnp.concatenate([add(near[:1024], first), near[1024:]], axis=0)
    wrap = jnp.concatenate([wrap[:1024], add(wrap[1024:], second)], axis=0)
    near = flip(near, ("xl",))
    wrap = flip(wrap, X)
    sum_q = part_for(0).astype(f32) + near.astype(f32) + wrap.astype(f32)
    old_q = lax.dynamic_slice_in_dim(q_cols, ring * 2048, 2048)
    new_q = (old_q.astype(f32) - step_rate * sum_q).astype(bf16)
    near = swap(new_q)
    far = lax.ppermute(
        new_q,
        ("xh", "xl", "core"),
        [
            (h * 4 + l * 2 + c, (1 - h) * 4 + c * 2 + l)
            for h in (0, 1)
            for l in (0, 1)
            for c in (0, 1)
        ],
    )
    near_other = flip(near, ("core",))
    far_other = flip(far, ("core",))
    near = ordered(near, near_other, core)
    far = ordered(far, far_other, core)
    low = ordered(near[0], far[0], xh)
    high = ordered(near[1], far[1], xh)
    roll_q = jnp.stack([low[0], high[0], low[1], high[1]], axis=0).reshape(D, HD)

    kv_sum = exchange(scaled_kv.reshape(8, 64, 2 * HD), MEM)
    kv_sum = kv_sum.astype(f32)
    kv_sum = jnp.sum(kv_sum, axis=0).astype(bf16)
    kv_sum = spread(kv_sum, MEM).reshape(block_len, 2 * HD)
    part_kv = lax.dot_general(
        normed_m, kv_sum, contract, preferred_element_type=f32
    ).astype(bf16)
    part_kv = exchange(part_kv.reshape(4, 256, 2 * HD), X).astype(f32)
    old_kv = wkv.reshape(4, 2, 8, 128, 2 * HD)
    old_kv = lax.dynamic_index_in_dim(old_kv, ring, 0, keepdims=False)
    old_kv = lax.dynamic_index_in_dim(old_kv, member, 1, keepdims=False).reshape(256, 2 * HD)
    new_kv = (old_kv.astype(f32) - step_rate * jnp.sum(part_kv, axis=0)).astype(bf16)
    new_kv = spread(new_kv, ("zl",))
    new_kv = x_ring(new_kv, xh, xl)
    new_kv = jnp.stack([new_kv[h][l] for h in (0, 1) for l in (0, 1)], axis=0)
    new_kv = jnp.stack(ordered(new_kv, flip(new_kv, ("core",)), core), axis=0)
    new_kv = new_kv.reshape(2, 4, 4, 2, 128, 2 * HD).transpose(1, 3, 2, 0, 4, 5).reshape(D, 2 * HD)
    return roll_q, new_kv[:, :HD], new_kv[:, HD:]


def solution(mesh):
    grid = Mesh(
        mesh.devices.reshape(2, 4, 2, 4, 2, 2), ("xh", "y", "zh", "zl", "xl", "core")
    )
    groups = ("xh", "core")
    in_specs = (
        P(groups, FS, None),
        P(groups, None, FS),
        P(groups, None),
        P(groups, None),
        P(FS, None),
        P(FS, None),
        P(FS, None),
    )
    out_specs = (P(None, FS), P(None, FS), P(None, FS))

    return jax.shard_map(local, mesh=grid, in_specs=in_specs, out_specs=out_specs, check_vma=False)
```

```python
import jax
import jax.numpy as jnp
from jax import lax
from jax.experimental import pallas as pl
from jax.experimental.pallas import tpu as pltpu
from jax.sharding import Mesh, PartitionSpec as P

D = 8192
HD = 128
RESP = 8

step_rate = 200.0
rope_base = 1000000.0
norm_eps = 1e-06
masked_score = -1e30

YZ = ("y", "zh", "zl")
MEM = ("zl", "core")
X = ("xh", "xl")
FS = ("y", "zh", "zl", "xl")


def rotate(field, cosine_table, sine_table):
    half_width = field.shape[-1] // 2
    lead_half = field[..., :half_width]
    tail_half = field[..., half_width:]
    return jnp.concatenate(
        [
            lead_half * cosine_table - tail_half * sine_table,
            tail_half * cosine_table + lead_half * sine_table,
        ],
        -1,
    )


def angles(seg_row):
    span_count = seg_row.shape[0]
    earlier = jnp.sum((seg_row[None, :] < seg_row[:, None]).astype(jnp.int32), axis=1)
    positions = jnp.arange(span_count, dtype=jnp.int32) - earlier
    frequency = rope_base ** (-jnp.arange(HD // 2, dtype=jnp.float32) * 2.0 / HD)
    phase_grid = positions.astype(jnp.float32)[:, None] * frequency[None, :]
    return jnp.cos(phase_grid), jnp.sin(phase_grid)


def token_weights(seg_row, advantage_row):
    id_range = jnp.arange(RESP + 1, dtype=jnp.int32)
    onehot = (seg_row[:, None] == id_range[None, :]).astype(jnp.float32)
    counts = jnp.sum(onehot, axis=0)[:RESP]
    per_token = -advantage_row / counts
    return jnp.sum(onehot[:, :RESP] * per_token[None, :], axis=1)


def attend_back(q_rot, k_rot, v_bf, grad_context, allowed):
    score_scale = HD ** (-0.5)
    f32 = jnp.float32
    scores = jnp.einsum("td,ud->tu", q_rot, k_rot, preferred_element_type=f32) * score_scale
    scores = jnp.where(allowed, scores, masked_score)
    row_top = jnp.max(scores, axis=-1, keepdims=True)
    exponent = jnp.exp(scores - row_top)
    attention = exponent / jnp.sum(exponent, axis=-1, keepdims=True)
    attention_bf = attention.astype(jnp.bfloat16)
    grad_prob = jnp.einsum("td,ud->tu", grad_context, v_bf, preferred_element_type=f32)
    inner_sum = jnp.sum(attention * grad_prob, axis=-1, keepdims=True)
    dscore = (attention * (grad_prob - inner_sum)).astype(jnp.bfloat16)
    grad_query = jnp.einsum("tu,ud->td", dscore, k_rot, preferred_element_type=f32) * score_scale
    grad_key = jnp.einsum("tu,td->ud", dscore, q_rot, preferred_element_type=f32) * score_scale
    grad_value = jnp.einsum("tu,td->ud", attention_bf, grad_context, preferred_element_type=f32)
    return grad_query, grad_key, grad_value


def swap(x):
    return lax.ppermute(x, ("xl", "core"), [(0, 0), (1, 2), (2, 1), (3, 3)])


def flip(x, axes):
    n = 2 ** len(axes)
    return lax.ppermute(x, axes, [(i, n - 1 - i) for i in range(n)])


def exchange(x, axes):
    return lax.all_to_all(x, axes, split_axis=0, concat_axis=0, tiled=True)


def spread(x, axes):
    n = lax.axis_size(axes)
    return exchange(jnp.broadcast_to(x[None], (n,) + x.shape), axes)


def ring_pieces(x):
    near, wrap = flip(x, ("xl",)), flip(x, X)
    half = x.shape[0] // 2
    return near, wrap, flip(wrap[:half], ("xl",)), flip(near[half:], X)


def pack_columns(w_query, w_key, w_value, at):
    def body(at_ref, q_ref, k_ref, v_ref, out_ref):
        for j in range(32):
            head = pl.multiple_of((2 * j + at_ref[2]) * HD, HD)
            out_ref[j, 0:64, :] = q_ref[:, pl.ds(head, HD)]
            key = slice(j // 4 * HD, (j // 4 + 1) * HD)
            out_ref[j, 64:96, :] = k_ref[:, key]
            out_ref[j, 96:128, :] = v_ref[:, key]

    quarter = pl.BlockSpec((32, 8 * HD), lambda i, at: (2 * at[1] + at[2], 0))
    return pl.pallas_call(
        body,
        out_shape=jax.ShapeDtypeStruct((32, 128, HD), jnp.bfloat16),
        grid_spec=pltpu.PrefetchScalarGridSpec(
            num_scalar_prefetch=1,
            grid=(1,),
            in_specs=[pl.BlockSpec((64, D), lambda i, at: (at[1], 0)), quarter, quarter],
            out_specs=pl.BlockSpec((32, 128, HD), lambda i, at: (0, 0, 0)),
        ),
        name="pack_columns",
    )(at, w_query, w_key, w_value)


def project(normed, pieces, others, at):
    def body(at_ref, rows_ref, *refs):
        mine, theirs = refs[:5], refs[5:10]
        out_ref, wq_ref, wkv_ref, member_ref = refs[10:]
        b = pl.program_id(0)
        xl, xh, core = at_ref[0], at_ref[1], at_ref[2]
        spots = ((xl, xh), (1 - xl, xh), (1 - xl, 1 - xh), (xl, 1 - xh))

        def block(group, n):
            if n < 3:
                return group[n][...]
            return jnp.where(b < 4, group[3][...], group[4][...])

        for n, (l, h) in enumerate(spots):
            own = block(mine, n)
            other = block(theirs, n)
            wq_ref[:, l, h] = own[:, :64]
            wkv_ref[:, l, h, core, :, 0:HD] = own[:, 64:96]
            wkv_ref[:, l, h, core, :, HD : 2 * HD] = own[:, 96:128]
            wkv_ref[:, l, h, 1 - core, :, 0:HD] = other[:, 64:96]
            wkv_ref[:, l, h, 1 - core, :, HD : 2 * HD] = other[:, 96:128]

        rows = rows_ref[...]
        member_ref[...] = rows_ref[:, pl.ds(pl.multiple_of(at_ref[3] * HD, HD), HD)]

        @pl.when(b == 0)
        def _():
            out_ref[...] = jnp.zeros_like(out_ref)

        out_ref[:, 0:HD] += jnp.dot(
            rows, wq_ref[...].reshape(1024, HD), preferred_element_type=jnp.float32
        )
        out_ref[:, HD : 3 * HD] += jnp.dot(
            rows, wkv_ref[...].reshape(1024, 2 * HD), preferred_element_type=jnp.float32
        )

    whole = pl.BlockSpec((4, 128, HD), lambda b, at: (b, 0, 0))
    first = pl.BlockSpec((4, 128, HD), lambda b, at: (jnp.minimum(b, 3), 0, 0))
    last = pl.BlockSpec((4, 128, HD), lambda b, at: (jnp.maximum(b, 4) - 4, 0, 0))
    group = [whole, whole, whole, first, last]
    bf16 = jnp.bfloat16
    return pl.pallas_call(
        body,
        out_shape=(
            jax.ShapeDtypeStruct((512, 3 * HD), jnp.float32),
            jax.ShapeDtypeStruct((32, 2, 2, 64, HD), bf16),
            jax.ShapeDtypeStruct((32, 2, 2, 2, 32, 2 * HD), bf16),
            jax.ShapeDtypeStruct((512, 1024), bf16),
        ),
        grid_spec=pltpu.PrefetchScalarGridSpec(
            num_scalar_prefetch=1,
            grid=(8,),
            in_specs=[pl.BlockSpec((512, 1024), lambda b, at: (0, b))] + group + group,
            out_specs=(
                pl.BlockSpec((512, 3 * HD), lambda b, at: (0, 0)),
                pl.BlockSpec((4, 2, 2, 64, HD), lambda b, at: (b, 0, 0, 0, 0)),
                pl.BlockSpec((4, 2, 2, 2, 32, 2 * HD), lambda b, at: (b, 0, 0, 0, 0, 0)),
                pl.BlockSpec((512, HD), lambda b, at: (0, b)),
            ),
        ),
        name="project",
    )(at, normed, *pieces, *others)


def unpack(q_pieces, kv_pieces, kv_others, at):
    def body(at_ref, *refs):
        q_in, mine, theirs = refs[:4], refs[4:9], refs[9:14]
        q_ref, k_ref, v_ref = refs[14:]
        xl, xh, core = at_ref[0], at_ref[1], at_ref[2]
        line = pl.program_id(0) % 4
        for (h, l), piece in zip(
            ((xh, core), (1 - xh, core), (xh, 1 - core), (1 - xh, 1 - core)), q_in
        ):
            q_ref[h, l] = piece[...]
        spots = ((xl, xh), (1 - xl, xh), (1 - xl, 1 - xh), (xl, 1 - xh))
        for group, c in ((mine, core), (theirs, 1 - core)):
            for n, (l, h) in enumerate(spots):
                if n < 3:
                    piece = group[n][...]
                else:
                    piece = jnp.where(line < 2, group[3][...], group[4][...])
                k_ref[h, l, 0, 0, c] = piece[0, :, 0:HD]
                v_ref[h, l, 0, 0, c] = piece[0, :, HD : 2 * HD]

    quarter = pl.BlockSpec((256, HD), lambda i, at: (i, 0))
    whole = pl.BlockSpec((1, HD, 2 * HD), lambda i, at: (i % 4, i // 4, 0))
    first = pl.BlockSpec((1, HD, 2 * HD), lambda i, at: (jnp.minimum(i % 4, 1), i // 4, 0))
    last = pl.BlockSpec((1, HD, 2 * HD), lambda i, at: (jnp.maximum(i % 4, 2) - 2, i // 4, 0))
    group = [whole, whole, whole, first, last]
    wide = pl.BlockSpec((2, 2, 1, 1, 2, HD, HD), lambda i, at: (0, 0, i // 4, i % 4, 0, 0, 0))
    bf16 = jnp.bfloat16
    outs = pl.pallas_call(
        body,
        out_shape=(
            jax.ShapeDtypeStruct((2, 2, 2048, HD), bf16),
            jax.ShapeDtypeStruct((2, 2, 2, 4, 2, HD, HD), bf16),
            jax.ShapeDtypeStruct((2, 2, 2, 4, 2, HD, HD), bf16),
        ),
        grid_spec=pltpu.PrefetchScalarGridSpec(
            num_scalar_prefetch=1,
            grid=(8,),
            in_specs=[quarter] * 4 + group + group,
            out_specs=(
                pl.BlockSpec((2, 2, 256, HD), lambda i, at: (0, 0, i, 0)),
                wide,
                wide,
            ),
        ),
        name="unpack",
    )(at, *q_pieces, *kv_pieces, *kv_others)
    return tuple(out.reshape(D, HD) for out in outs)


def local(hidden, cotangent, seg_ids, advantage, w_query, w_key, w_value):
    f32 = jnp.float32
    bf16 = jnp.bfloat16
    inv_width = D ** (-0.5)
    xh = lax.axis_index("xh")
    xl = lax.axis_index("xl")
    core = lax.axis_index("core")
    zl = lax.axis_index("zl")
    member = zl * 2 + core
    ring = xh * 2 + xl

    token_rows = hidden[0].astype(f32)
    normed_own = (
        token_rows * lax.rsqrt(jnp.mean(token_rows * token_rows, axis=-1, keepdims=True) + norm_eps)
    ).astype(bf16)
    normed = lax.all_gather(swap(normed_own), YZ + ("core",), axis=0, tiled=True)
    cot = swap(cotangent[0])
    seg_row = swap(seg_ids[0])
    adv_row = swap(advantage[0])
    block_len = 512

    at = jnp.stack([xl, xh, core, member]).astype(jnp.int32)
    cut = exchange(pack_columns(w_query, w_key, w_value, at), YZ)
    pieces = (cut,) + ring_pieces(cut)
    others = tuple(flip(p, ("core",)) for p in pieces)
    projected, q_cols, wkv, normed_m = project(normed, pieces, others, at)
    projected = projected * inv_width
    q_cols = q_cols.reshape(D, HD)

    cosine_table, sine_table = angles(seg_row)
    weight_row = token_weights(seg_row, adv_row)
    grad_context = (cot.astype(f32) * weight_row[:, None]).astype(bf16)
    position = jnp.arange(block_len, dtype=jnp.int32)
    allowed = (seg_row[:, None] == seg_row[None, :]) & (position[None, :] <= position[:, None])

    q_rot = rotate(projected[:, :HD], cosine_table, sine_table).astype(bf16)
    k_rot = rotate(projected[:, HD : 2 * HD], cosine_table, sine_table).astype(bf16)
    v_bf = projected[:, 2 * HD :].astype(bf16)

    grad_query, grad_key, grad_value = attend_back(q_rot, k_rot, v_bf, grad_context, allowed)
    scaled_q = (rotate(grad_query, cosine_table, -sine_table) * inv_width).astype(bf16)
    scaled_kv = (
        jnp.concatenate([rotate(grad_key, cosine_table, -sine_table), grad_value], -1) * inv_width
    ).astype(bf16)

    contract = (((0,), (0,)), ((), ()))
    part_q = lax.dot_general(normed, scaled_q, contract, preferred_element_type=f32)
    part_q = part_q.astype(bf16).reshape(4, 2048, HD)

    def part_for(mask):
        return lax.dynamic_index_in_dim(part_q, ring ^ mask, 0, keepdims=False)

    def add(a, b):
        return (a.astype(f32) + b.astype(f32)).astype(bf16)

    far = part_for(2)
    first = flip(far[:1024], X)
    second = flip(far[1024:], ("xl",))
    near, wrap = part_for(1), part_for(3)
    near = jnp.concatenate([add(near[:1024], first), near[1024:]], axis=0)
    wrap = jnp.concatenate([wrap[:1024], add(wrap[1024:], second)], axis=0)
    near = flip(near, ("xl",))
    wrap = flip(wrap, X)
    sum_q = part_for(0).astype(f32) + near.astype(f32) + wrap.astype(f32)
    old_q = lax.dynamic_slice_in_dim(q_cols, ring * 2048, 2048)
    new_q = (old_q.astype(f32) - step_rate * sum_q).astype(bf16)
    near = swap(new_q)
    far = lax.ppermute(
        new_q,
        ("xh", "xl", "core"),
        [
            (h * 4 + l * 2 + c, (1 - h) * 4 + c * 2 + l)
            for h in (0, 1)
            for l in (0, 1)
            for c in (0, 1)
        ],
    )
    near_other = flip(near, ("core",))
    far_other = flip(far, ("core",))
    kv_sum = exchange(scaled_kv.reshape(8, 64, 2 * HD), MEM)
    kv_sum = kv_sum.astype(f32)
    kv_sum = jnp.sum(kv_sum, axis=0).astype(bf16)
    kv_sum = spread(kv_sum, MEM).reshape(block_len, 2 * HD)
    part_kv = lax.dot_general(
        normed_m, kv_sum, contract, preferred_element_type=f32
    ).astype(bf16)
    part_kv = exchange(part_kv.reshape(4, 256, 2 * HD), X).astype(f32)
    old_kv = wkv.reshape(4, 2, 8, 128, 2 * HD)
    old_kv = lax.dynamic_index_in_dim(old_kv, ring, 0, keepdims=False)
    old_kv = lax.dynamic_index_in_dim(old_kv, member, 1, keepdims=False).reshape(256, 2 * HD)
    new_kv = (old_kv.astype(f32) - step_rate * jnp.sum(part_kv, axis=0)).astype(bf16)
    new_kv = spread(new_kv, ("zl",))
    kv_pieces = (new_kv,) + ring_pieces(new_kv)
    kv_others = tuple(flip(p, ("core",)) for p in kv_pieces)
    return unpack((near, far, near_other, far_other), kv_pieces, kv_others, at)


def solution(mesh):
    grid = Mesh(
        mesh.devices.reshape(2, 4, 2, 4, 2, 2), ("xh", "y", "zh", "zl", "xl", "core")
    )
    groups = ("xh", "core")
    in_specs = (
        P(groups, FS, None),
        P(groups, None, FS),
        P(groups, None),
        P(groups, None),
        P(FS, None),
        P(FS, None),
        P(FS, None),
    )
    out_specs = (P(None, FS), P(None, FS), P(None, FS))

    return jax.shard_map(local, mesh=grid, in_specs=in_specs, out_specs=out_specs, check_vma=False)
```

```python
import jax
import jax.numpy as jnp
from jax import lax
from jax.experimental import pallas as pl
from jax.experimental.pallas import tpu as pltpu
from jax.sharding import Mesh, PartitionSpec as P

D = 8192
HD = 128
RESP = 8

step_rate = 200.0
rope_base = 1000000.0
norm_eps = 1e-06
masked_score = -1e30

YZ = ("y", "zh", "zl")
MEM = ("zl", "core")
X = ("xh", "xl")
FS = ("y", "zh", "zl", "xl")


def rotate(field, cosine_table, sine_table):
    half_width = field.shape[-1] // 2
    lead_half = field[..., :half_width]
    tail_half = field[..., half_width:]
    return jnp.concatenate(
        [
            lead_half * cosine_table - tail_half * sine_table,
            tail_half * cosine_table + lead_half * sine_table,
        ],
        -1,
    )


def angles(seg_row):
    span_count = seg_row.shape[0]
    earlier = jnp.sum((seg_row[None, :] < seg_row[:, None]).astype(jnp.int32), axis=1)
    positions = jnp.arange(span_count, dtype=jnp.int32) - earlier
    frequency = rope_base ** (-jnp.arange(HD // 2, dtype=jnp.float32) * 2.0 / HD)
    phase_grid = positions.astype(jnp.float32)[:, None] * frequency[None, :]
    return jnp.cos(phase_grid), jnp.sin(phase_grid)


def token_weights(seg_row, advantage_row):
    id_range = jnp.arange(RESP + 1, dtype=jnp.int32)
    onehot = (seg_row[:, None] == id_range[None, :]).astype(jnp.float32)
    counts = jnp.sum(onehot, axis=0)[:RESP]
    per_token = -advantage_row / counts
    return jnp.sum(onehot[:, :RESP] * per_token[None, :], axis=1)


def attend_back(q_rot, k_rot, v_bf, grad_context, allowed):
    score_scale = HD ** (-0.5)
    f32 = jnp.float32
    scores = jnp.einsum("td,ud->tu", q_rot, k_rot, preferred_element_type=f32) * score_scale
    scores = jnp.where(allowed, scores, masked_score)
    row_top = jnp.max(scores, axis=-1, keepdims=True)
    exponent = jnp.exp(scores - row_top)
    attention = exponent / jnp.sum(exponent, axis=-1, keepdims=True)
    attention_bf = attention.astype(jnp.bfloat16)
    grad_prob = jnp.einsum("td,ud->tu", grad_context, v_bf, preferred_element_type=f32)
    inner_sum = jnp.sum(attention * grad_prob, axis=-1, keepdims=True)
    dscore = (attention * (grad_prob - inner_sum)).astype(jnp.bfloat16)
    grad_query = jnp.einsum("tu,ud->td", dscore, k_rot, preferred_element_type=f32) * score_scale
    grad_key = jnp.einsum("tu,td->ud", dscore, q_rot, preferred_element_type=f32) * score_scale
    grad_value = jnp.einsum("tu,td->ud", attention_bf, grad_context, preferred_element_type=f32)
    return grad_query, grad_key, grad_value


def swap(x):
    return lax.ppermute(x, ("xl", "core"), [(0, 0), (1, 2), (2, 1), (3, 3)])


def flip(x, axes):
    n = 2 ** len(axes)
    return lax.ppermute(x, axes, [(i, n - 1 - i) for i in range(n)])


def exchange(x, axes):
    return lax.all_to_all(x, axes, split_axis=0, concat_axis=0, tiled=True)


def spread(x, axes):
    n = lax.axis_size(axes)
    return exchange(jnp.broadcast_to(x[None], (n,) + x.shape), axes)


def ring_pieces(x):
    near, wrap = flip(x, ("xl",)), flip(x, X)
    half = x.shape[0] // 2
    return near, wrap, flip(wrap[:half], ("xl",)), flip(near[half:], X)


def pack_columns(w_query, w_key, w_value, at):
    def body(at_ref, q_ref, k_ref, v_ref, out_ref):
        for j in range(32):
            head = pl.multiple_of((2 * j + at_ref[2]) * HD, HD)
            out_ref[j, 0:64, :] = q_ref[:, pl.ds(head, HD)]
            key = slice(j // 4 * HD, (j // 4 + 1) * HD)
            out_ref[j, 64:96, :] = k_ref[:, key]
            out_ref[j, 96:128, :] = v_ref[:, key]

    quarter = pl.BlockSpec((32, 8 * HD), lambda i, at: (2 * at[1] + at[2], 0))
    return pl.pallas_call(
        body,
        out_shape=jax.ShapeDtypeStruct((32, 128, HD), jnp.bfloat16),
        grid_spec=pltpu.PrefetchScalarGridSpec(
            num_scalar_prefetch=1,
            grid=(1,),
            in_specs=[pl.BlockSpec((64, D), lambda i, at: (at[1], 0)), quarter, quarter],
            out_specs=pl.BlockSpec((32, 128, HD), lambda i, at: (0, 0, 0)),
        ),
        name="pack_columns",
    )(at, w_query, w_key, w_value)


def project(normed, pieces, others, at):
    def body(at_ref, rows_ref, *refs):
        mine, theirs = refs[:5], refs[5:10]
        out_ref, wq_ref, wkv_ref, member_ref = refs[10:]
        b = pl.program_id(0)
        xl, xh, core = at_ref[0], at_ref[1], at_ref[2]
        spots = ((xl, xh), (1 - xl, xh), (1 - xl, 1 - xh), (xl, 1 - xh))

        def block(group, n):
            if n < 3:
                return group[n][...]
            return jnp.where(b < 2, group[3][...], group[4][...])

        for n, (l, h) in enumerate(spots):
            own = block(mine, n)
            other = block(theirs, n)
            wq_ref[:, l, h] = own[:, :64]
            wkv_ref[:, l, h, core, :, 0:HD] = own[:, 64:96]
            wkv_ref[:, l, h, core, :, HD : 2 * HD] = own[:, 96:128]
            wkv_ref[:, l, h, 1 - core, :, 0:HD] = other[:, 0:32]
            wkv_ref[:, l, h, 1 - core, :, HD : 2 * HD] = other[:, 32:64]

        rows = rows_ref[...]
        for n in (0, 1):
            member_ref[:, n * HD : (n + 1) * HD] = rows_ref[
                :, pl.ds(pl.multiple_of(n * 1024 + at_ref[3] * HD, HD), HD)
            ]

        @pl.when(b == 0)
        def _():
            out_ref[...] = jnp.zeros_like(out_ref)

        out_ref[:, 0:HD] += jnp.dot(
            rows, wq_ref[...].reshape(2048, HD), preferred_element_type=jnp.float32
        )
        out_ref[:, HD : 3 * HD] += jnp.dot(
            rows, wkv_ref[...].reshape(2048, 2 * HD), preferred_element_type=jnp.float32
        )

        @pl.when(b == 3)
        def _():
            out_ref[...] *= D ** (-0.5)

    def group(rows, at_row):
        whole = pl.BlockSpec((8, rows, HD), lambda b, at: (b, at_row, 0))
        first = pl.BlockSpec((8, rows, HD), lambda b, at: (jnp.minimum(b, 1), at_row, 0))
        last = pl.BlockSpec((8, rows, HD), lambda b, at: (jnp.maximum(b, 2) - 2, at_row, 0))
        return [whole, whole, whole, first, last]

    bf16 = jnp.bfloat16
    return pl.pallas_call(
        body,
        out_shape=(
            jax.ShapeDtypeStruct((512, 3 * HD), jnp.float32),
            jax.ShapeDtypeStruct((32, 2, 2, 64, HD), bf16),
            jax.ShapeDtypeStruct((32, 2, 2, 2, 32, 2 * HD), bf16),
            jax.ShapeDtypeStruct((512, 1024), bf16),
        ),
        grid_spec=pltpu.PrefetchScalarGridSpec(
            num_scalar_prefetch=1,
            grid=(4,),
            in_specs=[pl.BlockSpec((512, 2048), lambda b, at: (0, b))]
            + group(128, 0)
            + group(64, 1),
            out_specs=(
                pl.BlockSpec((512, 3 * HD), lambda b, at: (0, 0)),
                pl.BlockSpec((8, 2, 2, 64, HD), lambda b, at: (b, 0, 0, 0, 0)),
                pl.BlockSpec((8, 2, 2, 2, 32, 2 * HD), lambda b, at: (b, 0, 0, 0, 0, 0)),
                pl.BlockSpec((512, 2 * HD), lambda b, at: (0, b)),
            ),
        ),
        name="project",
    )(at, normed, *pieces, *others)


def unpack(q_pieces, kv_pieces, kv_others, at):
    def body(at_ref, *refs):
        q_in, mine, theirs = refs[:4], refs[4:9], refs[9:14]
        q_ref, k_ref, v_ref = refs[14:]
        xl, xh, core = at_ref[0], at_ref[1], at_ref[2]
        line = pl.program_id(0)
        for (h, l), piece in zip(
            ((xh, core), (1 - xh, core), (xh, 1 - core), (1 - xh, 1 - core)), q_in
        ):
            q_ref[h, l] = piece[...]
        spots = ((xl, xh), (1 - xl, xh), (1 - xl, 1 - xh), (xl, 1 - xh))
        for group, c in ((mine, core), (theirs, 1 - core)):
            for n, (l, h) in enumerate(spots):
                if n < 3:
                    piece = group[n][...]
                else:
                    piece = jnp.where(line < 2, group[3][...], group[4][...])
                for z in (0, 1):
                    k_ref[h, l, z, 0, c] = piece[0, z * HD : (z + 1) * HD, 0:HD]
                    v_ref[h, l, z, 0, c] = piece[0, z * HD : (z + 1) * HD, HD : 2 * HD]

    quarter = pl.BlockSpec((512, HD), lambda i, at: (i, 0))
    whole = pl.BlockSpec((1, 2 * HD, 2 * HD), lambda i, at: (i, 0, 0))
    first = pl.BlockSpec((1, 2 * HD, 2 * HD), lambda i, at: (jnp.minimum(i, 1), 0, 0))
    last = pl.BlockSpec((1, 2 * HD, 2 * HD), lambda i, at: (jnp.maximum(i, 2) - 2, 0, 0))
    group = [whole, whole, whole, first, last]
    wide = pl.BlockSpec((2, 2, 2, 1, 2, HD, HD), lambda i, at: (0, 0, 0, i, 0, 0, 0))
    bf16 = jnp.bfloat16
    outs = pl.pallas_call(
        body,
        out_shape=(
            jax.ShapeDtypeStruct((2, 2, 2048, HD), bf16),
            jax.ShapeDtypeStruct((2, 2, 2, 4, 2, HD, HD), bf16),
            jax.ShapeDtypeStruct((2, 2, 2, 4, 2, HD, HD), bf16),
        ),
        grid_spec=pltpu.PrefetchScalarGridSpec(
            num_scalar_prefetch=1,
            grid=(4,),
            in_specs=[quarter] * 4 + group + group,
            out_specs=(
                pl.BlockSpec((2, 2, 512, HD), lambda i, at: (0, 0, i, 0)),
                wide,
                wide,
            ),
        ),
        name="unpack",
    )(at, *q_pieces, *kv_pieces, *kv_others)
    return tuple(out.reshape(D, HD) for out in outs)


def local(hidden, cotangent, seg_ids, advantage, w_query, w_key, w_value):
    f32 = jnp.float32
    bf16 = jnp.bfloat16
    inv_width = D ** (-0.5)
    xh = lax.axis_index("xh")
    xl = lax.axis_index("xl")
    core = lax.axis_index("core")
    zl = lax.axis_index("zl")
    member = zl * 2 + core
    ring = xh * 2 + xl

    token_rows = hidden[0].astype(f32)
    normed_own = (
        token_rows * lax.rsqrt(jnp.mean(token_rows * token_rows, axis=-1, keepdims=True) + norm_eps)
    ).astype(bf16)
    normed = lax.all_gather(swap(normed_own), YZ + ("core",), axis=0, tiled=True)
    cot = swap(cotangent[0])
    seg_row = swap(seg_ids[0])
    adv_row = swap(advantage[0])
    block_len = 512

    at = jnp.stack([xl, xh, core, member]).astype(jnp.int32)
    cut = exchange(pack_columns(w_query, w_key, w_value, at), YZ)
    pieces = (cut,) + ring_pieces(cut)
    others = tuple(flip(p, ("core",)) for p in pieces)
    projected, q_cols, wkv, normed_m = project(normed, pieces, others, at)
    q_cols = q_cols.reshape(D, HD)

    cosine_table, sine_table = angles(seg_row)
    weight_row = token_weights(seg_row, adv_row)
    grad_context = (cot.astype(f32) * weight_row[:, None]).astype(bf16)
    position = jnp.arange(block_len, dtype=jnp.int32)
    allowed = (seg_row[:, None] == seg_row[None, :]) & (position[None, :] <= position[:, None])

    q_rot = rotate(projected[:, :HD], cosine_table, sine_table).astype(bf16)
    k_rot = rotate(projected[:, HD : 2 * HD], cosine_table, sine_table).astype(bf16)
    v_bf = projected[:, 2 * HD :].astype(bf16)

    grad_query, grad_key, grad_value = attend_back(q_rot, k_rot, v_bf, grad_context, allowed)
    scaled_q = (rotate(grad_query, cosine_table, -sine_table) * inv_width).astype(bf16)
    scaled_kv = (
        jnp.concatenate([rotate(grad_key, cosine_table, -sine_table), grad_value], -1) * inv_width
    ).astype(bf16)

    contract = (((0,), (0,)), ((), ()))
    part_q = lax.dot_general(normed, scaled_q, contract, preferred_element_type=f32)
    part_q = part_q.astype(bf16).reshape(4, 2048, HD)

    def part_for(mask):
        return lax.dynamic_index_in_dim(part_q, ring ^ mask, 0, keepdims=False)

    def add(a, b):
        return (a.astype(f32) + b.astype(f32)).astype(bf16)

    far = part_for(2)
    first = flip(far[:1024], X)
    second = flip(far[1024:], ("xl",))
    near, wrap = part_for(1), part_for(3)
    near = jnp.concatenate([add(near[:1024], first), near[1024:]], axis=0)
    wrap = jnp.concatenate([wrap[:1024], add(wrap[1024:], second)], axis=0)
    near = flip(near, ("xl",))
    wrap = flip(wrap, X)
    sum_q = part_for(0).astype(f32) + near.astype(f32) + wrap.astype(f32)
    old_q = lax.dynamic_slice_in_dim(q_cols, ring * 2048, 2048)
    new_q = (old_q.astype(f32) - step_rate * sum_q).astype(bf16)
    near = swap(new_q)
    far = lax.ppermute(
        new_q,
        ("xh", "xl", "core"),
        [
            (h * 4 + l * 2 + c, (1 - h) * 4 + c * 2 + l)
            for h in (0, 1)
            for l in (0, 1)
            for c in (0, 1)
        ],
    )
    near_other = flip(near, ("core",))
    far_other = flip(far, ("core",))
    kv_sum = exchange(scaled_kv.reshape(8, 64, 2 * HD), MEM)
    kv_sum = jnp.sum(kv_sum.astype(f32), axis=0).astype(bf16)
    kv_sum = spread(kv_sum, MEM).reshape(block_len, 2 * HD)
    part_kv = lax.dot_general(
        normed_m, kv_sum, contract, preferred_element_type=f32
    ).astype(bf16)
    part_kv = exchange(part_kv.reshape(4, 256, 2 * HD), X)
    part_kv = part_kv.astype(f32)
    old_kv = wkv.reshape(4, 2, 8, 128, 2 * HD)
    old_kv = lax.dynamic_index_in_dim(old_kv, ring, 0, keepdims=False)
    old_kv = lax.dynamic_index_in_dim(old_kv, member, 1, keepdims=False).reshape(256, 2 * HD)
    new_kv = (old_kv.astype(f32) - step_rate * jnp.sum(part_kv, axis=0)).astype(bf16)
    new_kv = spread(new_kv, ("zl",))
    kv_pieces = (new_kv,) + ring_pieces(new_kv)
    kv_others = tuple(flip(p, ("core",)) for p in kv_pieces)
    return unpack((near, far, near_other, far_other), kv_pieces, kv_others, at)


def solution(mesh):
    grid = Mesh(
        mesh.devices.reshape(2, 4, 2, 4, 2, 2), ("xh", "y", "zh", "zl", "xl", "core")
    )
    groups = ("xh", "core")
    in_specs = (
        P(groups, FS, None),
        P(groups, None, FS),
        P(groups, None),
        P(groups, None),
        P(FS, None),
        P(FS, None),
        P(FS, None),
    )
    out_specs = (P(None, FS), P(None, FS), P(None, FS))

    return jax.shard_map(local, mesh=grid, in_specs=in_specs, out_specs=out_specs, check_vma=False)
```

```python
import jax
import jax.numpy as jnp
from jax import lax
from jax.experimental import pallas as pl
from jax.experimental.pallas import tpu as pltpu
from jax.sharding import Mesh, PartitionSpec as P

D = 8192
HD = 128
RESP = 8

step_rate = 200.0
rope_base = 1000000.0
norm_eps = 1e-06
masked_score = -1e30

YZ = ("y", "zh", "zl")
MEM = ("zl", "core")
X = ("xh", "xl")
FS = ("y", "zh", "zl", "xl")
Z = ("zh", "zl")


def rotate(field, cosine_table, sine_table):
    half_width = field.shape[-1] // 2
    lead_half = field[..., :half_width]
    tail_half = field[..., half_width:]
    return jnp.concatenate(
        [
            lead_half * cosine_table - tail_half * sine_table,
            tail_half * cosine_table + lead_half * sine_table,
        ],
        -1,
    )


def angles(seg_row, place):
    earlier = jnp.sum((seg_row[None, :] < seg_row[:, None]).astype(jnp.int32), axis=1)
    positions = place - earlier
    frequency = rope_base ** (-jnp.arange(HD // 2, dtype=jnp.float32) * 2.0 / HD)
    phase_grid = positions.astype(jnp.float32)[:, None] * frequency[None, :]
    return jnp.cos(phase_grid), jnp.sin(phase_grid)


def token_weights(seg_row, advantage_row):
    id_range = jnp.arange(RESP + 1, dtype=jnp.int32)
    onehot = (seg_row[:, None] == id_range[None, :]).astype(jnp.float32)
    counts = jnp.sum(onehot, axis=0)[:RESP]
    per_token = -advantage_row / counts
    return jnp.sum(onehot[:, :RESP] * per_token[None, :], axis=1)


def attend_back(q_rot, k_rot, v_bf, grad_context, allowed):
    score_scale = HD ** (-0.5)
    f32 = jnp.float32
    scores = jnp.einsum("td,ud->tu", q_rot, k_rot, preferred_element_type=f32) * score_scale
    scores = jnp.where(allowed, scores, masked_score)
    row_top = jnp.max(scores, axis=-1, keepdims=True)
    exponent = jnp.exp(scores - row_top)
    attention = exponent / jnp.sum(exponent, axis=-1, keepdims=True)
    attention_bf = attention.astype(jnp.bfloat16)
    grad_prob = jnp.einsum("td,ud->tu", grad_context, v_bf, preferred_element_type=f32)
    inner_sum = jnp.sum(attention * grad_prob, axis=-1, keepdims=True)
    dscore = (attention * (grad_prob - inner_sum)).astype(jnp.bfloat16)
    grad_query = jnp.einsum("tu,ud->td", dscore, k_rot, preferred_element_type=f32) * score_scale
    grad_key = jnp.einsum("tu,td->ud", dscore, q_rot, preferred_element_type=f32) * score_scale
    grad_value = jnp.einsum("tu,td->ud", attention_bf, grad_context, preferred_element_type=f32)
    return grad_query, grad_key, grad_value


def swap(x):
    return lax.ppermute(x, ("xl", "core"), [(0, 0), (1, 2), (2, 1), (3, 3)])


def flip(x, axes):
    n = 2 ** len(axes)
    return lax.ppermute(x, axes, [(i, n - 1 - i) for i in range(n)])


def shift(x, axes, step):
    n = lax.axis_size(axes)
    return lax.ppermute(x, axes, [((i + step) % n, i) for i in range(n)])


def exchange(x, axes):
    return lax.all_to_all(x, axes, split_axis=0, concat_axis=0, tiled=True)


def spread(x, axes):
    n = lax.axis_size(axes)
    return exchange(jnp.broadcast_to(x[None], (n,) + x.shape), axes)


def ring_pieces(x):
    near, wrap = flip(x, ("xl",)), flip(x, X)
    half = x.shape[0] // 2
    return near, wrap, flip(wrap[:half], ("xl",)), flip(near[half:], X)


def pack_columns(w_query, w_key, w_value, at):
    def body(at_ref, q_ref, k_ref, v_ref, out_ref):
        for j in range(32):
            head = pl.multiple_of((2 * j + at_ref[2]) * HD, HD)
            out_ref[j, 0:64, :] = q_ref[:, pl.ds(head, HD)]
            key = slice(j // 4 * HD, (j // 4 + 1) * HD)
            part = slice(j % 2 * 16, j % 2 * 16 + 16)
            out_ref[j, 64:80, :] = (k_ref if j % 4 < 2 else v_ref)[part, key]

    quarter = pl.BlockSpec((32, 8 * HD), lambda i, at: (2 * at[1] + at[2], 0))
    return pl.pallas_call(
        body,
        out_shape=jax.ShapeDtypeStruct((32, 80, HD), jnp.bfloat16),
        grid_spec=pltpu.PrefetchScalarGridSpec(
            num_scalar_prefetch=1,
            grid=(1,),
            in_specs=[pl.BlockSpec((64, D), lambda i, at: (at[1], 0)), quarter, quarter],
            out_specs=pl.BlockSpec((32, 80, HD), lambda i, at: (0, 0, 0)),
        ),
        name="pack_columns",
    )(at, w_query, w_key, w_value)


def project(normed, q_pieces, kv_pieces, kv_others, at):
    def body(at_ref, rows_ref, *refs):
        q_in, mine, theirs = refs[:5], refs[5:10], refs[10:15]
        out_ref, wq_ref, wkv_ref, member_ref = refs[15:]
        b = pl.program_id(0)
        xl, xh, core = at_ref[0], at_ref[1], at_ref[2]
        spots = ((xl, xh), (1 - xl, xh), (1 - xl, 1 - xh), (xl, 1 - xh))

        for n, (l, h) in enumerate(spots):
            if n < 3:
                wq_ref[:, l, h] = q_in[n][...]
            else:
                wq_ref[:, l, h] = jnp.where(b < 2, q_in[3][...], q_in[4][...])
            for group, c in ((mine, core), (theirs, 1 - core)):
                for part in range(4):
                    if n < 3:
                        piece = group[n][part]
                    else:
                        piece = group[3 + part // 2][part % 2]
                    row, col = part % 2 * 16, part // 2 * HD
                    wkv_ref[:, l, h, c, row : row + 16, col : col + HD] = piece

        rows = rows_ref[...]
        for n in (0, 1):
            member_ref[:, n * HD : (n + 1) * HD] = rows_ref[
                :, pl.ds(pl.multiple_of(n * 1024 + at_ref[3] * HD, HD), HD)
            ]

        @pl.when(b == 0)
        def _():
            out_ref[...] = jnp.zeros_like(out_ref)

        out_ref[:, 0:HD] += jnp.dot(
            rows, wq_ref[...].reshape(2048, HD), preferred_element_type=jnp.float32
        )
        out_ref[:, HD : 3 * HD] += jnp.dot(
            rows, wkv_ref[...].reshape(2048, 2 * HD), preferred_element_type=jnp.float32
        )

    whole = pl.BlockSpec((8, 64, HD), lambda b, at: (b, 0, 0))
    first = pl.BlockSpec((8, 64, HD), lambda b, at: (jnp.minimum(b, 1), 0, 0))
    last = pl.BlockSpec((8, 64, HD), lambda b, at: (jnp.maximum(b, 2) - 2, 0, 0))
    four = pl.BlockSpec((4, 8, 16, HD), lambda b, at: (0, b, 0, 0))
    two = pl.BlockSpec((2, 8, 16, HD), lambda b, at: (0, b, 0, 0))
    group = [four, four, four, two, two]
    bf16 = jnp.bfloat16
    return pl.pallas_call(
        body,
        out_shape=(
            jax.ShapeDtypeStruct((512, 3 * HD), jnp.float32),
            jax.ShapeDtypeStruct((32, 2, 2, 64, HD), bf16),
            jax.ShapeDtypeStruct((32, 2, 2, 2, 32, 2 * HD), bf16),
            jax.ShapeDtypeStruct((512, 1024), bf16),
        ),
        grid_spec=pltpu.PrefetchScalarGridSpec(
            num_scalar_prefetch=1,
            grid=(4,),
            in_specs=[pl.BlockSpec((512, 2048), lambda b, at: (0, b)), whole, whole, whole]
            + [first, last]
            + group
            + group,
            out_specs=(
                pl.BlockSpec((512, 3 * HD), lambda b, at: (0, 0)),
                pl.BlockSpec((8, 2, 2, 64, HD), lambda b, at: (b, 0, 0, 0, 0)),
                pl.BlockSpec((8, 2, 2, 2, 32, 2 * HD), lambda b, at: (b, 0, 0, 0, 0, 0)),
                pl.BlockSpec((512, 2 * HD), lambda b, at: (0, b)),
            ),
        ),
        name="project",
    )(at, normed, *q_pieces, *kv_pieces, *kv_others)


def unpack(q_pieces, kv_pieces, kv_others, at):
    def body(at_ref, *refs):
        q_in, mine, theirs = refs[:4], refs[4:9], refs[9:14]
        q_ref, k_ref, v_ref = refs[14:]
        xl, xh, core = at_ref[0], at_ref[1], at_ref[2]
        line = pl.program_id(0)
        for (h, l), piece in zip(
            ((xh, core), (1 - xh, core), (xh, 1 - core), (1 - xh, 1 - core)), q_in
        ):
            q_ref[h, l] = piece[...]
        spots = ((xl, xh), (1 - xl, xh), (1 - xl, 1 - xh), (xl, 1 - xh))
        for group, c in ((mine, core), (theirs, 1 - core)):
            for n, (l, h) in enumerate(spots):
                if n < 3:
                    piece = group[n][...]
                else:
                    piece = jnp.where(line < 2, group[3][...], group[4][...])
                for z in (0, 1):
                    k_ref[h, l, z, 0, c] = piece[0, z * HD : (z + 1) * HD, 0:HD]
                    v_ref[h, l, z, 0, c] = piece[0, z * HD : (z + 1) * HD, HD : 2 * HD]

    quarter = pl.BlockSpec((512, HD), lambda i, at: (i, 0))
    whole = pl.BlockSpec((1, 2 * HD, 2 * HD), lambda i, at: (i, 0, 0))
    first = pl.BlockSpec((1, 2 * HD, 2 * HD), lambda i, at: (jnp.minimum(i, 1), 0, 0))
    last = pl.BlockSpec((1, 2 * HD, 2 * HD), lambda i, at: (jnp.maximum(i, 2) - 2, 0, 0))
    group = [whole, whole, whole, first, last]
    wide = pl.BlockSpec((2, 2, 2, 1, 2, HD, HD), lambda i, at: (0, 0, 0, i, 0, 0, 0))
    bf16 = jnp.bfloat16
    outs = pl.pallas_call(
        body,
        out_shape=(
            jax.ShapeDtypeStruct((2, 2, 2048, HD), bf16),
            jax.ShapeDtypeStruct((2, 2, 2, 4, 2, HD, HD), bf16),
            jax.ShapeDtypeStruct((2, 2, 2, 4, 2, HD, HD), bf16),
        ),
        grid_spec=pltpu.PrefetchScalarGridSpec(
            num_scalar_prefetch=1,
            grid=(4,),
            in_specs=[quarter] * 4 + group + group,
            out_specs=(
                pl.BlockSpec((2, 2, 512, HD), lambda i, at: (0, 0, i, 0)),
                wide,
                wide,
            ),
        ),
        name="unpack",
    )(at, *q_pieces, *kv_pieces, *kv_others)
    return tuple(out.reshape(D, HD) for out in outs)


def local(hidden, cotangent, seg_ids, advantage, w_query, w_key, w_value):
    f32 = jnp.float32
    bf16 = jnp.bfloat16
    inv_width = D ** (-0.5)
    xh = lax.axis_index("xh")
    xl = lax.axis_index("xl")
    core = lax.axis_index("core")
    zl = lax.axis_index("zl")
    member = zl * 2 + core
    ring = xh * 2 + xl

    token_rows = hidden[0].astype(f32)
    normed_own = (
        token_rows * lax.rsqrt(jnp.mean(token_rows * token_rows, axis=-1, keepdims=True) + norm_eps)
    ).astype(bf16)
    normed_own = swap(normed_own)
    others = [shift(normed_own, ("y",), step) for step in (1, 2, 3)]
    normed = lax.all_gather(
        jnp.concatenate([normed_own] + others, axis=0), Z + ("core",), axis=0, tiled=True
    )
    y = lax.axis_index("y")

    def in_order(x):
        x = x.reshape((4, 8, 2, 8) + x.shape[1:])
        x = lax.dynamic_slice_in_dim(jnp.concatenate([x, x], axis=0), y, 4)
        return jnp.moveaxis(x, 0, 2).reshape((512,) + x.shape[4:])

    cot = in_order(swap(cotangent[0]))
    seg_row = in_order(swap(seg_ids[0]))
    place = in_order(jnp.arange(512, dtype=jnp.int32))
    adv_row = swap(advantage[0])
    block_len = 512

    at = jnp.stack([xl, xh, core, member]).astype(jnp.int32)
    packed = pack_columns(w_query, w_key, w_value, at)
    cut = exchange(packed, YZ)
    wkv = spread(cut[:, 64:], ("zl",))
    wq = cut[:, :64]
    q_pieces = (wq,) + ring_pieces(wq)
    kv_pieces = (wkv,) + ring_pieces(wkv)
    kv_others = tuple(flip(p, ("core",)) for p in kv_pieces)
    projected, q_cols, wkv, normed_m = project(normed, q_pieces, kv_pieces, kv_others, at)
    projected = projected * inv_width
    q_cols = q_cols.reshape(D, HD)

    cosine_table, sine_table = angles(seg_row, place)
    weight_row = token_weights(seg_row, adv_row)
    grad_context = (cot.astype(f32) * weight_row[:, None]).astype(bf16)
    allowed = (seg_row[:, None] == seg_row[None, :]) & (place[None, :] <= place[:, None])

    q_rot = rotate(projected[:, :HD], cosine_table, sine_table).astype(bf16)
    k_rot = rotate(projected[:, HD : 2 * HD], cosine_table, sine_table).astype(bf16)
    v_bf = projected[:, 2 * HD :].astype(bf16)

    grad_query, grad_key, grad_value = attend_back(q_rot, k_rot, v_bf, grad_context, allowed)
    scaled_q = (rotate(grad_query, cosine_table, -sine_table) * inv_width).astype(bf16)
    scaled_kv = (
        jnp.concatenate([rotate(grad_key, cosine_table, -sine_table), grad_value], -1) * inv_width
    ).astype(bf16)

    contract = (((0,), (0,)), ((), ()))
    part_q = lax.dot_general(normed, scaled_q, contract, preferred_element_type=f32)
    part_q = part_q.astype(bf16).reshape(4, 2048, HD)

    def part_for(mask):
        return lax.dynamic_index_in_dim(part_q, ring ^ mask, 0, keepdims=False)

    def add(a, b):
        return (a.astype(f32) + b.astype(f32)).astype(bf16)

    far = part_for(2)
    first = flip(far[:1024], X)
    second = flip(far[1024:], ("xl",))
    near, wrap = part_for(1), part_for(3)
    near = jnp.concatenate([add(near[:1024], first), near[1024:]], axis=0)
    wrap = jnp.concatenate([wrap[:1024], add(wrap[1024:], second)], axis=0)
    near = flip(near, ("xl",))
    wrap = flip(wrap, X)
    sum_q = part_for(0).astype(f32) + near.astype(f32) + wrap.astype(f32)
    old_q = lax.dynamic_slice_in_dim(q_cols, ring * 2048, 2048)
    new_q = (old_q.astype(f32) - step_rate * sum_q).astype(bf16)
    near = swap(new_q)
    far = lax.ppermute(
        new_q,
        ("xh", "xl", "core"),
        [
            (h * 4 + l * 2 + c, (1 - h) * 4 + c * 2 + l)
            for h in (0, 1)
            for l in (0, 1)
            for c in (0, 1)
        ],
    )
    near_other = flip(near, ("core",))
    far_other = flip(far, ("core",))
    kv_sum = exchange(scaled_kv.reshape(8, 64, 2 * HD), MEM)
    kv_sum = jnp.sum(kv_sum.astype(f32), axis=0).astype(bf16)
    kv_sum = spread(kv_sum, MEM).reshape(block_len, 2 * HD)
    part_kv = lax.dot_general(
        normed_m, kv_sum, contract, preferred_element_type=f32
    ).astype(bf16)
    part_kv = exchange(part_kv.reshape(4, 256, 2 * HD), X).astype(f32)
    old_kv = wkv.reshape(4, 2, 8, 128, 2 * HD)
    old_kv = lax.dynamic_index_in_dim(old_kv, ring, 0, keepdims=False)
    old_kv = lax.dynamic_index_in_dim(old_kv, member, 1, keepdims=False).reshape(256, 2 * HD)
    new_kv = (old_kv.astype(f32) - step_rate * jnp.sum(part_kv, axis=0)).astype(bf16)
    new_kv = spread(new_kv, ("zl",))
    kv_pieces = (new_kv,) + ring_pieces(new_kv)
    kv_others = tuple(flip(p, ("core",)) for p in kv_pieces)
    return unpack((near, far, near_other, far_other), kv_pieces, kv_others, at)


def solution(mesh):
    grid = Mesh(
        mesh.devices.reshape(2, 4, 2, 4, 2, 2), ("xh", "y", "zh", "zl", "xl", "core")
    )
    groups = ("xh", "core")
    in_specs = (
        P(groups, FS, None),
        P(groups, None, FS),
        P(groups, None),
        P(groups, None),
        P(FS, None),
        P(FS, None),
        P(FS, None),
    )
    out_specs = (P(None, FS), P(None, FS), P(None, FS))

    return jax.shard_map(local, mesh=grid, in_specs=in_specs, out_specs=out_specs, check_vma=False)
```

```python
import jax
import jax.numpy as jnp
from jax import lax
from jax.experimental import pallas as pl
from jax.experimental.pallas import tpu as pltpu
from jax.sharding import Mesh, PartitionSpec as P

D = 8192
HD = 128
RESP = 8

step_rate = 200.0
rope_base = 1000000.0
norm_eps = 1e-06
masked_score = -1e30

YZ = ("y", "zh", "zl")
MEM = ("zl", "core")
X = ("xh", "xl")
FS = ("y", "zh", "zl", "xl")


def rotate(field, cosine_table, sine_table):
    half_width = field.shape[-1] // 2
    lead_half = field[..., :half_width]
    tail_half = field[..., half_width:]
    return jnp.concatenate(
        [
            lead_half * cosine_table - tail_half * sine_table,
            tail_half * cosine_table + lead_half * sine_table,
        ],
        -1,
    )


def angles(seg_row):
    span_count = seg_row.shape[0]
    earlier = jnp.sum((seg_row[None, :] < seg_row[:, None]).astype(jnp.int32), axis=1)
    positions = jnp.arange(span_count, dtype=jnp.int32) - earlier
    frequency = rope_base ** (-jnp.arange(HD // 2, dtype=jnp.float32) * 2.0 / HD)
    phase_grid = positions.astype(jnp.float32)[:, None] * frequency[None, :]
    return jnp.cos(phase_grid), jnp.sin(phase_grid)


def token_weights(seg_row, advantage_row):
    id_range = jnp.arange(RESP + 1, dtype=jnp.int32)
    onehot = (seg_row[:, None] == id_range[None, :]).astype(jnp.float32)
    counts = jnp.sum(onehot, axis=0)[:RESP]
    per_token = -advantage_row / counts
    return jnp.sum(onehot[:, :RESP] * per_token[None, :], axis=1)


def attend_back(q_rot, k_rot, v_bf, grad_context, allowed):
    score_scale = HD ** (-0.5)
    f32 = jnp.float32
    scores = jnp.einsum("td,ud->tu", q_rot, k_rot, preferred_element_type=f32) * score_scale
    scores = jnp.where(allowed, scores, masked_score)
    row_top = jnp.max(scores, axis=-1, keepdims=True)
    exponent = jnp.exp(scores - row_top)
    attention = exponent / jnp.sum(exponent, axis=-1, keepdims=True)
    attention_bf = attention.astype(jnp.bfloat16)
    grad_prob = jnp.einsum("td,ud->tu", grad_context, v_bf, preferred_element_type=f32)
    inner_sum = jnp.sum(attention * grad_prob, axis=-1, keepdims=True)
    dscore = (attention * (grad_prob - inner_sum)).astype(jnp.bfloat16)
    grad_query = jnp.einsum("tu,ud->td", dscore, k_rot, preferred_element_type=f32) * score_scale
    grad_key = jnp.einsum("tu,td->ud", dscore, q_rot, preferred_element_type=f32) * score_scale
    grad_value = jnp.einsum("tu,td->ud", attention_bf, grad_context, preferred_element_type=f32)
    return grad_query, grad_key, grad_value


def swap(x):
    return lax.ppermute(x, ("xl", "core"), [(0, 0), (1, 2), (2, 1), (3, 3)])


def flip(x, axes):
    n = 2 ** len(axes)
    return lax.ppermute(x, axes, [(i, n - 1 - i) for i in range(n)])


def exchange(x, axes):
    return lax.all_to_all(x, axes, split_axis=0, concat_axis=0, tiled=True)


def spread(x, axes):
    n = lax.axis_size(axes)
    return exchange(jnp.broadcast_to(x[None], (n,) + x.shape), axes)


def ring_pieces(x):
    near, wrap = flip(x, ("xl",)), flip(x, X)
    half = x.shape[0] // 2
    return near, wrap, flip(wrap[:half], ("xl",)), flip(near[half:], X)


def pack_columns(w_query, w_key, w_value, at):
    def body(at_ref, q_ref, k_ref, v_ref, out_ref):
        for j in range(32):
            head = pl.multiple_of((2 * j + at_ref[2]) * HD, HD)
            out_ref[j, 0:64, :] = q_ref[:, pl.ds(head, HD)]
            key = slice(j // 4 * HD, (j // 4 + 1) * HD)
            out_ref[j, 64:96, :] = k_ref[:, key]
            out_ref[j, 96:128, :] = v_ref[:, key]

    quarter = pl.BlockSpec((32, 8 * HD), lambda i, at: (2 * at[1] + at[2], 0))
    return pl.pallas_call(
        body,
        out_shape=jax.ShapeDtypeStruct((32, 128, HD), jnp.bfloat16),
        grid_spec=pltpu.PrefetchScalarGridSpec(
            num_scalar_prefetch=1,
            grid=(1,),
            in_specs=[pl.BlockSpec((64, D), lambda i, at: (at[1], 0)), quarter, quarter],
            out_specs=pl.BlockSpec((32, 128, HD), lambda i, at: (0, 0, 0)),
        ),
        name="pack_columns",
    )(at, w_query, w_key, w_value)


def project(normed, pieces, others, at):
    def body(at_ref, rows_ref, *refs):
        mine, theirs = refs[:5], refs[5:10]
        out_ref, wq_ref, wkv_ref, member_ref = refs[10:]
        b = pl.program_id(0)
        xl, xh, core = at_ref[0], at_ref[1], at_ref[2]
        spots = ((xl, xh), (1 - xl, xh), (1 - xl, 1 - xh), (xl, 1 - xh))

        def block(group, n):
            if n < 3:
                return group[n][...]
            return jnp.where(b < 2, group[3][...], group[4][...])

        for n, (l, h) in enumerate(spots):
            own = block(mine, n)
            other = block(theirs, n)
            wq_ref[:, l, h] = own[:, :64]
            wkv_ref[:, l, h, core, :, 0:HD] = own[:, 64:96]
            wkv_ref[:, l, h, core, :, HD : 2 * HD] = own[:, 96:128]
            wkv_ref[:, l, h, 1 - core, :, 0:HD] = other[:, 64:96]
            wkv_ref[:, l, h, 1 - core, :, HD : 2 * HD] = other[:, 96:128]

        rows = rows_ref[...]
        for n in (0, 1):
            member_ref[:, n * HD : (n + 1) * HD] = rows_ref[
                :, pl.ds(pl.multiple_of(n * 1024 + at_ref[3] * HD, HD), HD)
            ]

        @pl.when(b == 0)
        def _():
            out_ref[...] = jnp.zeros_like(out_ref)

        out_ref[:, 0:HD] += jnp.dot(
            rows, wq_ref[...].reshape(2048, HD), preferred_element_type=jnp.float32
        )
        out_ref[:, HD : 3 * HD] += jnp.dot(
            rows, wkv_ref[...].reshape(2048, 2 * HD), preferred_element_type=jnp.float32
        )

    whole = pl.BlockSpec((8, 128, HD), lambda b, at: (b, 0, 0))
    first = pl.BlockSpec((8, 128, HD), lambda b, at: (jnp.minimum(b, 1), 0, 0))
    last = pl.BlockSpec((8, 128, HD), lambda b, at: (jnp.maximum(b, 2) - 2, 0, 0))
    group = [whole, whole, whole, first, last]
    bf16 = jnp.bfloat16
    return pl.pallas_call(
        body,
        out_shape=(
            jax.ShapeDtypeStruct((512, 3 * HD), jnp.float32),
            jax.ShapeDtypeStruct((32, 2, 2, 64, HD), bf16),
            jax.ShapeDtypeStruct((32, 2, 2, 2, 32, 2 * HD), bf16),
            jax.ShapeDtypeStruct((512, 1024), bf16),
        ),
        grid_spec=pltpu.PrefetchScalarGridSpec(
            num_scalar_prefetch=1,
            grid=(4,),
            in_specs=[pl.BlockSpec((512, 2048), lambda b, at: (0, b))] + group + group,
            out_specs=(
                pl.BlockSpec((512, 3 * HD), lambda b, at: (0, 0)),
                pl.BlockSpec((8, 2, 2, 64, HD), lambda b, at: (b, 0, 0, 0, 0)),
                pl.BlockSpec((8, 2, 2, 2, 32, 2 * HD), lambda b, at: (b, 0, 0, 0, 0, 0)),
                pl.BlockSpec((512, 2 * HD), lambda b, at: (0, b)),
            ),
        ),
        name="project",
    )(at, normed, *pieces, *others)


WIDE = jax.ShapeDtypeStruct((2, 2, 2, 4, 2, HD, HD), jnp.bfloat16)


def unpack_query(q_pieces, at):
    def body(at_ref, near_ref, far_ref, near_other_ref, far_other_ref, out_ref):
        xh, core = at_ref[1], at_ref[2]
        out_ref[xh, core] = near_ref[...]
        out_ref[1 - xh, core] = far_ref[...]
        out_ref[xh, 1 - core] = near_other_ref[...]
        out_ref[1 - xh, 1 - core] = far_other_ref[...]

    return pl.pallas_call(
        body,
        out_shape=jax.ShapeDtypeStruct((2, 2, 2048, HD), jnp.bfloat16),
        grid_spec=pltpu.PrefetchScalarGridSpec(
            num_scalar_prefetch=1,
            grid=(4,),
            in_specs=[pl.BlockSpec((512, HD), lambda i, at: (i, 0))] * 4,
            out_specs=pl.BlockSpec((2, 2, 512, HD), lambda i, at: (0, 0, i, 0)),
        ),
        name="unpack_query",
    )(at, *q_pieces)


def unpack_near(kv_pieces, kv_others, at):
    def body(at_ref, *refs):
        mine, theirs = refs[:3], refs[3:6]
        k_ref, v_ref = refs[6:]
        core = at_ref[2]
        for n in range(3):

            @pl.when(pl.program_id(0) == n)
            def _(n=n):
                for group, c in ((mine, core), (theirs, 1 - core)):
                    for line in range(4):
                        for z in range(2):
                            rows = slice(z * HD, (z + 1) * HD)
                            k_ref[0, 0, z, line, c] = group[n][line, rows, 0:HD]
                            v_ref[0, 0, z, line, c] = group[n][line, rows, HD : 2 * HD]

    def spot(n, at):
        xl, xh = at[0], at[1]
        return (jnp.where(n == 2, 1 - xh, xh), jnp.where(n == 0, xl, 1 - xl), 0, 0, 0, 0, 0)

    whole = pl.BlockSpec((4, 2 * HD, 2 * HD), lambda n, at: (0, 0, 0))
    wide = pl.BlockSpec((1, 1, 2, 4, 2, HD, HD), spot)
    return pl.pallas_call(
        body,
        out_shape=(WIDE, WIDE),
        grid_spec=pltpu.PrefetchScalarGridSpec(
            num_scalar_prefetch=1, grid=(3,), in_specs=[whole] * 6, out_specs=(wide, wide)
        ),
        name="unpack_near",
    )(at, *kv_pieces, *kv_others)


def unpack_far(far, far_other, keys, values, at):
    def body(at_ref, low_ref, high_ref, low_other_ref, high_other_ref, _k, _v, k_ref, v_ref):
        core = at_ref[2]
        for n, group in enumerate(((low_ref, low_other_ref), (high_ref, high_other_ref))):

            @pl.when(pl.program_id(0) == n)
            def _(group=group):
                for piece, c in zip(group, (core, 1 - core)):
                    for line in range(2):
                        for z in range(2):
                            rows = slice(z * HD, (z + 1) * HD)
                            k_ref[0, 0, z, line, c] = piece[line, rows, 0:HD]
                            v_ref[0, 0, z, line, c] = piece[line, rows, HD : 2 * HD]

    whole = pl.BlockSpec((2, 2 * HD, 2 * HD), lambda n, at: (0, 0, 0))
    wide = pl.BlockSpec((1, 1, 2, 2, 2, HD, HD), lambda n, at: (1 - at[1], at[0], 0, n, 0, 0, 0))
    there = pl.BlockSpec(memory_space=pl.ANY)
    return pl.pallas_call(
        body,
        out_shape=(WIDE, WIDE),
        grid_spec=pltpu.PrefetchScalarGridSpec(
            num_scalar_prefetch=1,
            grid=(2,),
            in_specs=[whole] * 4 + [there, there],
            out_specs=(wide, wide),
        ),
        input_output_aliases={5: 0, 6: 1},
        name="unpack_far",
    )(at, *far, *far_other, keys, values)


def local(hidden, cotangent, seg_ids, advantage, w_query, w_key, w_value):
    f32 = jnp.float32
    bf16 = jnp.bfloat16
    inv_width = D ** (-0.5)
    xh = lax.axis_index("xh")
    xl = lax.axis_index("xl")
    core = lax.axis_index("core")
    zl = lax.axis_index("zl")
    member = zl * 2 + core
    ring = xh * 2 + xl

    token_rows = hidden[0].astype(f32)
    normed_own = (
        token_rows * lax.rsqrt(jnp.mean(token_rows * token_rows, axis=-1, keepdims=True) + norm_eps)
    ).astype(bf16)
    normed = lax.all_gather(swap(normed_own), YZ + ("core",), axis=0, tiled=True)
    cot = swap(cotangent[0])
    seg_row = swap(seg_ids[0])
    adv_row = swap(advantage[0])
    block_len = 512

    at = jnp.stack([xl, xh, core, member]).astype(jnp.int32)
    cut = exchange(pack_columns(w_query, w_key, w_value, at), YZ)
    pieces = (cut,) + ring_pieces(cut)
    others = tuple(flip(p, ("core",)) for p in pieces)
    projected, q_cols, wkv, normed_m = project(normed, pieces, others, at)
    projected = projected * inv_width
    q_cols = q_cols.reshape(D, HD)

    cosine_table, sine_table = angles(seg_row)
    weight_row = token_weights(seg_row, adv_row)
    grad_context = (cot.astype(f32) * weight_row[:, None]).astype(bf16)
    position = jnp.arange(block_len, dtype=jnp.int32)
    allowed = (seg_row[:, None] == seg_row[None, :]) & (position[None, :] <= position[:, None])

    q_rot = rotate(projected[:, :HD], cosine_table, sine_table).astype(bf16)
    k_rot = rotate(projected[:, HD : 2 * HD], cosine_table, sine_table).astype(bf16)
    v_bf = projected[:, 2 * HD :].astype(bf16)

    grad_query, grad_key, grad_value = attend_back(q_rot, k_rot, v_bf, grad_context, allowed)
    scaled_q = (rotate(grad_query, cosine_table, -sine_table) * inv_width).astype(bf16)
    scaled_kv = (
        jnp.concatenate([rotate(grad_key, cosine_table, -sine_table), grad_value], -1) * inv_width
    ).astype(bf16)

    contract = (((0,), (0,)), ((), ()))
    part_q = lax.dot_general(normed, scaled_q, contract, preferred_element_type=f32)
    part_q = part_q.astype(bf16).reshape(4, 2048, HD)

    def part_for(mask):
        return lax.dynamic_index_in_dim(part_q, ring ^ mask, 0, keepdims=False)

    def add(a, b):
        return (a.astype(f32) + b.astype(f32)).astype(bf16)

    far = part_for(2)
    first = flip(far[:1024], X)
    second = flip(far[1024:], ("xl",))
    near, wrap = part_for(1), part_for(3)
    near = jnp.concatenate([add(near[:1024], first), near[1024:]], axis=0)
    wrap = jnp.concatenate([wrap[:1024], add(wrap[1024:], second)], axis=0)
    near = flip(near, ("xl",))
    wrap = flip(wrap, X)
    sum_q = part_for(0).astype(f32) + near.astype(f32) + wrap.astype(f32)
    old_q = lax.dynamic_slice_in_dim(q_cols, ring * 2048, 2048)
    new_q = (old_q.astype(f32) - step_rate * sum_q).astype(bf16)
    near = swap(new_q)
    far = lax.ppermute(
        new_q,
        ("xh", "xl", "core"),
        [
            (h * 4 + l * 2 + c, (1 - h) * 4 + c * 2 + l)
            for h in (0, 1)
            for l in (0, 1)
            for c in (0, 1)
        ],
    )
    near_other = flip(near, ("core",))
    far_other = flip(far, ("core",))
    kv_sum = exchange(scaled_kv.reshape(8, 64, 2 * HD), MEM)
    kv_sum = jnp.sum(kv_sum.astype(f32), axis=0).astype(bf16)
    kv_sum = spread(kv_sum, MEM).reshape(block_len, 2 * HD)
    part_kv = lax.dot_general(
        normed_m, kv_sum, contract, preferred_element_type=f32
    ).astype(bf16)
    part_kv = exchange(part_kv.reshape(4, 256, 2 * HD), X)
    part_kv = part_kv.astype(f32)
    old_kv = wkv.reshape(4, 2, 8, 128, 2 * HD)
    old_kv = lax.dynamic_index_in_dim(old_kv, ring, 0, keepdims=False)
    old_kv = lax.dynamic_index_in_dim(old_kv, member, 1, keepdims=False).reshape(256, 2 * HD)
    new_kv = (old_kv.astype(f32) - step_rate * jnp.sum(part_kv, axis=0)).astype(bf16)
    new_kv = spread(new_kv, ("zl",))
    near_kv, wrap_kv = flip(new_kv, ("xl",)), flip(new_kv, X)
    far_kv = (flip(wrap_kv[:2], ("xl",)), flip(near_kv[2:], X))
    kv_pieces = (new_kv, near_kv, wrap_kv)
    kv_others = tuple(flip(p, ("core",)) for p in kv_pieces)
    far_others = tuple(flip(p, ("core",)) for p in far_kv)
    roll_q = unpack_query((near, far, near_other, far_other), at)
    keys, values = unpack_near(kv_pieces, kv_others, at)
    keys, values = unpack_far(far_kv, far_others, keys, values, at)
    return tuple(out.reshape(D, HD) for out in (roll_q, keys, values))


def solution(mesh):
    grid = Mesh(
        mesh.devices.reshape(2, 4, 2, 4, 2, 2), ("xh", "y", "zh", "zl", "xl", "core")
    )
    groups = ("xh", "core")
    in_specs = (
        P(groups, FS, None),
        P(groups, None, FS),
        P(groups, None),
        P(groups, None),
        P(FS, None),
        P(FS, None),
        P(FS, None),
    )
    out_specs = (P(None, FS), P(None, FS), P(None, FS))

    return jax.shard_map(local, mesh=grid, in_specs=in_specs, out_specs=out_specs, check_vma=False)
```

```python
import jax
import jax.numpy as jnp
from jax import lax
from jax.experimental import pallas as pl
from jax.experimental.pallas import tpu as pltpu
from jax.sharding import Mesh, PartitionSpec as P

D = 8192
HD = 128
RESP = 8

step_rate = 200.0
rope_base = 1000000.0
norm_eps = 1e-06
masked_score = -1e30

YZ = ("y", "zh", "zl")
MEM = ("zl", "core")
X = ("xh", "xl")
FS = ("y", "zh", "zl", "xl")


def rotate(field, cosine_table, sine_table):
    half_width = field.shape[-1] // 2
    lead_half = field[..., :half_width]
    tail_half = field[..., half_width:]
    return jnp.concatenate(
        [
            lead_half * cosine_table - tail_half * sine_table,
            tail_half * cosine_table + lead_half * sine_table,
        ],
        -1,
    )


def angles(seg_row):
    span_count = seg_row.shape[0]
    earlier = jnp.sum((seg_row[None, :] < seg_row[:, None]).astype(jnp.int32), axis=1)
    positions = jnp.arange(span_count, dtype=jnp.int32) - earlier
    frequency = rope_base ** (-jnp.arange(HD // 2, dtype=jnp.float32) * 2.0 / HD)
    phase_grid = positions.astype(jnp.float32)[:, None] * frequency[None, :]
    return jnp.cos(phase_grid), jnp.sin(phase_grid)


def token_weights(seg_row, advantage_row):
    id_range = jnp.arange(RESP + 1, dtype=jnp.int32)
    onehot = (seg_row[:, None] == id_range[None, :]).astype(jnp.float32)
    counts = jnp.sum(onehot, axis=0)[:RESP]
    per_token = -advantage_row / counts
    return jnp.sum(onehot[:, :RESP] * per_token[None, :], axis=1)


def attend_back(q_rot, k_rot, v_bf, grad_context, allowed):
    score_scale = HD ** (-0.5)
    f32 = jnp.float32
    scores = jnp.einsum("td,ud->tu", q_rot, k_rot, preferred_element_type=f32) * score_scale
    scores = jnp.where(allowed, scores, masked_score)
    row_top = jnp.max(scores, axis=-1, keepdims=True)
    exponent = jnp.exp(scores - row_top)
    attention = exponent / jnp.sum(exponent, axis=-1, keepdims=True)
    attention_bf = attention.astype(jnp.bfloat16)
    grad_prob = jnp.einsum("td,ud->tu", grad_context, v_bf, preferred_element_type=f32)
    inner_sum = jnp.sum(attention * grad_prob, axis=-1, keepdims=True)
    dscore = (attention * (grad_prob - inner_sum)).astype(jnp.bfloat16)
    grad_query = jnp.einsum("tu,ud->td", dscore, k_rot, preferred_element_type=f32) * score_scale
    grad_key = jnp.einsum("tu,td->ud", dscore, q_rot, preferred_element_type=f32) * score_scale
    grad_value = jnp.einsum("tu,td->ud", attention_bf, grad_context, preferred_element_type=f32)
    return grad_query, grad_key, grad_value


def swap(x):
    return lax.ppermute(x, ("xl", "core"), [(0, 0), (1, 2), (2, 1), (3, 3)])


def flip(x, axes):
    n = 2 ** len(axes)
    return lax.ppermute(x, axes, [(i, n - 1 - i) for i in range(n)])


def exchange(x, axes):
    return lax.all_to_all(x, axes, split_axis=0, concat_axis=0, tiled=True)


def spread(x, axes):
    n = lax.axis_size(axes)
    return exchange(jnp.broadcast_to(x[None], (n,) + x.shape), axes)


def ring_pieces(x):
    near, wrap = flip(x, ("xl",)), flip(x, X)
    half = x.shape[0] // 2
    return near, wrap, flip(wrap[:half], ("xl",)), flip(near[half:], X)


def pack_columns(w_query, w_key, w_value, at):
    def body(at_ref, q_ref, k_ref, v_ref, out_ref):
        for j in range(32):
            head = pl.multiple_of((2 * j + at_ref[2]) * HD, HD)
            out_ref[j, 0:64, :] = q_ref[:, pl.ds(head, HD)]
            key = slice(j // 4 * HD, (j // 4 + 1) * HD)
            out_ref[j, 64:96, :] = k_ref[:, key]
            out_ref[j, 96:128, :] = v_ref[:, key]

    quarter = pl.BlockSpec((32, 8 * HD), lambda i, at: (2 * at[1] + at[2], 0))
    return pl.pallas_call(
        body,
        out_shape=jax.ShapeDtypeStruct((32, 128, HD), jnp.bfloat16),
        grid_spec=pltpu.PrefetchScalarGridSpec(
            num_scalar_prefetch=1,
            grid=(1,),
            in_specs=[pl.BlockSpec((64, D), lambda i, at: (at[1], 0)), quarter, quarter],
            out_specs=pl.BlockSpec((32, 128, HD), lambda i, at: (0, 0, 0)),
        ),
        name="pack_columns",
    )(at, w_query, w_key, w_value)


def project(normed, pieces, others, at):
    def body(at_ref, rows_ref, *refs):
        mine, theirs = refs[:5], refs[5:10]
        out_ref, wq_ref, wkv_ref, member_ref = refs[10:]
        b = pl.program_id(0)
        xl, xh, core = at_ref[0], at_ref[1], at_ref[2]
        spots = ((xl, xh), (1 - xl, xh), (1 - xl, 1 - xh), (xl, 1 - xh))

        def block(group, n):
            if n < 3:
                return group[n][...]
            return jnp.where(b < 2, group[3][...], group[4][...])

        for n, (l, h) in enumerate(spots):
            own = block(mine, n)
            other = block(theirs, n)
            wq_ref[:, l, h] = own[:, :64]
            wkv_ref[:, l, h, core, :, 0:HD] = own[:, 64:96]
            wkv_ref[:, l, h, core, :, HD : 2 * HD] = own[:, 96:128]
            wkv_ref[:, l, h, 1 - core, :, 0:HD] = other[:, 64:96]
            wkv_ref[:, l, h, 1 - core, :, HD : 2 * HD] = other[:, 96:128]

        rows = rows_ref[...]
        for n in (0, 1):
            member_ref[:, n * HD : (n + 1) * HD] = rows_ref[
                :, pl.ds(pl.multiple_of(n * 1024 + at_ref[3] * HD, HD), HD)
            ]

        @pl.when(b == 0)
        def _():
            out_ref[...] = jnp.zeros_like(out_ref)

        out_ref[:, 0:HD] += jnp.dot(
            rows, wq_ref[...].reshape(2048, HD), preferred_element_type=jnp.float32
        )
        out_ref[:, HD : 3 * HD] += jnp.dot(
            rows, wkv_ref[...].reshape(2048, 2 * HD), preferred_element_type=jnp.float32
        )

    whole = pl.BlockSpec((8, 128, HD), lambda b, at: (b, 0, 0))
    first = pl.BlockSpec((8, 128, HD), lambda b, at: (jnp.minimum(b, 1), 0, 0))
    last = pl.BlockSpec((8, 128, HD), lambda b, at: (jnp.maximum(b, 2) - 2, 0, 0))
    group = [whole, whole, whole, first, last]
    bf16 = jnp.bfloat16
    return pl.pallas_call(
        body,
        out_shape=(
            jax.ShapeDtypeStruct((512, 3 * HD), jnp.float32),
            jax.ShapeDtypeStruct((32, 2, 2, 64, HD), bf16),
            jax.ShapeDtypeStruct((32, 2, 2, 2, 32, 2 * HD), bf16),
            jax.ShapeDtypeStruct((512, 1024), bf16),
        ),
        grid_spec=pltpu.PrefetchScalarGridSpec(
            num_scalar_prefetch=1,
            grid=(4,),
            in_specs=[pl.BlockSpec((512, 2048), lambda b, at: (0, b))] + group + group,
            out_specs=(
                pl.BlockSpec((512, 3 * HD), lambda b, at: (0, 0)),
                pl.BlockSpec((8, 2, 2, 64, HD), lambda b, at: (b, 0, 0, 0, 0)),
                pl.BlockSpec((8, 2, 2, 2, 32, 2 * HD), lambda b, at: (b, 0, 0, 0, 0, 0)),
                pl.BlockSpec((512, 2 * HD), lambda b, at: (0, b)),
            ),
        ),
        name="project",
    )(at, normed, *pieces, *others)


def unpack(q_pieces, kv_pieces, kv_others, at):
    def body(at_ref, *refs):
        q_in, mine, theirs = refs[:4], refs[4:9], refs[9:14]
        q_ref, k_ref, v_ref = refs[14:]
        xl, xh, core = at_ref[0], at_ref[1], at_ref[2]
        line = pl.program_id(0)
        for (h, l), piece in zip(
            ((xh, core), (1 - xh, core), (xh, 1 - core), (1 - xh, 1 - core)), q_in
        ):
            q_ref[h, l] = piece[...]
        spots = ((xl, xh), (1 - xl, xh), (1 - xl, 1 - xh), (xl, 1 - xh))
        for group, c in ((mine, core), (theirs, 1 - core)):
            for n, (l, h) in enumerate(spots):
                if n < 3:
                    piece = group[n][...]
                else:
                    piece = jnp.where(line < 2, group[3][...], group[4][...])
                for z in (0, 1):
                    k_ref[h, l, z, 0, c] = piece[0, z * HD : (z + 1) * HD, 0:HD]
                    v_ref[h, l, z, 0, c] = piece[0, z * HD : (z + 1) * HD, HD : 2 * HD]

    quarter = pl.BlockSpec((512, HD), lambda i, at: (i, 0))
    whole = pl.BlockSpec((1, 2 * HD, 2 * HD), lambda i, at: (i, 0, 0))
    first = pl.BlockSpec((1, 2 * HD, 2 * HD), lambda i, at: (jnp.minimum(i, 1), 0, 0))
    last = pl.BlockSpec((1, 2 * HD, 2 * HD), lambda i, at: (jnp.maximum(i, 2) - 2, 0, 0))
    group = [whole, whole, whole, first, last]
    wide = pl.BlockSpec((2, 2, 2, 1, 2, HD, HD), lambda i, at: (0, 0, 0, i, 0, 0, 0))
    bf16 = jnp.bfloat16
    outs = pl.pallas_call(
        body,
        out_shape=(
            jax.ShapeDtypeStruct((2, 2, 2048, HD), bf16),
            jax.ShapeDtypeStruct((2, 2, 2, 4, 2, HD, HD), bf16),
            jax.ShapeDtypeStruct((2, 2, 2, 4, 2, HD, HD), bf16),
        ),
        grid_spec=pltpu.PrefetchScalarGridSpec(
            num_scalar_prefetch=1,
            grid=(4,),
            in_specs=[quarter] * 4 + group + group,
            out_specs=(
                pl.BlockSpec((2, 2, 512, HD), lambda i, at: (0, 0, i, 0)),
                wide,
                wide,
            ),
        ),
        name="unpack",
    )(at, *q_pieces, *kv_pieces, *kv_others)
    return tuple(out.reshape(D, HD) for out in outs)


def local(hidden, cotangent, seg_ids, advantage, w_query, w_key, w_value):
    f32 = jnp.float32
    bf16 = jnp.bfloat16
    inv_width = D ** (-0.5)
    xh = lax.axis_index("xh")
    xl = lax.axis_index("xl")
    core = lax.axis_index("core")
    zl = lax.axis_index("zl")
    member = zl * 2 + core
    ring = xh * 2 + xl

    token_rows = hidden[0].astype(f32)
    normed_own = (
        token_rows * lax.rsqrt(jnp.mean(token_rows * token_rows, axis=-1, keepdims=True) + norm_eps)
    ).astype(bf16)
    normed = lax.all_gather(swap(normed_own), YZ + ("core",), axis=0, tiled=True)
    cot = swap(cotangent[0])
    seg_row = swap(seg_ids[0])
    adv_row = swap(advantage[0])
    block_len = 512

    at = jnp.stack([xl, xh, core, member]).astype(jnp.int32)
    cut = exchange(pack_columns(w_query, w_key, w_value, at), YZ)
    pieces = (cut,) + ring_pieces(cut)
    others = tuple(flip(p, ("core",)) for p in pieces)
    projected, q_cols, wkv, normed_m = project(normed, pieces, others, at)
    projected = projected * inv_width
    q_cols = q_cols.reshape(D, HD)

    cosine_table, sine_table = angles(seg_row)
    weight_row = token_weights(seg_row, adv_row)
    grad_context = (cot.astype(f32) * weight_row[:, None]).astype(bf16)
    position = jnp.arange(block_len, dtype=jnp.int32)
    allowed = (seg_row[:, None] == seg_row[None, :]) & (position[None, :] <= position[:, None])

    q_rot = rotate(projected[:, :HD], cosine_table, sine_table).astype(bf16)
    k_rot = rotate(projected[:, HD : 2 * HD], cosine_table, sine_table).astype(bf16)
    v_bf = projected[:, 2 * HD :].astype(bf16)

    grad_query, grad_key, grad_value = attend_back(q_rot, k_rot, v_bf, grad_context, allowed)
    scaled_q = (rotate(grad_query, cosine_table, -sine_table) * inv_width).astype(bf16)
    scaled_kv = (
        jnp.concatenate([rotate(grad_key, cosine_table, -sine_table), grad_value], -1) * inv_width
    ).astype(bf16)

    contract = (((0,), (0,)), ((), ()))
    part_q = lax.dot_general(normed, scaled_q, contract, preferred_element_type=f32)
    part_q = part_q.astype(bf16).reshape(4, 2048, HD)

    def part_for(mask):
        return lax.dynamic_index_in_dim(part_q, ring ^ mask, 0, keepdims=False)

    def add(a, b):
        return (a.astype(f32) + b.astype(f32)).astype(bf16)

    far = part_for(2)
    first = flip(far[:1024], X)
    second = flip(far[1024:], ("xl",))
    near, wrap = part_for(1), part_for(3)
    near = jnp.concatenate([add(near[:1024], first), near[1024:]], axis=0)
    wrap = jnp.concatenate([wrap[:1024], add(wrap[1024:], second)], axis=0)
    near = flip(near, ("xl",))
    wrap = flip(wrap, X)
    sum_q = part_for(0).astype(f32) + near.astype(f32) + wrap.astype(f32)
    old_q = lax.dynamic_slice_in_dim(q_cols, ring * 2048, 2048)
    new_q = (old_q.astype(f32) - step_rate * sum_q).astype(bf16)
    near = swap(new_q)
    far = lax.ppermute(
        new_q,
        ("xh", "xl", "core"),
        [
            (h * 4 + l * 2 + c, (1 - h) * 4 + c * 2 + l)
            for h in (0, 1)
            for l in (0, 1)
            for c in (0, 1)
        ],
    )
    near_other = flip(near, ("core",))
    far_other = flip(far, ("core",))
    kv_sum = exchange(scaled_kv.reshape(8, 64, 2 * HD), MEM)
    kv_sum = jnp.sum(kv_sum.astype(f32), axis=0).astype(bf16)
    kv_sum = spread(kv_sum, MEM).reshape(block_len, 2 * HD)
    part_kv = lax.dot_general(
        normed_m, kv_sum, contract, preferred_element_type=f32
    ).astype(bf16)
    part_kv = exchange(part_kv.reshape(4, 256, 2 * HD), X)
    part_kv = part_kv.astype(f32)
    old_kv = wkv.reshape(4, 2, 8, 128, 2 * HD)
    old_kv = lax.dynamic_index_in_dim(old_kv, ring, 0, keepdims=False)
    old_kv = lax.dynamic_index_in_dim(old_kv, member, 1, keepdims=False).reshape(256, 2 * HD)
    new_kv = (old_kv.astype(f32) - step_rate * jnp.sum(part_kv, axis=0)).astype(bf16)
    new_kv = spread(new_kv, ("zl",))
    kv_pieces = (new_kv,) + ring_pieces(new_kv)
    kv_others = tuple(flip(p, ("core",)) for p in kv_pieces)
    return unpack((near, far, near_other, far_other), kv_pieces, kv_others, at)


def solution(mesh):
    grid = Mesh(
        mesh.devices.reshape(2, 4, 2, 4, 2, 2), ("xh", "y", "zh", "zl", "xl", "core")
    )
    groups = ("xh", "core")
    in_specs = (
        P(groups, FS, None),
        P(groups, None, FS),
        P(groups, None),
        P(groups, None),
        P(FS, None),
        P(FS, None),
        P(FS, None),
    )
    out_specs = (P(None, FS), P(None, FS), P(None, FS))

    return jax.shard_map(local, mesh=grid, in_specs=in_specs, out_specs=out_specs, check_vma=False)
```

```python
import jax
import jax.numpy as jnp
from jax import lax
from jax.experimental import pallas as pl
from jax.experimental.pallas import tpu as pltpu
from jax.sharding import Mesh, PartitionSpec as P

D = 8192
HD = 128
RESP = 8

step_rate = 200.0
rope_base = 1000000.0
norm_eps = 1e-06
masked_score = -1e30

YZ = ("y", "zh", "zl")
MEM = ("zl", "core")
X = ("xh", "xl")
FS = ("y", "zh", "zl", "xl")


def rotate(field, cosine_table, sine_table):
    half_width = field.shape[-1] // 2
    lead_half = field[..., :half_width]
    tail_half = field[..., half_width:]
    return jnp.concatenate(
        [
            lead_half * cosine_table - tail_half * sine_table,
            tail_half * cosine_table + lead_half * sine_table,
        ],
        -1,
    )


def angles(seg_row):
    span_count = seg_row.shape[0]
    earlier = jnp.sum((seg_row[None, :] < seg_row[:, None]).astype(jnp.int32), axis=1)
    positions = jnp.arange(span_count, dtype=jnp.int32) - earlier
    frequency = rope_base ** (-jnp.arange(HD // 2, dtype=jnp.float32) * 2.0 / HD)
    phase_grid = positions.astype(jnp.float32)[:, None] * frequency[None, :]
    return jnp.cos(phase_grid), jnp.sin(phase_grid)


def token_weights(seg_row, advantage_row):
    id_range = jnp.arange(RESP + 1, dtype=jnp.int32)
    onehot = (seg_row[:, None] == id_range[None, :]).astype(jnp.float32)
    counts = jnp.sum(onehot, axis=0)[:RESP]
    per_token = -advantage_row / counts
    return jnp.sum(onehot[:, :RESP] * per_token[None, :], axis=1)


def attend_back(q_rot, k_rot, v_bf, grad_context, allowed):
    score_scale = HD ** (-0.5)
    f32 = jnp.float32
    scores = jnp.einsum("td,ud->tu", q_rot, k_rot, preferred_element_type=f32) * score_scale
    scores = jnp.where(allowed, scores, masked_score)
    row_top = jnp.max(scores, axis=-1, keepdims=True)
    exponent = jnp.exp(scores - row_top)
    attention = exponent / jnp.sum(exponent, axis=-1, keepdims=True)
    attention_bf = attention.astype(jnp.bfloat16)
    grad_prob = jnp.einsum("td,ud->tu", grad_context, v_bf, preferred_element_type=f32)
    inner_sum = jnp.sum(attention * grad_prob, axis=-1, keepdims=True)
    dscore = (attention * (grad_prob - inner_sum)).astype(jnp.bfloat16)
    grad_query = jnp.einsum("tu,ud->td", dscore, k_rot, preferred_element_type=f32) * score_scale
    grad_key = jnp.einsum("tu,td->ud", dscore, q_rot, preferred_element_type=f32) * score_scale
    grad_value = jnp.einsum("tu,td->ud", attention_bf, grad_context, preferred_element_type=f32)
    return grad_query, grad_key, grad_value


def swap(x):
    return lax.ppermute(x, ("xl", "core"), [(0, 0), (1, 2), (2, 1), (3, 3)])


def flip(x, axes):
    n = 2 ** len(axes)
    return lax.ppermute(x, axes, [(i, n - 1 - i) for i in range(n)])


def exchange(x, axes):
    return lax.all_to_all(x, axes, split_axis=0, concat_axis=0, tiled=True)


def spread(x, axes):
    n = lax.axis_size(axes)
    return exchange(jnp.broadcast_to(x[None], (n,) + x.shape), axes)


def ring_pieces(x):
    near, wrap = flip(x, ("xl",)), flip(x, X)
    half = x.shape[0] // 2
    return near, wrap, flip(wrap[:half], ("xl",)), flip(near[half:], X)


def pack_columns(w_query, w_key, w_value, at):
    def body(at_ref, q_ref, k_ref, v_ref, out_ref):
        for j in range(32):
            head = pl.multiple_of((2 * j + at_ref[2]) * HD, HD)
            out_ref[j, 0:64, :] = q_ref[:, pl.ds(head, HD)]
            key = slice(j // 4 * HD, (j // 4 + 1) * HD)
            out_ref[j, 64:96, :] = k_ref[:, key]
            out_ref[j, 96:128, :] = v_ref[:, key]

    quarter = pl.BlockSpec((32, 8 * HD), lambda i, at: (2 * at[1] + at[2], 0))
    return pl.pallas_call(
        body,
        out_shape=jax.ShapeDtypeStruct((32, 128, HD), jnp.bfloat16),
        grid_spec=pltpu.PrefetchScalarGridSpec(
            num_scalar_prefetch=1,
            grid=(1,),
            in_specs=[pl.BlockSpec((64, D), lambda i, at: (at[1], 0)), quarter, quarter],
            out_specs=pl.BlockSpec((32, 128, HD), lambda i, at: (0, 0, 0)),
        ),
        name="pack_columns",
    )(at, w_query, w_key, w_value)


def project(normed, pieces, others, at):
    def body(at_ref, rows_ref, *refs):
        mine, theirs = refs[:5], refs[5:10]
        out_ref, w_ref, member_ref = refs[10:]
        b = pl.program_id(0)
        xl, xh, core = at_ref[0], at_ref[1], at_ref[2]
        spots = ((xl, xh), (1 - xl, xh), (1 - xl, 1 - xh), (xl, 1 - xh))

        def block(group, n):
            if n < 3:
                return group[n][...]
            return jnp.where(b < 2, group[3][...], group[4][...])

        for n, (l, h) in enumerate(spots):
            own = block(mine, n)
            other = block(theirs, n)
            w_ref[:, l, h, :, 0:HD] = own[:, :64]
            w_ref[:, l, h, pl.ds(pl.multiple_of((core) * 32, 32), 32), HD : 2 * HD] = own[:, 64:96]
            w_ref[:, l, h, pl.ds(pl.multiple_of((core) * 32, 32), 32), 2 * HD : 3 * HD] = own[:, 96:128]
            w_ref[:, l, h, pl.ds(pl.multiple_of((1 - core) * 32, 32), 32), HD : 2 * HD] = other[:, 64:96]
            w_ref[:, l, h, pl.ds(pl.multiple_of((1 - core) * 32, 32), 32), 2 * HD : 3 * HD] = other[:, 96:128]

        rows = rows_ref[...]
        for n in range(2):
            member_ref[:, n * HD : (n + 1) * HD] = rows_ref[
                :, pl.ds(pl.multiple_of(n * 1024 + at_ref[3] * HD, HD), HD)
            ]

        @pl.when(b == 0)
        def _():
            out_ref[...] = jnp.zeros_like(out_ref)

        out_ref[...] += jnp.dot(
            rows, w_ref[...].reshape(2048, 3 * HD), preferred_element_type=jnp.float32
        )

    whole = pl.BlockSpec((8, 128, HD), lambda b, at: (b, 0, 0))
    first = pl.BlockSpec((8, 128, HD), lambda b, at: (jnp.minimum(b, 1), 0, 0))
    last = pl.BlockSpec((8, 128, HD), lambda b, at: (jnp.maximum(b, 2) - 2, 0, 0))
    group = [whole, whole, whole, first, last]
    bf16 = jnp.bfloat16
    return pl.pallas_call(
        body,
        out_shape=(
            jax.ShapeDtypeStruct((512, 3 * HD), jnp.float32),
            jax.ShapeDtypeStruct((32, 2, 2, 64, 3 * HD), bf16),
            jax.ShapeDtypeStruct((512, 1024), bf16),
        ),
        grid_spec=pltpu.PrefetchScalarGridSpec(
            num_scalar_prefetch=1,
            grid=(4,),
            in_specs=[pl.BlockSpec((512, 2048), lambda b, at: (0, b))] + group + group,
            out_specs=(
                pl.BlockSpec((512, 3 * HD), lambda b, at: (0, 0)),
                pl.BlockSpec((8, 2, 2, 64, 3 * HD), lambda b, at: (b, 0, 0, 0, 0)),
                pl.BlockSpec((512, 2 * HD), lambda b, at: (0, b)),
            ),
        ),
        name="project",
    )(at, normed, *pieces, *others)


def unpack(q_pieces, kv_pieces, kv_others, at):
    def body(at_ref, *refs):
        q_in, mine, theirs = refs[:4], refs[4:9], refs[9:14]
        q_ref, k_ref, v_ref = refs[14:]
        xl, xh, core = at_ref[0], at_ref[1], at_ref[2]
        line = pl.program_id(0)
        for (h, l), piece in zip(
            ((xh, core), (1 - xh, core), (xh, 1 - core), (1 - xh, 1 - core)), q_in
        ):
            q_ref[h, l] = piece[...]
        spots = ((xl, xh), (1 - xl, xh), (1 - xl, 1 - xh), (xl, 1 - xh))
        for group, c in ((mine, core), (theirs, 1 - core)):
            for n, (l, h) in enumerate(spots):
                if n < 3:
                    piece = group[n][...]
                else:
                    piece = jnp.where(line < 2, group[3][...], group[4][...])
                for z in (0, 1):
                    k_ref[h, l, z, 0, c] = piece[0, z * HD : (z + 1) * HD, 0:HD]
                    v_ref[h, l, z, 0, c] = piece[0, z * HD : (z + 1) * HD, HD : 2 * HD]

    quarter = pl.BlockSpec((512, HD), lambda i, at: (i, 0))
    whole = pl.BlockSpec((1, 2 * HD, 2 * HD), lambda i, at: (i, 0, 0))
    first = pl.BlockSpec((1, 2 * HD, 2 * HD), lambda i, at: (jnp.minimum(i, 1), 0, 0))
    last = pl.BlockSpec((1, 2 * HD, 2 * HD), lambda i, at: (jnp.maximum(i, 2) - 2, 0, 0))
    group = [whole, whole, whole, first, last]
    wide = pl.BlockSpec((2, 2, 2, 1, 2, HD, HD), lambda i, at: (0, 0, 0, i, 0, 0, 0))
    bf16 = jnp.bfloat16
    outs = pl.pallas_call(
        body,
        out_shape=(
            jax.ShapeDtypeStruct((2, 2, 2048, HD), bf16),
            jax.ShapeDtypeStruct((2, 2, 2, 4, 2, HD, HD), bf16),
            jax.ShapeDtypeStruct((2, 2, 2, 4, 2, HD, HD), bf16),
        ),
        grid_spec=pltpu.PrefetchScalarGridSpec(
            num_scalar_prefetch=1,
            grid=(4,),
            in_specs=[quarter] * 4 + group + group,
            out_specs=(
                pl.BlockSpec((2, 2, 512, HD), lambda i, at: (0, 0, i, 0)),
                wide,
                wide,
            ),
        ),
        name="unpack",
    )(at, *q_pieces, *kv_pieces, *kv_others)
    return tuple(out.reshape(D, HD) for out in outs)


def local(hidden, cotangent, seg_ids, advantage, w_query, w_key, w_value):
    f32 = jnp.float32
    bf16 = jnp.bfloat16
    inv_width = D ** (-0.5)
    xh = lax.axis_index("xh")
    xl = lax.axis_index("xl")
    core = lax.axis_index("core")
    zl = lax.axis_index("zl")
    member = zl * 2 + core
    ring = xh * 2 + xl

    token_rows = hidden[0].astype(f32)
    normed_own = (
        token_rows * lax.rsqrt(jnp.mean(token_rows * token_rows, axis=-1, keepdims=True) + norm_eps)
    ).astype(bf16)
    normed = lax.all_gather(swap(normed_own), YZ + ("core",), axis=0, tiled=True)
    cot = swap(cotangent[0])
    seg_row = swap(seg_ids[0])
    adv_row = swap(advantage[0])
    block_len = 512

    at = jnp.stack([xl, xh, core, member]).astype(jnp.int32)
    cut = exchange(pack_columns(w_query, w_key, w_value, at), YZ)
    pieces = (cut,) + ring_pieces(cut)
    others = tuple(flip(p, ("core",)) for p in pieces)
    projected, columns, normed_m = project(normed, pieces, others, at)
    projected = projected * inv_width
    columns = columns.reshape(D, 3 * HD)

    cosine_table, sine_table = angles(seg_row)
    weight_row = token_weights(seg_row, adv_row)
    grad_context = (cot.astype(f32) * weight_row[:, None]).astype(bf16)
    position = jnp.arange(block_len, dtype=jnp.int32)
    allowed = (seg_row[:, None] == seg_row[None, :]) & (position[None, :] <= position[:, None])

    q_rot = rotate(projected[:, :HD], cosine_table, sine_table).astype(bf16)
    k_rot = rotate(projected[:, HD : 2 * HD], cosine_table, sine_table).astype(bf16)
    v_bf = projected[:, 2 * HD :].astype(bf16)

    grad_query, grad_key, grad_value = attend_back(q_rot, k_rot, v_bf, grad_context, allowed)
    scaled_q = (rotate(grad_query, cosine_table, -sine_table) * inv_width).astype(bf16)
    scaled_kv = (
        jnp.concatenate([rotate(grad_key, cosine_table, -sine_table), grad_value], -1) * inv_width
    ).astype(bf16)

    contract = (((0,), (0,)), ((), ()))
    part_q = lax.dot_general(normed, scaled_q, contract, preferred_element_type=f32)
    part_q = part_q.astype(bf16).reshape(4, 2048, HD)

    def part_for(mask):
        return lax.dynamic_index_in_dim(part_q, ring ^ mask, 0, keepdims=False)

    def add(a, b):
        return (a.astype(f32) + b.astype(f32)).astype(bf16)

    far = part_for(2)
    first = flip(far[:1024], X)
    second = flip(far[1024:], ("xl",))
    near, wrap = part_for(1), part_for(3)
    near = jnp.concatenate([add(near[:1024], first), near[1024:]], axis=0)
    wrap = jnp.concatenate([wrap[:1024], add(wrap[1024:], second)], axis=0)
    near = flip(near, ("xl",))
    wrap = flip(wrap, X)
    sum_q = part_for(0).astype(f32) + near.astype(f32) + wrap.astype(f32)
    old_q = lax.dynamic_slice(columns, (ring * 2048, 0), (2048, HD))
    new_q = (old_q.astype(f32) - step_rate * sum_q).astype(bf16)
    near = swap(new_q)
    far = lax.ppermute(
        new_q,
        ("xh", "xl", "core"),
        [
            (h * 4 + l * 2 + c, (1 - h) * 4 + c * 2 + l)
            for h in (0, 1)
            for l in (0, 1)
            for c in (0, 1)
        ],
    )
    near_other = flip(near, ("core",))
    far_other = flip(far, ("core",))
    kv_sum = exchange(scaled_kv.reshape(8, 64, 2 * HD), MEM)
    kv_sum = jnp.sum(kv_sum.astype(f32), axis=0).astype(bf16)
    kv_sum = spread(kv_sum, MEM).reshape(block_len, 2 * HD)
    part_kv = lax.dot_general(
        normed_m, kv_sum, contract, preferred_element_type=f32
    ).astype(bf16)
    part_kv = exchange(part_kv.reshape(4, 256, 2 * HD), X).astype(f32)
    old_kv = columns.reshape(4, 2, 8, 128, 3 * HD)
    old_kv = lax.dynamic_slice(old_kv, (ring, 0, member, 0, HD), (1, 2, 1, 128, 2 * HD))
    old_kv = old_kv.reshape(256, 2 * HD)
    new_kv = (old_kv.astype(f32) - step_rate * jnp.sum(part_kv, axis=0)).astype(bf16)
    new_kv = spread(new_kv, ("zl",))
    kv_pieces = (new_kv,) + ring_pieces(new_kv)
    kv_others = tuple(flip(p, ("core",)) for p in kv_pieces)
    return unpack((near, far, near_other, far_other), kv_pieces, kv_others, at)


def solution(mesh):
    grid = Mesh(
        mesh.devices.reshape(2, 4, 2, 4, 2, 2), ("xh", "y", "zh", "zl", "xl", "core")
    )
    groups = ("xh", "core")
    in_specs = (
        P(groups, FS, None),
        P(groups, None, FS),
        P(groups, None),
        P(groups, None),
        P(FS, None),
        P(FS, None),
        P(FS, None),
    )
    out_specs = (P(None, FS), P(None, FS), P(None, FS))

    return jax.shard_map(local, mesh=grid, in_specs=in_specs, out_specs=out_specs, check_vma=False)
```

```python
import jax
import jax.numpy as jnp
from jax import lax
from jax.experimental import pallas as pl
from jax.experimental.pallas import tpu as pltpu
from jax.sharding import Mesh, PartitionSpec as P

D = 8192
HD = 128
RESP = 8

step_rate = 200.0
rope_base = 1000000.0
norm_eps = 1e-06
masked_score = -1e30

YZ = ("y", "zh", "zl")
MEM = ("zl", "core")
X = ("xh", "xl")
FS = ("y", "zh", "zl", "xl")


def rotate(field, cosine_table, sine_table):
    half_width = field.shape[-1] // 2
    lead_half = field[..., :half_width]
    tail_half = field[..., half_width:]
    return jnp.concatenate(
        [
            lead_half * cosine_table - tail_half * sine_table,
            tail_half * cosine_table + lead_half * sine_table,
        ],
        -1,
    )


def angles(seg_row):
    span_count = seg_row.shape[0]
    earlier = jnp.sum((seg_row[None, :] < seg_row[:, None]).astype(jnp.int32), axis=1)
    positions = jnp.arange(span_count, dtype=jnp.int32) - earlier
    frequency = rope_base ** (-jnp.arange(HD // 2, dtype=jnp.float32) * 2.0 / HD)
    phase_grid = positions.astype(jnp.float32)[:, None] * frequency[None, :]
    return jnp.cos(phase_grid), jnp.sin(phase_grid)


def token_weights(seg_row, advantage_row):
    id_range = jnp.arange(RESP + 1, dtype=jnp.int32)
    onehot = (seg_row[:, None] == id_range[None, :]).astype(jnp.float32)
    counts = jnp.sum(onehot, axis=0)[:RESP]
    per_token = -advantage_row / counts
    return jnp.sum(onehot[:, :RESP] * per_token[None, :], axis=1)


def attend_back(q_rot, k_rot, v_bf, grad_context, allowed):
    score_scale = HD ** (-0.5)
    f32 = jnp.float32
    scores = jnp.einsum("td,ud->tu", q_rot, k_rot, preferred_element_type=f32) * score_scale
    scores = jnp.where(allowed, scores, masked_score)
    row_top = jnp.max(scores, axis=-1, keepdims=True)
    exponent = jnp.exp(scores - row_top)
    attention = exponent / jnp.sum(exponent, axis=-1, keepdims=True)
    attention_bf = attention.astype(jnp.bfloat16)
    grad_prob = jnp.einsum("td,ud->tu", grad_context, v_bf, preferred_element_type=f32)
    inner_sum = jnp.sum(attention * grad_prob, axis=-1, keepdims=True)
    dscore = (attention * (grad_prob - inner_sum)).astype(jnp.bfloat16)
    grad_query = jnp.einsum("tu,ud->td", dscore, k_rot, preferred_element_type=f32) * score_scale
    grad_key = jnp.einsum("tu,td->ud", dscore, q_rot, preferred_element_type=f32) * score_scale
    grad_value = jnp.einsum("tu,td->ud", attention_bf, grad_context, preferred_element_type=f32)
    return grad_query, grad_key, grad_value


def swap(x):
    return lax.ppermute(x, ("xl", "core"), [(0, 0), (1, 2), (2, 1), (3, 3)])


def flip(x, axes):
    n = 2 ** len(axes)
    return lax.ppermute(x, axes, [(i, n - 1 - i) for i in range(n)])


def exchange(x, axes):
    return lax.all_to_all(x, axes, split_axis=0, concat_axis=0, tiled=True)


def spread(x, axes):
    n = lax.axis_size(axes)
    return exchange(jnp.broadcast_to(x[None], (n,) + x.shape), axes)


def ring_pieces(x):
    near, wrap = flip(x, ("xl",)), flip(x, X)
    half = x.shape[0] // 2
    return near, wrap, flip(wrap[:half], ("xl",)), flip(near[half:], X)


def pack_columns(w_query, w_key, w_value, at):
    def body(at_ref, q_ref, k_ref, v_ref, out_ref):
        for j in range(32):
            head = pl.multiple_of((2 * j + at_ref[2]) * HD, HD)
            out_ref[j, 0:64, :] = q_ref[:, pl.ds(head, HD)]
            key = slice(j // 4 * HD, (j // 4 + 1) * HD)
            out_ref[j, 64:96, :] = k_ref[:, key]
            out_ref[j, 96:128, :] = v_ref[:, key]

    quarter = pl.BlockSpec((32, 8 * HD), lambda i, at: (2 * at[1] + at[2], 0))
    return pl.pallas_call(
        body,
        out_shape=jax.ShapeDtypeStruct((32, 128, HD), jnp.bfloat16),
        grid_spec=pltpu.PrefetchScalarGridSpec(
            num_scalar_prefetch=1,
            grid=(1,),
            in_specs=[pl.BlockSpec((64, D), lambda i, at: (at[1], 0)), quarter, quarter],
            out_specs=pl.BlockSpec((32, 128, HD), lambda i, at: (0, 0, 0)),
        ),
        name="pack_columns",
    )(at, w_query, w_key, w_value)


def project(normed, pieces, others, at):
    def body(at_ref, rows_ref, *refs):
        mine, theirs = refs[:5], refs[5:10]
        out_ref, wq_ref, wkv_ref, member_ref = refs[10:]
        b = pl.program_id(0)
        xl, xh, core = at_ref[0], at_ref[1], at_ref[2]
        spots = ((xl, xh), (1 - xl, xh), (1 - xl, 1 - xh), (xl, 1 - xh))

        def block(group, n):
            if n < 3:
                return group[n][...]
            return jnp.where(b < 1, group[3][...], group[4][...])

        for n, (l, h) in enumerate(spots):
            own = block(mine, n)
            other = block(theirs, n)
            wq_ref[:, l, h] = own[:, :64]
            wkv_ref[:, l, h, core, :, 0:HD] = own[:, 64:96]
            wkv_ref[:, l, h, core, :, HD : 2 * HD] = own[:, 96:128]
            wkv_ref[:, l, h, 1 - core, :, 0:HD] = other[:, 64:96]
            wkv_ref[:, l, h, 1 - core, :, HD : 2 * HD] = other[:, 96:128]

        rows = rows_ref[...]
        for n in range(4):
            member_ref[:, n * HD : (n + 1) * HD] = rows_ref[
                :, pl.ds(pl.multiple_of(n * 1024 + at_ref[3] * HD, HD), HD)
            ]

        @pl.when(b == 0)
        def _():
            out_ref[...] = jnp.zeros_like(out_ref)

        out_ref[:, 0:HD] += jnp.dot(
            rows, wq_ref[...].reshape(4096, HD), preferred_element_type=jnp.float32
        )
        out_ref[:, HD : 3 * HD] += jnp.dot(
            rows, wkv_ref[...].reshape(4096, 2 * HD), preferred_element_type=jnp.float32
        )

    whole = pl.BlockSpec((16, 128, HD), lambda b, at: (b, 0, 0))
    first = pl.BlockSpec((16, 128, HD), lambda b, at: (jnp.minimum(b, 0), 0, 0))
    last = pl.BlockSpec((16, 128, HD), lambda b, at: (jnp.maximum(b, 1) - 1, 0, 0))
    group = [whole, whole, whole, first, last]
    bf16 = jnp.bfloat16
    return pl.pallas_call(
        body,
        out_shape=(
            jax.ShapeDtypeStruct((512, 3 * HD), jnp.float32),
            jax.ShapeDtypeStruct((32, 2, 2, 64, HD), bf16),
            jax.ShapeDtypeStruct((32, 2, 2, 2, 32, 2 * HD), bf16),
            jax.ShapeDtypeStruct((512, 1024), bf16),
        ),
        grid_spec=pltpu.PrefetchScalarGridSpec(
            num_scalar_prefetch=1,
            grid=(2,),
            in_specs=[pl.BlockSpec((512, 4096), lambda b, at: (0, b))] + group + group,
            out_specs=(
                pl.BlockSpec((512, 3 * HD), lambda b, at: (0, 0)),
                pl.BlockSpec((16, 2, 2, 64, HD), lambda b, at: (b, 0, 0, 0, 0)),
                pl.BlockSpec((16, 2, 2, 2, 32, 2 * HD), lambda b, at: (b, 0, 0, 0, 0, 0)),
                pl.BlockSpec((512, 4 * HD), lambda b, at: (0, b)),
            ),
        ),
        name="project",
    )(at, normed, *pieces, *others)


def unpack(q_pieces, kv_pieces, kv_others, at):
    def body(at_ref, *refs):
        q_in, mine, theirs = refs[:4], refs[4:9], refs[9:14]
        q_ref, k_ref, v_ref = refs[14:]
        xl, xh, core = at_ref[0], at_ref[1], at_ref[2]
        line = pl.program_id(0)
        for (h, l), piece in zip(
            ((xh, core), (1 - xh, core), (xh, 1 - core), (1 - xh, 1 - core)), q_in
        ):
            q_ref[h, l] = piece[...]
        spots = ((xl, xh), (1 - xl, xh), (1 - xl, 1 - xh), (xl, 1 - xh))
        for group, c in ((mine, core), (theirs, 1 - core)):
            for n, (l, h) in enumerate(spots):
                if n < 3:
                    piece = group[n][...]
                else:
                    piece = jnp.where(line < 2, group[3][...], group[4][...])
                for z in (0, 1):
                    k_ref[h, l, z, 0, c] = piece[0, z * HD : (z + 1) * HD, 0:HD]
                    v_ref[h, l, z, 0, c] = piece[0, z * HD : (z + 1) * HD, HD : 2 * HD]

    quarter = pl.BlockSpec((512, HD), lambda i, at: (i, 0))
    whole = pl.BlockSpec((1, 2 * HD, 2 * HD), lambda i, at: (i, 0, 0))
    first = pl.BlockSpec((1, 2 * HD, 2 * HD), lambda i, at: (jnp.minimum(i, 1), 0, 0))
    last = pl.BlockSpec((1, 2 * HD, 2 * HD), lambda i, at: (jnp.maximum(i, 2) - 2, 0, 0))
    group = [whole, whole, whole, first, last]
    wide = pl.BlockSpec((2, 2, 2, 1, 2, HD, HD), lambda i, at: (0, 0, 0, i, 0, 0, 0))
    bf16 = jnp.bfloat16
    outs = pl.pallas_call(
        body,
        out_shape=(
            jax.ShapeDtypeStruct((2, 2, 2048, HD), bf16),
            jax.ShapeDtypeStruct((2, 2, 2, 4, 2, HD, HD), bf16),
            jax.ShapeDtypeStruct((2, 2, 2, 4, 2, HD, HD), bf16),
        ),
        grid_spec=pltpu.PrefetchScalarGridSpec(
            num_scalar_prefetch=1,
            grid=(4,),
            in_specs=[quarter] * 4 + group + group,
            out_specs=(
                pl.BlockSpec((2, 2, 512, HD), lambda i, at: (0, 0, i, 0)),
                wide,
                wide,
            ),
        ),
        name="unpack",
    )(at, *q_pieces, *kv_pieces, *kv_others)
    return tuple(out.reshape(D, HD) for out in outs)


def local(hidden, cotangent, seg_ids, advantage, w_query, w_key, w_value):
    f32 = jnp.float32
    bf16 = jnp.bfloat16
    inv_width = D ** (-0.5)
    xh = lax.axis_index("xh")
    xl = lax.axis_index("xl")
    core = lax.axis_index("core")
    zl = lax.axis_index("zl")
    member = zl * 2 + core
    ring = xh * 2 + xl

    token_rows = hidden[0].astype(f32)
    normed_own = (
        token_rows * lax.rsqrt(jnp.mean(token_rows * token_rows, axis=-1, keepdims=True) + norm_eps)
    ).astype(bf16)
    normed = lax.all_gather(swap(normed_own), YZ + ("core",), axis=0, tiled=True)
    cot = swap(cotangent[0])
    seg_row = swap(seg_ids[0])
    adv_row = swap(advantage[0])
    block_len = 512

    at = jnp.stack([xl, xh, core, member]).astype(jnp.int32)
    cut = exchange(pack_columns(w_query, w_key, w_value, at), YZ)
    pieces = (cut,) + ring_pieces(cut)
    others = tuple(flip(p, ("core",)) for p in pieces)
    projected, q_cols, wkv, normed_m = project(normed, pieces, others, at)
    projected = projected * inv_width
    q_cols = q_cols.reshape(D, HD)

    cosine_table, sine_table = angles(seg_row)
    weight_row = token_weights(seg_row, adv_row)
    grad_context = (cot.astype(f32) * weight_row[:, None]).astype(bf16)
    position = jnp.arange(block_len, dtype=jnp.int32)
    allowed = (seg_row[:, None] == seg_row[None, :]) & (position[None, :] <= position[:, None])

    q_rot = rotate(projected[:, :HD], cosine_table, sine_table).astype(bf16)
    k_rot = rotate(projected[:, HD : 2 * HD], cosine_table, sine_table).astype(bf16)
    v_bf = projected[:, 2 * HD :].astype(bf16)

    grad_query, grad_key, grad_value = attend_back(q_rot, k_rot, v_bf, grad_context, allowed)
    scaled_q = (rotate(grad_query, cosine_table, -sine_table) * inv_width).astype(bf16)
    scaled_kv = (
        jnp.concatenate([rotate(grad_key, cosine_table, -sine_table), grad_value], -1) * inv_width
    ).astype(bf16)

    contract = (((0,), (0,)), ((), ()))
    part_q = lax.dot_general(normed, scaled_q, contract, preferred_element_type=f32)
    part_q = part_q.astype(bf16).reshape(4, 2048, HD)

    def part_for(mask):
        return lax.dynamic_index_in_dim(part_q, ring ^ mask, 0, keepdims=False)

    def add(a, b):
        return (a.astype(f32) + b.astype(f32)).astype(bf16)

    far = part_for(2)
    first = flip(far[:1024], X)
    second = flip(far[1024:], ("xl",))
    near, wrap = part_for(1), part_for(3)
    near = jnp.concatenate([add(near[:1024], first), near[1024:]], axis=0)
    wrap = jnp.concatenate([wrap[:1024], add(wrap[1024:], second)], axis=0)
    near = flip(near, ("xl",))
    wrap = flip(wrap, X)
    sum_q = part_for(0).astype(f32) + near.astype(f32) + wrap.astype(f32)
    old_q = lax.dynamic_slice_in_dim(q_cols, ring * 2048, 2048)
    new_q = (old_q.astype(f32) - step_rate * sum_q).astype(bf16)
    near = swap(new_q)
    far = lax.ppermute(
        new_q,
        ("xh", "xl", "core"),
        [
            (h * 4 + l * 2 + c, (1 - h) * 4 + c * 2 + l)
            for h in (0, 1)
            for l in (0, 1)
            for c in (0, 1)
        ],
    )
    near_other = flip(near, ("core",))
    far_other = flip(far, ("core",))
    kv_sum = exchange(scaled_kv.reshape(8, 64, 2 * HD), MEM)
    kv_sum = jnp.sum(kv_sum.astype(f32), axis=0).astype(bf16)
    kv_sum = spread(kv_sum, MEM).reshape(block_len, 2 * HD)
    part_kv = lax.dot_general(
        normed_m, kv_sum, contract, preferred_element_type=f32
    ).astype(bf16)
    part_kv = exchange(part_kv.reshape(4, 256, 2 * HD), X).astype(f32)
    old_kv = wkv.reshape(4, 2, 8, 128, 2 * HD)
    old_kv = lax.dynamic_index_in_dim(old_kv, ring, 0, keepdims=False)
    old_kv = lax.dynamic_index_in_dim(old_kv, member, 1, keepdims=False).reshape(256, 2 * HD)
    new_kv = (old_kv.astype(f32) - step_rate * jnp.sum(part_kv, axis=0)).astype(bf16)
    new_kv = spread(new_kv, ("zl",))
    kv_pieces = (new_kv,) + ring_pieces(new_kv)
    kv_others = tuple(flip(p, ("core",)) for p in kv_pieces)
    return unpack((near, far, near_other, far_other), kv_pieces, kv_others, at)


def solution(mesh):
    grid = Mesh(
        mesh.devices.reshape(2, 4, 2, 4, 2, 2), ("xh", "y", "zh", "zl", "xl", "core")
    )
    groups = ("xh", "core")
    in_specs = (
        P(groups, FS, None),
        P(groups, None, FS),
        P(groups, None),
        P(groups, None),
        P(FS, None),
        P(FS, None),
        P(FS, None),
    )
    out_specs = (P(None, FS), P(None, FS), P(None, FS))

    return jax.shard_map(local, mesh=grid, in_specs=in_specs, out_specs=out_specs, check_vma=False)
```
